32 devices in a mesh: batch: 4 (over x, core), seq: 8 (over z, y).
Axes of the slice: x: 2, y: 2, z: 4, core: 2. Of those that a mesh axis runs over, the one named last changes fastest.
Arguments:
- inputs: bfloat16 [16, 2048, 512], P('batch', 'seq'), may hold values from -6 to 6
- cotangent: float32 [16, 2048, 512], P('batch', 'seq'), may hold values from -6 to 6
- query_weight: bfloat16 [512, 512], P('seq', 'batch'), may hold values from -0.25 to 0.25
- key_weight: bfloat16 [512, 512], P('seq', 'batch'), may hold values from -0.25 to 0.25
- value_weight: bfloat16 [512, 512], P('seq', 'batch'), may hold values from -0.25 to 0.25
- out_weight: bfloat16 [512, 512], P('seq', 'batch'), may hold values from -0.75 to 0.75
- up_weight: bfloat16 [512, 2048], P('seq', 'batch'), may hold values from -0.25 to 0.25
- down_weight: bfloat16 [2048, 512], P('seq', 'batch'), may hold values from -0.125 to 0.125
- norm1_gain: bfloat16 [512], P('seq'), may hold values from 0.5 to 1.5
- norm1_bias: bfloat16 [512], P('seq'), may hold values from -0.59765625 to 0.59765625
- norm2_gain: bfloat16 [512], P('seq'), may hold values from 0.5 to 1.5
- norm2_bias: bfloat16 [512], P('seq'), may hold values from -0.59765625 to 0.59765625
- out_bias: bfloat16 [512], P('seq'), may hold values from -0.59765625 to 0.59765625
- up_bias: bfloat16 [2048], P('seq'), may hold values from -0.59765625 to 0.59765625
- down_bias: bfloat16 [512], P('seq'), may hold values from -0.59765625 to 0.59765625
Outputs:
- outputs: bfloat16 [16, 2048, 512], P('batch', 'seq')
- input_grad: float32 [16, 2048, 512], P('batch', 'seq')
- query_grad: float32 [512, 512], P('seq', 'batch')
- key_grad: float32 [512, 512], P('seq', 'batch')
- value_grad: float32 [512, 512], P('seq', 'batch')
- out_grad: float32 [512, 512], P('seq', 'batch')
- up_grad: float32 [512, 2048], P('seq', 'batch')
- down_grad: float32 [2048, 512], P('seq', 'batch')
- norm1_gain_grad: float32 [512], P('seq')
- norm1_bias_grad: float32 [512], P('seq')
- norm2_gain_grad: float32 [512], P('seq')
- norm2_bias_grad: float32 [512], P('seq')
- out_bias_grad: float32 [512], P('seq')
- up_bias_grad: float32 [2048], P('seq')
- down_bias_grad: float32 [512], P('seq')
The draws below stay inside these ranges and needn't reach their ends.
All inputs are finite; a program needn't handle non-finite values.
Results may differ from the reference program's by a relative error of at most 0.014.
Values may be sent and summed in bfloat16 or wider, within the bound.
No kernel may reach another device: no remote copies, remote signals or barrier semaphores. Data moves between devices by JAX's collectives and lax.ppermute only.
A program may use at most 128 MiB of HBM per device.

```python
import jax
import jax.numpy as jnp
from jax import lax

D = 512
HEADS = 8
HEAD = 64
FF = 2048
BLOCK = 256
SPAN = 128
SEQUENCES = 16
LENGTH = 2048


def draw_inputs(key, part):
    rough_key = jax.random.fold_in(key, 11)
    common_key = jax.random.fold_in(key, 12)
    span_count = LENGTH // SPAN
    rough = jax.random.normal(rough_key, (SEQUENCES, LENGTH, D), jnp.float32)
    common = jax.random.normal(common_key, (SEQUENCES, span_count, 1, D), jnp.float32)
    common = jnp.broadcast_to(common, (SEQUENCES, span_count, SPAN, D)).reshape(SEQUENCES, LENGTH, D)
    return jnp.clip(0.8 * rough + 0.8 * common, -6.0, 6.0).astype(jnp.bfloat16)


def shard_levels(stream_key, dims, split, least, high):
    factor_of, own = 1.0, jax.random.fold_in(stream_key, 6)
    for dim, blocks in split:
        heights = jnp.exp(jax.random.uniform(jax.random.fold_in(own, dim), (blocks,), jnp.float32, least / len(split), high / len(split)))
        factor_of = factor_of * jnp.repeat(heights, dims[dim] // blocks).reshape([-1 if axis == dim else 1 for axis in range(len(dims))])
    return factor_of


def bell_draw(own_key, extent, spread, bound, cuts=(), held_as=jnp.bfloat16):
    array = jax.random.normal(own_key, extent, jnp.float32) * spread
    if len(cuts) > 0:
        array = shard_levels(own_key, extent, cuts, -0.22, 0.18) * array
    return jnp.clip(array, min=-bound, max=bound).astype(held_as)


def setup_inputs(seed: int = 0) -> dict:
    arg_keys = jax.random.split(jax.random.key(seed), 16)
    return {
        "inputs": draw_inputs(jax.random.fold_in(arg_keys[15], 71), 0),
        "cotangent": bell_draw(arg_keys[1], (SEQUENCES, LENGTH, D), 1.0, 6.0, ((0, 4), (1, 8)), jnp.float32),
        "query_weight": bell_draw(arg_keys[2], (D, D), D ** -0.5, 0.25, ((0, 8), (1, 4))),
        "key_weight": bell_draw(arg_keys[3], (D, D), D ** -0.5, 0.25, ((0, 8), (1, 4))),
        "value_weight": bell_draw(arg_keys[4], (D, D), D ** -0.5, 0.25, ((0, 8), (1, 4))),
        "out_weight": bell_draw(arg_keys[5], (D, D), (D // 8) ** -0.5, 0.75, ((0, 8), (1, 4))),
        "up_weight": bell_draw(arg_keys[6], (D, FF), D ** -0.5, 0.25, ((0, 8), (1, 4))),
        "down_weight": bell_draw(arg_keys[7], (FF, D), FF ** -0.5, 0.125, ((0, 8), (1, 4))),
        "norm1_gain": jnp.clip(1.0 + 0.1 * jax.random.normal(arg_keys[8], (D,), jnp.float32), 0.5, 1.5).astype(jnp.bfloat16),
        "norm1_bias": bell_draw(arg_keys[9], (D,), 0.1, 0.59765625, ((0, 8),)),
        "norm2_gain": jnp.clip(1.0 + 0.1 * jax.random.normal(arg_keys[10], (D,), jnp.float32), 0.5, 1.5).astype(jnp.bfloat16),
        "norm2_bias": bell_draw(arg_keys[11], (D,), 0.1, 0.59765625, ((0, 8),)),
        "out_bias": bell_draw(arg_keys[12], (D,), 0.1, 0.59765625, ((0, 8),)),
        "up_bias": bell_draw(arg_keys[13], (FF,), 0.1, 0.59765625, ((0, 8),)),
        "down_bias": bell_draw(arg_keys[14], (D,), 0.1, 0.59765625, ((0, 8),)),
    }


@jax.custom_vjp
def low(v):
    return lax.optimization_barrier(v.astype(jnp.bfloat16)).astype(jnp.float32)

@jax.custom_vjp
def low_back(v):
    return v

def low_keep(v):
    return (low(v), None)

def low_pass(kept, grad):
    return (grad,)

def back_keep(v):
    return (v, None)

def back_low(kept, grad):
    return (low(grad),)
low.defvjp(low_keep, low_pass)
low_back.defvjp(back_keep, back_low)
highest = lax.Precision.HIGHEST

def product(left, right):
    return jnp.matmul(left, right, precision=highest)

def layer_norm(values, gain, shift):
    centre = lax.optimization_barrier(jnp.mean(values, -1, keepdims=True))
    centred = values - centre
    variance = lax.optimization_barrier(jnp.mean(centred * centred, -1, keepdims=True))
    return centred * lax.rsqrt(variance + 1e-05) * gain + shift

def attend(queries, keys, values, sum_keys, sum_values):
    blocks = queries.shape[0] // BLOCK
    span_count = sum_keys.shape[0]
    score_scale = HEAD ** (-0.5)
    query_blocks = queries.reshape(blocks, BLOCK, HEADS, HEAD)
    key_blocks = keys.reshape(blocks, BLOCK, HEADS, HEAD)
    value_blocks = values.reshape(blocks, BLOCK, HEADS, HEAD)
    span_keys = sum_keys.reshape(span_count, HEADS, HEAD)
    span_values = sum_values.reshape(span_count, HEADS, HEAD)
    direct = low_back(jnp.einsum('bqhe,bkhe->bhqk', query_blocks, key_blocks, precision=highest) * score_scale)
    remote = low_back(jnp.einsum('bqhe,jhe->bhqj', query_blocks, span_keys, precision=highest) * score_scale)
    visible = lax.broadcasted_iota(jnp.int32, (blocks, span_count), 1) < 2 * lax.broadcasted_iota(jnp.int32, (blocks, span_count), 0)
    remote = jnp.where(visible[:, None, None, :], remote, -1e+30)
    joined = jnp.concatenate([direct, remote], -1)
    row_top = lax.optimization_barrier(jnp.max(joined, -1, keepdims=True))
    powers = jnp.exp(joined - row_top)
    attn_probs = low(powers / lax.optimization_barrier(jnp.sum(powers, -1, keepdims=True)))
    mixed = jnp.einsum('bhqk,bkhe->bqhe', attn_probs[..., :BLOCK], value_blocks, precision=highest)
    mixed = mixed + jnp.einsum('bhqj,jhe->bqhe', attn_probs[..., BLOCK:], span_values, precision=highest)
    return mixed.reshape(queries.shape)

def forward_one(inputs, query_weight, key_weight, value_weight, out_weight, up_weight, down_weight, norm1_gain, norm1_bias, norm2_gain, norm2_bias, out_bias, up_bias, down_bias):
    normed = low(layer_norm(inputs, norm1_gain, norm1_bias))
    queries = low(low_back(product(normed, query_weight)))
    key_full = low_back(product(normed, key_weight))
    value_full = low_back(product(normed, value_weight))
    span_count = inputs.shape[0] // SPAN
    sum_keys = low(lax.optimization_barrier(jnp.mean(key_full.reshape(span_count, SPAN, D), 1)))
    sum_values = low(lax.optimization_barrier(jnp.mean(value_full.reshape(span_count, SPAN, D), 1)))
    mixed = low(low_back(jax.checkpoint(attend)(queries, low(key_full), low(value_full), sum_keys, sum_values)))
    branch = low_back(product(mixed, out_weight) + out_bias)
    middle = inputs + branch
    normed_two = low(layer_norm(middle, norm2_gain, norm2_bias))
    hidden = low_back(product(normed_two, up_weight) + up_bias)
    active = low(jax.nn.gelu(hidden, approximate=False))
    feed = low_back(product(active, down_weight) + down_bias)
    return middle + feed

def reference(inputs, cotangent, query_weight, key_weight, value_weight, out_weight, up_weight, down_weight, norm1_gain, norm1_bias, norm2_gain, norm2_bias, out_bias, up_bias, down_bias):
    params = tuple((member.astype(jnp.float32) for member in (query_weight, key_weight, value_weight, out_weight, up_weight, down_weight, norm1_gain, norm1_bias, norm2_gain, norm2_bias, out_bias, up_bias, down_bias)))

    def one_sequence(totals, couple):
        sequence, tangent = couple
        result, pullback = jax.vjp(forward_one, sequence.astype(jnp.float32), *params)
        gradients = pullback(tangent)
        updated = tuple((running + gradient for running, gradient in zip(totals, gradients[1:])))
        return (updated, (result.astype(jnp.bfloat16), gradients[0]))
    starting = tuple((jnp.zeros_like(member) for member in params))
    totals, (outputs, input_grad) = lax.scan(one_sequence, starting, (inputs, cotangent))
    return (outputs, input_grad, totals[0], totals[1], totals[2], totals[3], totals[4], totals[5], totals[6], totals[7], totals[8], totals[9], totals[10], totals[11], totals[12])
```

```python
import jax
import jax.numpy as jnp
from jax import lax
from jax.experimental import pallas as pl
from jax.experimental.pallas import tpu as pltpu
from jax.sharding import PartitionSpec as P

HEADS = 8
HEAD = 64
VEC_ROWS = 32
F32 = jnp.float32
BF16 = jnp.bfloat16


def swap(array, axis, bit):
    count = lax.axis_size(axis)
    return lax.ppermute(array, axis, [(i, i ^ bit) for i in range(count)])


def bits_down(count):
    return [1 << k for k in range(count.bit_length() - 2, -1, -1)]


def outer_stages():
    seq = [("seq", bit) for bit in bits_down(lax.axis_size("seq")) if bit > 1]
    batch = [("batch", bit) for bit in bits_down(lax.axis_size("batch")) if bit > 2]
    return batch + seq


def relative_ids(stages):
    ids = [(0, 0)]
    for axis, bit in stages:
        moved = [(s ^ bit, b) if axis == "seq" else (s, b ^ bit) for s, b in ids]
        ids = ids + moved
    return ids


X_STAGE = ("batch", 2)
Y_STAGE = ("seq", 1)
CORE = ("batch", 1)


def gather_all(pack):
    rows = pack.shape[0]
    half = rows // 2
    state = pack[None]
    outer = outer_stages()
    for stage in outer:
        state = jnp.concatenate([state, swap(state, *stage)], 0)
    pieces = []
    for first, order in ((0, (X_STAGE, Y_STAGE)), (half, (Y_STAGE, X_STAGE))):
        part = state[:, first : first + half]
        part = jnp.concatenate([part, swap(part, *order[0])], 0)
        far = swap(part, *order[1])
        ids = relative_ids(outer + [order[0]])
        full = relative_ids(outer + list(order))
        far_ids = full[len(ids) :]
        for piece, names in ((part, ids), (far, far_ids)):
            pieces.append((piece, names, first))
            pieces.append((swap(piece, *CORE), [(s, b ^ 1) for s, b in names], first))
    return pieces


def place():
    return jnp.stack([lax.axis_index("seq"), lax.axis_index("batch")]).astype(jnp.int32)


def cuts(segments, first, half):
    found = []
    at = 0
    for name, rows in segments:
        low, high = max(at, first), min(at + rows, first + half)
        if low < high:
            found.append((name, low - at, low - first, high - low))
        at += rows
    return found


def unpack(pieces, segments, targets, shapes):
    arrays = [piece for piece, _, _ in pieces]

    def kernel(spot, *refs):
        ins, outs = refs[: len(arrays)], refs[len(arrays) :]
        for ref, (piece, names, first) in zip(ins, pieces):
            for p, (sr, br) in enumerate(names):
                s, b = spot[0] ^ sr, spot[1] ^ br
                for name, row, here, size in cuts(segments, first, piece.shape[1]):
                    if name == "vec" and br != 0:
                        continue
                    number, top, left = targets(name, row, s, b)
                    outs[number][
                        pl.ds(pl.multiple_of(top, 16), size), pl.ds(pl.multiple_of(left, 128), 128)
                    ] = ref[p, here : here + size, :]

    return pl.pallas_call(
        kernel,
        out_shape=[jax.ShapeDtypeStruct(shape, BF16) for shape in shapes],
        in_specs=[pl.BlockSpec(memory_space=pltpu.SMEM)]
        + [pl.BlockSpec(memory_space=pltpu.VMEM) for _ in arrays],
        out_specs=[pl.BlockSpec(memory_space=pltpu.VMEM) for _ in shapes],
    )(place(), *arrays)


def pack_order():
    outer = outer_stages()
    return [
        relative_ids(outer + [Y_STAGE, X_STAGE, CORE]),
        relative_ids(outer + [X_STAGE, Y_STAGE, CORE]),
    ]


def pack(arrays, segments, targets):
    rows = sum(size for _, size in segments)
    half = rows // 2
    orders = pack_order()

    def kernel(spot, *refs):
        ins, outs = refs[: len(arrays)], refs[len(arrays) :]
        for out, names, first in zip(outs, orders, (0, half)):
            for p, (sr, br) in enumerate(names):
                s, b = spot[0] ^ sr, spot[1] ^ br
                for name, row, here, size in cuts(segments, first, half):
                    number, top, left = targets(name, row, s, b)
                    out[p, here : here + size, :] = ins[number][
                        pl.ds(pl.multiple_of(top, 16), size), pl.ds(pl.multiple_of(left, 128), 128)
                    ].astype(BF16)

    return pl.pallas_call(
        kernel,
        out_shape=[jax.ShapeDtypeStruct((len(names), half, 128), BF16) for names in orders],
        in_specs=[pl.BlockSpec(memory_space=pltpu.SMEM)]
        + [pl.BlockSpec(memory_space=pltpu.VMEM) for _ in arrays],
        out_specs=[pl.BlockSpec(memory_space=pltpu.VMEM) for _ in orders],
    )(place(), *arrays)


def add_low(mine, theirs):
    return (mine.astype(F32) + theirs.astype(F32)).astype(BF16)


def join_pair(array):
    count = VEC_ROWS // 2
    return array[..., -VEC_ROWS:-count, :].astype(F32) + array[..., -count:, :].astype(F32)


def split_pair(total):
    high = lax.reduce_precision(total, 8, 7)
    return [high.astype(BF16), (total - high).astype(BF16)]


def add_pairs(mine, theirs):
    total = join_pair(mine) + join_pair(theirs)
    low = add_low(mine[..., :-VEC_ROWS, :], theirs[..., :-VEC_ROWS, :])
    return jnp.concatenate([low] + split_pair(total), -2)


def reduce_all(halves, pairs):
    outer = outer_stages()[::-1]
    done = []
    for k, (state, order) in enumerate(
        zip(halves, ((CORE, X_STAGE, Y_STAGE), (CORE, Y_STAGE, X_STAGE)))
    ):
        add = add_pairs if pairs and k == 1 else add_low
        stages = list(order) + outer
        for stage in stages:
            count = state.shape[0] // 2
            theirs = swap(state[count:], *stage)
            mine = state[:count]
            if stage is stages[-1]:
                if add is add_pairs:
                    total = join_pair(mine) + join_pair(theirs)
                    body = mine[:, :-VEC_ROWS].astype(F32) + theirs[:, :-VEC_ROWS].astype(F32)
                    state = jnp.concatenate([body, total], 1)
                else:
                    state = mine.astype(F32) + theirs.astype(F32)
            else:
                state = add(mine, theirs)
        done.append(state[0])
    return jnp.concatenate(done, 0)


def seq_stages():
    return [("seq", bit) for bit in bits_down(lax.axis_size("seq"))]


def gather_seq(array):
    state = array[None]
    for stage in seq_stages():
        state = jnp.concatenate([state, swap(state, *stage)], 0)
    return state


def reduce_seq(state):
    for stage in seq_stages()[::-1]:
        count = state.shape[0] // 2
        theirs = swap(state[count:], *stage)
        total = state[:count].astype(F32) + theirs.astype(F32)
        state = total if count == 1 else total.astype(BF16)
    return state[0]


def columns(weights):
    return [
        ((i, c), weight.shape[0])
        for i, weight in enumerate(weights)
        for c in range(weight.shape[1] // 128)
    ]


def packed(weights):
    return [
        weight[:, c : c + 128] for weight in weights for c in range(0, weight.shape[1], 128)
    ]


def spots(weights):
    def targets(name, row, s, b):
        if name == "vec":
            return (len(weights), s * VEC_ROWS + row, 0)
        i, c = name
        rows, width = weights[i].shape
        return (i, s * rows + row, b * width + c * 128)

    return targets


def whole(weights):
    return [
        (w.shape[0] * lax.axis_size("seq"), w.shape[1] * lax.axis_size("batch")) for w in weights
    ]


def gather_group(weights, vectors, after=None):
    blocks = packed(weights)
    segments = columns(weights)
    shapes = whole(weights)
    if vectors:
        flat = jnp.concatenate(vectors).reshape(-1, 128)
        blocks = blocks + [jnp.pad(flat, ((0, VEC_ROWS - flat.shape[0]), (0, 0)))]
        segments = segments + [("vec", VEC_ROWS)]
        shapes = shapes + [(lax.axis_size("seq") * VEC_ROWS, 128)]
    block = jnp.concatenate(blocks, 0)
    if after is not None:
        block = lax.optimization_barrier((block, after))[0]
    pieces = gather_all(block)
    return unpack(pieces, segments, spots(weights), shapes), pieces[-1][0]


def gather_weights(weights, vectors):
    if weights[0].shape[1] % 128:
        wide = [lax.all_gather(w, "batch", axis=1, tiled=True) for w in weights]
        wide = [lax.all_gather(w, "seq", axis=0, tiled=True) for w in wide]
        return wide, [lax.all_gather(v, "seq", axis=0, tiled=True) for v in vectors]
    first, last = gather_group(weights[:3], vectors)
    second, _ = gather_group(weights[3:], [], last)
    sizes = [v.shape[0] for v in vectors]
    flat = first[3].reshape(lax.axis_size("seq"), VEC_ROWS * 128)
    wide = []
    at = 0
    for size in sizes:
        wide.append(flat[:, at : at + size].reshape(-1))
        at += size
    return first[:3] + second, wide


def reduce_group(weights, grads, vectors=None):
    segments = columns(weights)
    arrays = list(grads)
    if vectors:
        count = lax.axis_size("seq")
        flat = jnp.concatenate([v.reshape(count, -1) for v in vectors], 1)
        flat = flat.reshape(count, -1, 128)
        flat = jnp.pad(flat, ((0, 0), (0, VEC_ROWS // 2 - flat.shape[1]), (0, 0)))
        high = lax.reduce_precision(flat, 8, 7)
        arrays.append(jnp.concatenate([high, flat - high], 1).reshape(-1, 128))
        segments = segments + [("vec", VEC_ROWS)]
    halves = pack(arrays, segments, spots(weights))
    rows = reduce_all(halves, bool(vectors))
    outs = []
    at = 0
    for weight in weights:
        parts = []
        for _ in range(weight.shape[1] // 128):
            parts.append(rows[at : at + weight.shape[0]])
            at += weight.shape[0]
        outs.append(parts[0] if len(parts) == 1 else jnp.concatenate(parts, 1))
    if vectors:
        flat = rows[at:].reshape(-1)
        at = 0
        for v in vectors:
            size = v.shape[0] // lax.axis_size("seq")
            outs.append(flat[at : at + size])
            at += size
    return outs


def reduce_plain(weights, grads, vectors):
    outs = [
        lax.psum_scatter(g.astype(BF16), "batch", scatter_dimension=1, tiled=True).astype(F32)
        for g in grads
    ]
    outs = outs + list(lax.psum(tuple(vectors), "batch"))
    return [lax.psum_scatter(o, "seq", scatter_dimension=0, tiled=True) for o in outs]


def layer_norm(values, gain, shift):
    centre = jnp.mean(values, -1, keepdims=True)
    centred = values - centre
    variance = jnp.mean(centred * centred, -1, keepdims=True)
    return centred * lax.rsqrt(variance + 1e-05) * gain + shift


def gelu_exact(values):
    return jax.nn.gelu(values, approximate=False)


def local(
    inputs,
    cotangent,
    query_weight,
    key_weight,
    value_weight,
    out_weight,
    up_weight,
    down_weight,
    norm1_gain,
    norm1_bias,
    norm2_gain,
    norm2_bias,
    out_bias,
    up_bias,
    down_bias,
):
    shards = [query_weight, key_weight, value_weight, out_weight, up_weight, down_weight]
    slices = [norm1_gain, norm1_bias, norm2_gain, norm2_bias, out_bias, up_bias, down_bias]
    wide, gathered = gather_weights(shards, slices)
    w_query, w_key, w_value, w_out, w_up, w_down = wide
    gain_one, bias_one, gain_two, bias_two, bias_out, bias_up, bias_down = [
        member.astype(jnp.float32) for member in gathered
    ]
    seq_count, block_len, model_width = inputs.shape
    row_count = seq_count * block_len
    half_span = block_len // 2
    score_scale = HEAD ** (-0.5)
    flat_in = inputs.astype(jnp.float32).reshape(row_count, model_width)
    normed = layer_norm(flat_in, gain_one, bias_one).astype(jnp.bfloat16)
    queries = jnp.dot(normed, w_query, preferred_element_type=jnp.float32).astype(jnp.bfloat16)
    key_full = jnp.dot(normed, w_key, preferred_element_type=jnp.float32)
    value_full = jnp.dot(normed, w_value, preferred_element_type=jnp.float32)
    pooled = jnp.concatenate(
        [
            jnp.mean(key_full.reshape(seq_count, 2, half_span, model_width), 2),
            jnp.mean(value_full.reshape(seq_count, 2, half_span, model_width), 2),
        ],
        -1,
    )
    pooled = jnp.transpose(pooled, (1, 0, 2)).astype(jnp.bfloat16)
    summaries = gather_seq(pooled).reshape(-1, seq_count, 2 * model_width)
    sum_count = summaries.shape[0]
    sum_keys = summaries[:, :, :model_width].reshape(sum_count, seq_count, HEADS, HEAD)
    sum_values = summaries[:, :, model_width:].reshape(sum_count, seq_count, HEADS, HEAD)
    query_heads = queries.reshape(seq_count, block_len, HEADS, HEAD)
    key_heads = key_full.astype(jnp.bfloat16).reshape(seq_count, block_len, HEADS, HEAD)
    value_heads = value_full.astype(jnp.bfloat16).reshape(seq_count, block_len, HEADS, HEAD)
    here = lax.axis_index("seq")
    marks = jnp.array([s for s, _ in relative_ids(seq_stages())], jnp.int32)
    visible = jnp.repeat(marks ^ here, 2) < here

    def score_pair():
        direct = (
            jnp.einsum(
                "sqhe,skhe->shqk", query_heads, key_heads, preferred_element_type=jnp.float32
            )
            * score_scale
        )
        remote = (
            jnp.einsum("sqhe,jshe->shqj", query_heads, sum_keys, preferred_element_type=jnp.float32)
            * score_scale
        )
        return (direct, jnp.where(visible, remote, -1e30))

    direct, remote = score_pair()
    row_top = jnp.maximum(jnp.max(direct, -1), jnp.max(remote, -1))[..., None]
    log_total = row_top + jnp.log(
        jnp.sum(jnp.exp(direct - row_top), -1, keepdims=True)
        + jnp.sum(jnp.exp(remote - row_top), -1, keepdims=True)
    )
    near_low = jnp.exp(direct - log_total).astype(jnp.bfloat16)
    far_low = jnp.exp(remote - log_total).astype(jnp.bfloat16)
    mixed = jnp.einsum("shqk,skhe->sqhe", near_low, value_heads, preferred_element_type=jnp.float32)
    mixed = mixed + jnp.einsum(
        "shqj,jshe->sqhe", far_low, sum_values, preferred_element_type=jnp.float32
    )
    mixed = mixed.reshape(row_count, model_width).astype(jnp.bfloat16)
    middle = flat_in + (jnp.dot(mixed, w_out, preferred_element_type=jnp.float32) + bias_out)
    normed_two = layer_norm(middle, gain_two, bias_two).astype(jnp.bfloat16)
    hidden = jnp.dot(normed_two, w_up, preferred_element_type=jnp.float32) + bias_up
    active = gelu_exact(hidden).astype(jnp.bfloat16)
    final = middle + (jnp.dot(active, w_down, preferred_element_type=jnp.float32) + bias_down)
    outputs = final.astype(jnp.bfloat16).reshape(seq_count, block_len, model_width)
    tangent = cotangent.reshape(row_count, model_width)
    feed_grad = tangent.astype(jnp.bfloat16)
    down_grad = jnp.einsum("ra,rb->ab", active, feed_grad, preferred_element_type=jnp.float32)
    down_bias_grad = jnp.sum(feed_grad.astype(jnp.float32), 0)
    active_grad = jnp.einsum("rb,ab->ra", feed_grad, w_down, preferred_element_type=jnp.float32)
    hidden_grad = jax.vjp(gelu_exact, hidden)[1](active_grad)[0].astype(jnp.bfloat16)
    up_grad = jnp.einsum("rd,rf->df", normed_two, hidden_grad, preferred_element_type=jnp.float32)
    up_bias_grad = jnp.sum(hidden_grad.astype(jnp.float32), 0)
    normed_two_grad = jnp.einsum("rf,df->rd", hidden_grad, w_up, preferred_element_type=jnp.float32)
    middle_part, gain_two_grad, bias_two_grad = jax.vjp(layer_norm, middle, gain_two, bias_two)[1](
        normed_two_grad
    )
    middle_grad = tangent + middle_part
    branch_grad = middle_grad.astype(jnp.bfloat16)
    out_bias_grad = jnp.sum(branch_grad.astype(jnp.float32), 0)
    out_grad = jnp.einsum("ra,rb->ab", mixed, branch_grad, preferred_element_type=jnp.float32)
    mixed_grad = jnp.einsum(
        "rb,ab->ra", branch_grad, w_out, preferred_element_type=jnp.float32
    ).astype(jnp.bfloat16)
    mixed_grad = mixed_grad.reshape(seq_count, block_len, HEADS, HEAD)
    direct, remote = score_pair()
    near_probs = jnp.exp(direct - log_total)
    far_probs = jnp.exp(remote - log_total)
    near_dots = jnp.einsum(
        "sqhe,skhe->shqk", mixed_grad, value_heads, preferred_element_type=jnp.float32
    )
    far_dots = jnp.einsum(
        "sqhe,jshe->shqj", mixed_grad, sum_values, preferred_element_type=jnp.float32
    )
    row_dot = jnp.sum(near_probs * near_dots, -1, keepdims=True) + jnp.sum(
        far_probs * far_dots, -1, keepdims=True
    )
    near_scores = (near_probs * (near_dots - row_dot)).astype(jnp.bfloat16)
    far_scores = (far_probs * (far_dots - row_dot)).astype(jnp.bfloat16)
    query_act = jnp.einsum(
        "shqk,skhe->sqhe", near_scores, key_heads, preferred_element_type=jnp.float32
    )
    query_act = query_act + jnp.einsum(
        "shqj,jshe->sqhe", far_scores, sum_keys, preferred_element_type=jnp.float32
    )
    query_act = (score_scale * query_act).reshape(row_count, model_width).astype(jnp.bfloat16)
    key_direct = score_scale * jnp.einsum(
        "shqk,sqhe->skhe", near_scores, query_heads, preferred_element_type=jnp.float32
    )
    value_direct = jnp.einsum(
        "shqk,sqhe->skhe", near_low, mixed_grad, preferred_element_type=jnp.float32
    )
    key_term = score_scale * jnp.einsum(
        "shqj,sqhe->jshe", far_scores, query_heads, preferred_element_type=jnp.float32
    )
    value_term = jnp.einsum(
        "shqj,sqhe->jshe", far_low, mixed_grad, preferred_element_type=jnp.float32
    )
    terms = jnp.concatenate(
        [
            key_term.reshape(-1, 2, seq_count, model_width),
            value_term.reshape(-1, 2, seq_count, model_width),
        ],
        -1,
    ).astype(jnp.bfloat16)
    owned = reduce_seq(terms)
    spread = jnp.transpose(owned, (1, 0, 2))[:, :, None, :] / half_span
    spread = jnp.broadcast_to(spread, (seq_count, 2, half_span, 2 * model_width)).reshape(
        row_count, 2 * model_width
    )
    key_act = (key_direct.reshape(row_count, model_width) + spread[:, :model_width]).astype(
        jnp.bfloat16
    )
    value_act = (value_direct.reshape(row_count, model_width) + spread[:, model_width:]).astype(
        jnp.bfloat16
    )
    query_grad = jnp.einsum("rd,re->de", normed, query_act, preferred_element_type=jnp.float32)
    key_grad = jnp.einsum("rd,re->de", normed, key_act, preferred_element_type=jnp.float32)
    value_grad = jnp.einsum("rd,re->de", normed, value_act, preferred_element_type=jnp.float32)
    normed_grad = jnp.einsum("re,de->rd", query_act, w_query, preferred_element_type=jnp.float32)
    normed_grad = normed_grad + jnp.einsum(
        "re,de->rd", key_act, w_key, preferred_element_type=jnp.float32
    )
    normed_grad = normed_grad + jnp.einsum(
        "re,de->rd", value_act, w_value, preferred_element_type=jnp.float32
    )
    input_part, gain_one_grad, bias_one_grad = jax.vjp(layer_norm, flat_in, gain_one, bias_one)[1](
        normed_grad
    )
    input_grad = (middle_grad + input_part).reshape(seq_count, block_len, model_width)
    first = [query_grad, key_grad, value_grad]
    second = [out_grad, up_grad, down_grad]
    vectors = [
        gain_one_grad,
        bias_one_grad,
        gain_two_grad,
        bias_two_grad,
        out_bias_grad,
        up_bias_grad,
        down_bias_grad,
    ]
    if query_weight.shape[1] % 128:
        reduced = reduce_plain(shards, first + second, vectors)
        matrices, vectors = reduced[:6], reduced[6:]
    else:
        tail = reduce_group(shards[3:], second)
        front = reduce_group(shards[:3], first, vectors)
        matrices, vectors = front[:3] + tail, front[3:]
    return (
        outputs,
        input_grad,
        matrices[0],
        matrices[1],
        matrices[2],
        matrices[3],
        matrices[4],
        matrices[5],
        vectors[0],
        vectors[1],
        vectors[2],
        vectors[3],
        vectors[4],
        vectors[5],
        vectors[6],
    )


def solution(mesh):
    placed = (
        P("batch", "seq", None),
        P("batch", "seq", None),
        P("seq", "batch"),
        P("seq", "batch"),
        P("seq", "batch"),
        P("seq", "batch"),
        P("seq", "batch"),
        P("seq", "batch"),
        P("seq"),
        P("seq"),
        P("seq"),
        P("seq"),
        P("seq"),
        P("seq"),
        P("seq"),
    )
    return jax.shard_map(
        local,
        mesh=mesh,
        in_specs=placed,
        out_specs=(
            P("batch", "seq", None),
            P("batch", "seq", None),
            P("seq", "batch"),
            P("seq", "batch"),
            P("seq", "batch"),
            P("seq", "batch"),
            P("seq", "batch"),
            P("seq", "batch"),
            P("seq"),
            P("seq"),
            P("seq"),
            P("seq"),
            P("seq"),
            P("seq"),
            P("seq"),
        ),
        check_vma=False,
    )
```

```python
import jax
import jax.numpy as jnp
from jax import lax
from jax.experimental import pallas as pl
from jax.experimental.pallas import tpu as pltpu
from jax.sharding import PartitionSpec as P

HEADS = 8
HEAD = 64
VEC_ROWS = 32
F32 = jnp.float32
BF16 = jnp.bfloat16


def swap(array, axis, bit):
    count = lax.axis_size(axis)
    return lax.ppermute(array, axis, [(i, i ^ bit) for i in range(count)])


def bits_down(count):
    return [1 << k for k in range(count.bit_length() - 2, -1, -1)]


def outer_stages():
    seq = [("seq", bit) for bit in bits_down(lax.axis_size("seq")) if bit > 1]
    batch = [("batch", bit) for bit in bits_down(lax.axis_size("batch")) if bit > 2]
    return batch + seq


def relative_ids(stages):
    ids = [(0, 0)]
    for axis, bit in stages:
        moved = [(s ^ bit, b) if axis == "seq" else (s, b ^ bit) for s, b in ids]
        ids = ids + moved
    return ids


X_STAGE = ("batch", 2)
Y_STAGE = ("seq", 1)
CORE = ("batch", 1)


def gather_all(pack):
    rows = pack.shape[0]
    half = rows // 2
    state = pack[None]
    outer = outer_stages()
    for stage in outer:
        state = jnp.concatenate([state, swap(state, *stage)], 0)
    pieces = []
    for first, order in ((0, (X_STAGE, Y_STAGE)), (half, (Y_STAGE, X_STAGE))):
        part = state[:, first : first + half]
        part = jnp.concatenate([part, swap(part, *order[0])], 0)
        far = swap(part, *order[1])
        ids = relative_ids(outer + [order[0]])
        full = relative_ids(outer + list(order))
        far_ids = full[len(ids) :]
        for piece, names in ((part, ids), (far, far_ids)):
            pieces.append((piece, names, first))
            pieces.append((swap(piece, *CORE), [(s, b ^ 1) for s, b in names], first))
    return pieces


def place():
    return jnp.stack([lax.axis_index("seq"), lax.axis_index("batch")]).astype(jnp.int32)


def cuts(segments, first, half):
    found = []
    at = 0
    for name, rows in segments:
        low, high = max(at, first), min(at + rows, first + half)
        if low < high:
            found.append((name, low - at, low - first, high - low))
        at += rows
    return found


def unpack(pieces, segments, targets, shapes):
    arrays = [piece for piece, _, _ in pieces]

    def kernel(spot, *refs):
        ins, outs = refs[: len(arrays)], refs[len(arrays) :]
        for ref, (piece, names, first) in zip(ins, pieces):
            for p, (sr, br) in enumerate(names):
                s, b = spot[0] ^ sr, spot[1] ^ br
                for name, row, here, size in cuts(segments, first, piece.shape[1]):
                    if name == "vec" and br != 0:
                        continue
                    number, top, left = targets(name, row, s, b)
                    outs[number][
                        pl.ds(pl.multiple_of(top, 16), size), pl.ds(pl.multiple_of(left, 128), 128)
                    ] = ref[p, here : here + size, :]

    return pl.pallas_call(
        kernel,
        out_shape=[jax.ShapeDtypeStruct(shape, BF16) for shape in shapes],
        in_specs=[pl.BlockSpec(memory_space=pltpu.SMEM)]
        + [pl.BlockSpec(memory_space=pltpu.VMEM) for _ in arrays],
        out_specs=[pl.BlockSpec(memory_space=pltpu.VMEM) for _ in shapes],
    )(place(), *arrays)


def pack_order():
    outer = outer_stages()
    return [
        relative_ids(outer + [Y_STAGE, X_STAGE, CORE]),
        relative_ids(outer + [X_STAGE, Y_STAGE, CORE]),
    ]


def write_packed(spot, ins, vec_block, outs, segments, targets, orders):
    half = sum(size for _, size in segments) // 2
    for out, names, first in zip(outs, orders, (0, half)):
        for p, (sr, br) in enumerate(names):
            s, b = spot[0] ^ sr, spot[1] ^ br
            for name, row, here, size in cuts(segments, first, half):
                if name == "vec":
                    out[p, here : here + size, :] = vec_block(s)
                else:
                    number, top, left = targets(name, row, s, b)
                    out[p, here : here + size, :] = ins[number][
                        pl.ds(pl.multiple_of(top, 16), size), pl.ds(pl.multiple_of(left, 128), 128)
                    ].astype(BF16)


def add_low(mine, theirs):
    return (mine.astype(F32) + theirs.astype(F32)).astype(BF16)


def join_pair(array):
    count = VEC_ROWS // 2
    return array[..., -VEC_ROWS:-count, :].astype(F32) + array[..., -count:, :].astype(F32)


def split_pair(total):
    high = lax.reduce_precision(total, 8, 7)
    return [high.astype(BF16), (total - high).astype(BF16)]


def add_pairs(mine, theirs):
    total = join_pair(mine) + join_pair(theirs)
    low = add_low(mine[..., :-VEC_ROWS, :], theirs[..., :-VEC_ROWS, :])
    return jnp.concatenate([low] + split_pair(total), -2)


def reduce_all(halves, pairs):
    outer = outer_stages()[::-1]
    done = []
    for k, (state, order) in enumerate(
        zip(halves, ((CORE, X_STAGE, Y_STAGE), (CORE, Y_STAGE, X_STAGE)))
    ):
        add = add_pairs if pairs and k == 1 else add_low
        stages = list(order) + outer
        for stage in stages:
            count = state.shape[0] // 2
            theirs = swap(state[count:], *stage)
            mine = state[:count]
            if stage is stages[-1]:
                if add is add_pairs:
                    total = join_pair(mine) + join_pair(theirs)
                    body = mine[:, :-VEC_ROWS].astype(F32) + theirs[:, :-VEC_ROWS].astype(F32)
                    state = jnp.concatenate([body, total], 1)
                else:
                    state = mine.astype(F32) + theirs.astype(F32)
            else:
                state = add(mine, theirs)
        done.append(state[0])
    return jnp.concatenate(done, 0)


def seq_stages():
    return [("seq", bit) for bit in bits_down(lax.axis_size("seq"))]


def gather_seq(array):
    state = array[None]
    for stage in seq_stages():
        state = jnp.concatenate([state, swap(state, *stage)], 0)
    return state


def reduce_seq(state):
    for stage in seq_stages()[::-1]:
        count = state.shape[0] // 2
        theirs = swap(state[count:], *stage)
        total = state[:count].astype(F32) + theirs.astype(F32)
        state = total if count == 1 else total.astype(BF16)
    return state[0]


def whole_tiles(weights, vectors):
    return (
        all(w.shape[0] % 16 == 0 and w.shape[1] % 128 == 0 for w in weights)
        and all(128 % v.shape[0] == 0 or v.shape[0] % 128 == 0 for v in vectors)
        and sum(v.shape[0] for v in vectors) % 128 == 0
    )


def columns(weights):
    return [
        ((i, c), weight.shape[0])
        for i, weight in enumerate(weights)
        for c in range(weight.shape[1] // 128)
    ]


def packed(weights):
    return [
        weight[:, c : c + 128] for weight in weights for c in range(0, weight.shape[1], 128)
    ]


def spots(weights):
    def targets(name, row, s, b):
        if name == "vec":
            return (len(weights), s * VEC_ROWS + row, 0)
        i, c = name
        rows, width = weights[i].shape
        return (i, s * rows + row, b * width + c * 128)

    return targets


def whole(weights):
    return [
        (w.shape[0] * lax.axis_size("seq"), w.shape[1] * lax.axis_size("batch")) for w in weights
    ]


def gather_group(weights, vectors, after=None):
    blocks = packed(weights)
    segments = columns(weights)
    shapes = whole(weights)
    if vectors:
        flat = jnp.concatenate(vectors).reshape(-1, 128)
        blocks = blocks + [jnp.pad(flat, ((0, VEC_ROWS - flat.shape[0]), (0, 0)))]
        segments = segments + [("vec", VEC_ROWS)]
        shapes = shapes + [(lax.axis_size("seq") * VEC_ROWS, 128)]
    block = jnp.concatenate(blocks, 0)
    if after is not None:
        block = lax.optimization_barrier((block, after))[0]
    pieces = gather_all(block)
    return unpack(pieces, segments, spots(weights), shapes), pieces[-1][0]


def gather_weights(weights, vectors):
    if not whole_tiles(weights, vectors):
        wide = [lax.all_gather(w, "batch", axis=1, tiled=True) for w in weights]
        wide = [lax.all_gather(w, "seq", axis=0, tiled=True) for w in wide]
        return wide, [lax.all_gather(v, "seq", axis=0, tiled=True) for v in vectors]
    first, last = gather_group(weights[:3], vectors)
    second, _ = gather_group(weights[3:], [], last)
    sizes = [v.shape[0] for v in vectors]
    flat = first[3].reshape(lax.axis_size("seq"), VEC_ROWS * 128)
    wide = []
    at = 0
    for size in sizes:
        wide.append(flat[:, at : at + size].reshape(-1))
        at += size
    return first[:3] + second, wide


def reduce_group(weights, halves, sizes):
    rows = reduce_all(halves, True)
    outs = []
    at = 0
    for weight in weights:
        parts = []
        for _ in range(weight.shape[1] // 128):
            parts.append(rows[at : at + weight.shape[0]])
            at += weight.shape[0]
        outs.append(parts[0] if len(parts) == 1 else jnp.concatenate(parts, 1))
    lanes = rows[at:]
    row = 0
    for size in sizes:
        if size < 128:
            part = lax.axis_index("seq") % (128 // size)
            outs.append(lax.dynamic_slice(lanes[row], (part * size,), (size,)))
            row += 1
        else:
            outs.append(lanes[row : row + size // 128].reshape(-1))
            row += size // 128
    return outs


def reduce_plain(weights, grads, vectors):
    outs = [
        lax.psum_scatter(g.astype(BF16), "batch", scatter_dimension=1, tiled=True).astype(F32)
        for g in grads
    ]
    outs = outs + list(lax.psum(tuple(vectors), "batch"))
    return [lax.psum_scatter(o, "seq", scatter_dimension=0, tiled=True) for o in outs]


def dot(left, right, a=1, b=0):
    return lax.dot_general(left, right, (((a,), (b,)), ((), ())), preferred_element_type=F32)


def norm_parts(values):
    centred = values - jnp.mean(values, -1, keepdims=True)
    scale = lax.rsqrt(jnp.mean(centred * centred, -1, keepdims=True) + 1e-05)
    return centred * scale, scale


def norm_back(grad, unit, scale, gain):
    inner = grad * gain
    pull = jnp.mean(inner, -1, keepdims=True)
    twist = jnp.mean(inner * unit, -1, keepdims=True)
    return scale * (inner - pull - unit * twist)


def gelu_pair(values):
    bell = jnp.exp(-0.5 * values * values)
    t = 1.0 / (1.0 + (0.3275911 * 0.5**0.5) * jnp.abs(values))
    poly = 1.061405429 * 0.5
    for factor in (-1.453152027, 1.421413741, -0.284496736, 0.254829592):
        poly = poly * t + factor * 0.5
    below = poly * t * bell
    share = jnp.where(values < 0, below, 1.0 - below)
    return values * share, share + values * bell * 0.3989422804014327


def full(shape):
    return pl.BlockSpec(shape, lambda i: (0,) * len(shape))


def each(shape):
    return pl.BlockSpec((1,) + tuple(shape[1:]), lambda i: (i,) + (0,) * (len(shape) - 1))


def project(inputs, w_query, w_key, w_value, gain, shift):
    count, rows, width = inputs.shape
    half = rows // 2

    def kernel(x_ref, q_ref, k_ref, v_ref, gain_ref, shift_ref, out_ref, pooled_ref):
        unit, _ = norm_parts(x_ref[0].astype(F32))
        normed = (unit * gain_ref[...] + shift_ref[...]).astype(BF16)
        out_ref[0, :, :width] = dot(normed, q_ref[...]).astype(BF16)
        for k, ref in enumerate((k_ref, v_ref)):
            product = dot(normed, ref[...])
            out_ref[0, :, (k + 1) * width : (k + 2) * width] = product.astype(BF16)
            for j in range(2):
                mean = jnp.sum(product[j * half : (j + 1) * half], 0, keepdims=True) / half
                pooled_ref[0, j : j + 1, k * width : (k + 1) * width] = mean.astype(BF16)

    shapes = [(count, rows, 3 * width), (count, 2, 2 * width)]
    return pl.pallas_call(
        kernel,
        grid=(count,),
        in_specs=[each(inputs.shape)] + [full((width, width))] * 3 + [full((1, width))] * 2,
        out_specs=[each(shape) for shape in shapes],
        out_shape=[jax.ShapeDtypeStruct(shape, BF16) for shape in shapes],
    )(inputs, w_query, w_key, w_value, gain, shift)


def head_mask(rows, lane_half):
    lane = lax.broadcasted_iota(jnp.int32, (rows, 2 * HEAD), 1)
    return (lane < HEAD) if lane_half == 0 else (lane >= HEAD)


def only(array, lane_half):
    return jnp.where(head_mask(array.shape[0], lane_half), array, jnp.zeros_like(array))


def scores_of(keys, query, visible, rows):
    scores = dot(keys, query, 1, 1) * HEAD ** (-0.5)
    far = jnp.where(visible > 0, scores[rows:], -1e30)
    return jnp.concatenate([scores[:rows], far], 0)


def attend(qkv, summaries, visible, inputs, w_out, bias_out):
    count, rows, width = inputs.shape
    far = summaries.shape[1]

    def kernel(qkv_ref, sum_ref, vis_ref, x_ref, w_ref, bias_ref, mixed_ref, lse_ref, middle_ref):
        seen = vis_ref[...]
        for pair in range(HEADS // 2):
            at = pair * 2 * HEAD
            query = qkv_ref[0, :, at : at + 2 * HEAD]
            keys = jnp.concatenate(
                [
                    qkv_ref[0, :, width + at : width + at + 2 * HEAD],
                    sum_ref[0, :, at : at + 2 * HEAD],
                ],
                0,
            )
            values = jnp.concatenate(
                [
                    qkv_ref[0, :, 2 * width + at : 2 * width + at + 2 * HEAD],
                    sum_ref[0, :, width + at : width + at + 2 * HEAD],
                ],
                0,
            )
            total = None
            for side in range(2):
                scores = scores_of(keys, only(query, side), seen, rows)
                top = jnp.max(scores, 0, keepdims=True)
                powers = jnp.exp(scores - top)
                mass = jnp.sum(powers, 0, keepdims=True)
                head = 2 * pair + side
                lse_ref[0, head : head + 1, :] = top + jnp.log(mass)
                probs = (powers * (1.0 / mass)).astype(BF16)
                part = dot(only(values, side), probs, 0, 0)
                total = part if total is None else total + part
            mixed_ref[0, :, at : at + 2 * HEAD] = total.T.astype(BF16)
        branch = dot(mixed_ref[0], w_ref[...]) + bias_ref[...]
        middle_ref[0] = x_ref[0].astype(F32) + branch

    return pl.pallas_call(
        kernel,
        grid=(count,),
        in_specs=[
            each(qkv.shape),
            each(summaries.shape),
            full((far, rows)),
            each(inputs.shape),
            full((width, width)),
            full((1, width)),
        ],
        out_specs=[each(inputs.shape), each((count, HEADS, rows)), each(inputs.shape)],
        out_shape=[
            jax.ShapeDtypeStruct(inputs.shape, BF16),
            jax.ShapeDtypeStruct((count, HEADS, rows), F32),
            jax.ShapeDtypeStruct(inputs.shape, F32),
        ],
    )(qkv, summaries, visible, inputs, w_out, bias_out)


def split_rows(total):
    high = total.astype(BF16).astype(F32)
    return high, total - high


def vector_block(narrow, wide, per):
    def block(s):
        left = pl.multiple_of(s * per // 128 * 128, 128)
        found = narrow[:, pl.ds(left, 128)]
        if wide is not None:
            step = wide.shape[1] // narrow.shape[1] * per
            for k in range(step // 128):
                chunk = wide[:, pl.ds(pl.multiple_of(s * step + k * 128, 128), 128)]
                row = lax.broadcasted_iota(jnp.int32, chunk.shape, 0)
                keep = (row % (VEC_ROWS // 2)) == 4 + k
                found = found + jnp.where(keep, chunk, 0.0)
        return found.astype(BF16)

    return block


def feed(
    middle, cotangent, mixed, w_out, w_up, w_down, gain, shift, bias_up, bias_down, shards, tiles
):
    count, rows, width = middle.shape
    hidden_width = w_up.shape[1]
    step = 512
    grads = [(width, width), (width, hidden_width), (hidden_width, width)]
    segments = columns(shards) + [("vec", VEC_ROWS)]
    targets = spots(shards)
    orders = pack_order() if tiles else None
    half = sum(size for _, size in segments) // 2
    per = width // lax.axis_size("seq")

    def kernel(spot, middle_ref, cot_ref, mixed_ref, wo_ref, wu_ref, wd_ref, gain_ref, shift_ref,
               bu_ref, bd_ref, out_ref, mgrad_ref, xgrad_ref, narrow_ref, wide_ref, *rest):
        if tiles:
            packs, (go_ref, gu_ref, gd_ref, high_ref, long_ref) = rest[:2], rest[2:]
        else:
            go_ref, gu_ref, gd_ref = rest
        step_id = pl.program_id(0)

        @pl.when(step_id == 0)
        def _():
            for ref in (go_ref, gu_ref, gd_ref, narrow_ref, wide_ref):
                ref[...] = jnp.zeros_like(ref)

        middle = middle_ref[0]
        cot = cot_ref[0]
        tangent = cot.astype(BF16)
        unit, scale = norm_parts(middle)
        normed = (unit * gain_ref[...] + shift_ref[...]).astype(BF16)
        flipped = normed.T
        final = middle + bd_ref[...]
        back = None
        for at in range(0, hidden_width, step):
            here = slice(at, at + step)
            hidden = dot(normed, wu_ref[:, here]) + bu_ref[:, here]
            active, slope = gelu_pair(hidden)
            active = active.astype(BF16)
            final = final + dot(active, wd_ref[here, :])
            gd_ref[here, :] += dot(active, tangent, 0, 0)
            grad = (dot(tangent, wd_ref[here, :], 1, 1) * slope).astype(BF16)
            gu_ref[:, here] += dot(flipped, grad)
            wide_ref[0:1, here] += jnp.sum(grad.astype(F32), 0, keepdims=True)
            part = dot(grad, wu_ref[:, here], 1, 1)
            back = part if back is None else back + part
        out_ref[0] = final.astype(BF16)
        narrow_ref[0:1, :] += jnp.sum(back * unit, 0, keepdims=True)
        narrow_ref[1:2, :] += jnp.sum(back, 0, keepdims=True)
        middle_grad = cot + norm_back(back, unit, scale, gain_ref[...])
        mgrad_ref[0] = middle_grad
        branch = middle_grad.astype(BF16)
        narrow_ref[2:3, :] += jnp.sum(branch.astype(F32), 0, keepdims=True)
        narrow_ref[3:4, :] += jnp.sum(tangent.astype(F32), 0, keepdims=True)
        go_ref[...] += dot(mixed_ref[0], branch, 0, 0)
        xgrad_ref[0] = dot(branch, wo_ref[...], 1, 1).astype(BF16)

        if tiles:

            @pl.when(step_id == count - 1)
            def _():
                for ref, source, k in ((high_ref, narrow_ref, 8), (long_ref, wide_ref, 1)):
                    high, low = split_rows(source[...])
                    zero = jnp.zeros((8, source.shape[1]), F32)
                    if k == 1:
                        high = jnp.broadcast_to(high[0:1], zero.shape)
                        low = jnp.broadcast_to(low[0:1], zero.shape)
                    ref[...] = jnp.concatenate([high, zero, low, zero], 0)
                write_packed(
                    spot,
                    (go_ref, gu_ref, gd_ref),
                    vector_block(high_ref, long_ref, per),
                    packs,
                    segments,
                    targets,
                    orders,
                )

    block = middle.shape
    out_shape = [
        jax.ShapeDtypeStruct(block, BF16),
        jax.ShapeDtypeStruct(block, F32),
        jax.ShapeDtypeStruct(block, BF16),
        jax.ShapeDtypeStruct((8, width), F32),
        jax.ShapeDtypeStruct((8, hidden_width), F32),
    ]
    out_specs = [each(block)] * 3 + [full((8, width)), full((8, hidden_width))]
    scratch = []
    if tiles:
        out_shape += [jax.ShapeDtypeStruct((len(names), half, 128), BF16) for names in orders]
        out_specs += [full((len(names), half, 128)) for names in orders]
        scratch = [pltpu.VMEM(shape, F32) for shape in grads]
        scratch += [pltpu.VMEM((VEC_ROWS, width), F32), pltpu.VMEM((VEC_ROWS, hidden_width), F32)]
    else:
        out_shape += [jax.ShapeDtypeStruct(shape, F32) for shape in grads]
        out_specs += [full(shape) for shape in grads]
    return pl.pallas_call(
        kernel,
        grid=(count,),
        in_specs=[pl.BlockSpec(memory_space=pltpu.SMEM)]
        + [each(block)] * 3
        + [full(shape) for shape in ((width, width), (width, hidden_width), (hidden_width, width))]
        + [full((1, width)), full((1, width)), full((1, hidden_width)), full((1, width))],
        out_specs=out_specs,
        out_shape=out_shape,
        scratch_shapes=scratch,
    )(
        place(), middle, cotangent, mixed, w_out, w_up, w_down, gain, shift, bias_up, bias_down
    )


def attend_back(qkv, summaries, visible, lse, mixed_grad):
    count, rows, width = mixed_grad.shape
    far = summaries.shape[1]

    def kernel(qkv_ref, sum_ref, vis_ref, lse_ref, grad_ref, dq_ref, dk_ref, dv_ref, far_ref):
        seen = vis_ref[...]
        for pair in range(HEADS // 2):
            at = pair * 2 * HEAD
            lanes = slice(at, at + 2 * HEAD)
            query = qkv_ref[0, :, lanes]
            pull = grad_ref[0, :, lanes]
            keys = jnp.concatenate(
                [qkv_ref[0, :, width + at : width + at + 2 * HEAD], sum_ref[0, :, lanes]], 0
            )
            values = jnp.concatenate(
                [
                    qkv_ref[0, :, 2 * width + at : 2 * width + at + 2 * HEAD],
                    sum_ref[0, :, width + at : width + at + 2 * HEAD],
                ],
                0,
            )
            d_query = d_keys = d_values = 0.0
            for side in range(2):
                head = 2 * pair + side
                own = only(query, side)
                own_pull = only(pull, side)
                scores = scores_of(keys, own, seen, rows)
                probs = jnp.exp(scores - lse_ref[0, head : head + 1, :])
                dots = dot(values, own_pull, 1, 1)
                centre = jnp.sum(probs * dots, 0, keepdims=True)
                slope = (probs * (dots - centre)).astype(BF16)
                d_values = d_values + dot(probs.astype(BF16), own_pull)
                d_keys = d_keys + dot(slope, own)
                d_query = d_query + dot(only(keys, side), slope, 0, 0)
            d_keys = d_keys * HEAD ** (-0.5)
            dq_ref[0, :, lanes] = (d_query * HEAD ** (-0.5)).T.astype(BF16)
            dk_ref[0, :, lanes] = d_keys[:rows]
            dv_ref[0, :, lanes] = d_values[:rows]
            far_ref[0, :, lanes] = d_keys[rows:].astype(BF16)
            far_ref[0, :, width + at : width + at + 2 * HEAD] = d_values[rows:].astype(BF16)

    block = mixed_grad.shape
    return pl.pallas_call(
        kernel,
        grid=(count,),
        in_specs=[
            each(qkv.shape),
            each(summaries.shape),
            full((far, rows)),
            each(lse.shape),
            each(block),
        ],
        out_specs=[each(block)] * 3 + [each(summaries.shape)],
        out_shape=[
            jax.ShapeDtypeStruct(block, BF16),
            jax.ShapeDtypeStruct(block, F32),
            jax.ShapeDtypeStruct(block, F32),
            jax.ShapeDtypeStruct(summaries.shape, BF16),
        ],
    )(qkv, summaries, visible, lse, mixed_grad)


def project_back(
    inputs, d_query, d_keys, d_values, owned, weights, gain, shift, middle_grad, shards, tiles
):
    count, rows, width = inputs.shape
    half_span = rows // 2
    segments = columns(shards) + [("vec", VEC_ROWS)]
    targets = spots(shards)
    orders = pack_order() if tiles else None
    half = sum(size for _, size in segments) // 2
    per = width // lax.axis_size("seq")

    def kernel(spot, x_ref, dq_ref, dk_ref, dv_ref, own_ref, wq_ref, wk_ref, wv_ref, gain_ref,
               shift_ref, mgrad_ref, igrad_ref, narrow_ref, *rest):
        if tiles:
            packs, (gq_ref, gk_ref, gv_ref, high_ref) = rest[:2], rest[2:]
        else:
            gq_ref, gk_ref, gv_ref = rest
        step_id = pl.program_id(0)

        @pl.when(step_id == 0)
        def _():
            for ref in (gq_ref, gk_ref, gv_ref, narrow_ref):
                ref[...] = jnp.zeros_like(ref)

        unit, scale = norm_parts(x_ref[0].astype(F32))
        flipped = (unit * gain_ref[...] + shift_ref[...]).astype(BF16).T
        back = dot(dq_ref[0], wq_ref[...], 1, 1)
        gq_ref[...] += dot(flipped, dq_ref[0])
        for k, (direct, w_ref, g_ref) in enumerate(
            ((dk_ref, wk_ref, gk_ref), (dv_ref, wv_ref, gv_ref))
        ):
            act = jnp.concatenate(
                [
                    direct[0, j * half_span : (j + 1) * half_span, :]
                    + own_ref[0, j : j + 1, k * width : (k + 1) * width] / half_span
                    for j in range(2)
                ],
                0,
            ).astype(BF16)
            g_ref[...] += dot(flipped, act)
            back = back + dot(act, w_ref[...], 1, 1)
        narrow_ref[0:1, :] += jnp.sum(back * unit, 0, keepdims=True)
        narrow_ref[1:2, :] += jnp.sum(back, 0, keepdims=True)
        igrad_ref[0] = mgrad_ref[0] + norm_back(back, unit, scale, gain_ref[...])

        if tiles:

            @pl.when(step_id == count - 1)
            def _():
                high, low = split_rows(narrow_ref[...])
                zero = jnp.zeros_like(high)
                high_ref[...] = jnp.concatenate([high, zero, low, zero], 0)
                write_packed(
                    spot,
                    (gq_ref, gk_ref, gv_ref),
                    vector_block(high_ref, None, per),
                    packs,
                    segments,
                    targets,
                    orders,
                )

    block = inputs.shape
    square = (width, width)
    out_shape = [jax.ShapeDtypeStruct(block, F32), jax.ShapeDtypeStruct((8, width), F32)]
    out_specs = [each(block), full((8, width))]
    scratch = []
    if tiles:
        out_shape += [jax.ShapeDtypeStruct((len(names), half, 128), BF16) for names in orders]
        out_specs += [full((len(names), half, 128)) for names in orders]
        scratch = [pltpu.VMEM(square, F32)] * 3 + [pltpu.VMEM((VEC_ROWS, width), F32)]
    else:
        out_shape += [jax.ShapeDtypeStruct(square, F32)] * 3
        out_specs += [full(square)] * 3
    return pl.pallas_call(
        kernel,
        grid=(count,),
        in_specs=[pl.BlockSpec(memory_space=pltpu.SMEM)]
        + [each(block)] * 4
        + [each(owned.shape)]
        + [full(square)] * 3
        + [full((1, width))] * 2
        + [each(block)],
        out_specs=out_specs,
        out_shape=out_shape,
        scratch_shapes=scratch,
    )(place(), inputs, d_query, d_keys, d_values, owned, *weights, gain, shift, middle_grad)


def local(
    inputs,
    cotangent,
    query_weight,
    key_weight,
    value_weight,
    out_weight,
    up_weight,
    down_weight,
    norm1_gain,
    norm1_bias,
    norm2_gain,
    norm2_bias,
    out_bias,
    up_bias,
    down_bias,
):
    shards = [query_weight, key_weight, value_weight, out_weight, up_weight, down_weight]
    slices = [norm1_gain, norm1_bias, norm2_gain, norm2_bias, out_bias, up_bias, down_bias]
    tiles = whole_tiles(shards, slices)
    wide, gathered = gather_weights(shards, slices)
    w_query, w_key, w_value, w_out, w_up, w_down = wide
    gain_one, bias_one, gain_two, bias_two, bias_out, bias_up, bias_down = [
        member.astype(F32)[None] for member in gathered
    ]
    count, rows, width = inputs.shape
    qkv, pooled = project(inputs, w_query, w_key, w_value, gain_one, bias_one)
    summaries = jnp.transpose(gather_seq(pooled), (1, 0, 2, 3)).reshape(count, -1, 2 * width)
    here = lax.axis_index("seq")
    marks = jnp.array([s for s, _ in relative_ids(seq_stages())], jnp.int32)
    visible = jnp.repeat((marks ^ here) < here, 2).astype(F32)
    visible = jnp.broadcast_to(visible[:, None], (visible.shape[0], rows))
    mixed, lse, middle = attend(qkv, summaries, visible, inputs, w_out, bias_out)
    outputs, middle_grad, mixed_grad, narrow_two, wide_two, *second = feed(
        middle,
        cotangent,
        mixed,
        w_out,
        w_up,
        w_down,
        gain_two,
        bias_two,
        bias_up,
        bias_down,
        shards[3:],
        tiles,
    )
    d_query, d_keys, d_values, terms = attend_back(qkv, summaries, visible, lse, mixed_grad)
    terms = jnp.transpose(terms.reshape(count, -1, 2, 2 * width), (1, 0, 2, 3))
    owned = reduce_seq(terms)
    input_grad, narrow_one, *first = project_back(
        inputs,
        d_query,
        d_keys,
        d_values,
        owned,
        (w_query, w_key, w_value),
        gain_one,
        bias_one,
        middle_grad,
        shards[:3],
        tiles,
    )
    if tiles:
        size = norm1_gain.shape[0]
        tail = reduce_group(shards[3:], second, [size] * 4 + [up_bias.shape[0]])
        front = reduce_group(shards[:3], first, [size] * 2)
        matrices = front[:3] + tail[:3]
        vectors = front[3:] + tail[3:6] + [tail[7], tail[6]]
    else:
        vectors = [
            narrow_one[0],
            narrow_one[1],
            narrow_two[0],
            narrow_two[1],
            narrow_two[2],
            wide_two[0],
            narrow_two[3],
        ]
        reduced = reduce_plain(shards, list(first) + list(second), vectors)
        matrices, vectors = reduced[:6], reduced[6:]
    return (outputs, input_grad, *matrices, *vectors)


def solution(mesh):
    placed = (
        P("batch", "seq", None),
        P("batch", "seq", None),
        P("seq", "batch"),
        P("seq", "batch"),
        P("seq", "batch"),
        P("seq", "batch"),
        P("seq", "batch"),
        P("seq", "batch"),
        P("seq"),
        P("seq"),
        P("seq"),
        P("seq"),
        P("seq"),
        P("seq"),
        P("seq"),
    )
    return jax.shard_map(
        local,
        mesh=mesh,
        in_specs=placed,
        out_specs=(
            P("batch", "seq", None),
            P("batch", "seq", None),
            P("seq", "batch"),
            P("seq", "batch"),
            P("seq", "batch"),
            P("seq", "batch"),
            P("seq", "batch"),
            P("seq", "batch"),
            P("seq"),
            P("seq"),
            P("seq"),
            P("seq"),
            P("seq"),
            P("seq"),
            P("seq"),
        ),
        check_vma=False,
    )
```

```python
import jax
import jax.numpy as jnp
from jax import lax
from jax.experimental import pallas as pl
from jax.experimental.pallas import tpu as pltpu
from jax.sharding import PartitionSpec as P

HEADS = 8
HEAD = 64
VEC_ROWS = 32
F32 = jnp.float32
BF16 = jnp.bfloat16


def swap(array, axis, bit):
    count = lax.axis_size(axis)
    return lax.ppermute(array, axis, [(i, i ^ bit) for i in range(count)])


def bits_down(count):
    return [1 << k for k in range(count.bit_length() - 2, -1, -1)]


def outer_stages():
    seq = [("seq", bit) for bit in bits_down(lax.axis_size("seq")) if bit > 1]
    batch = [("batch", bit) for bit in bits_down(lax.axis_size("batch")) if bit > 2]
    return batch + seq


def relative_ids(stages):
    ids = [(0, 0)]
    for axis, bit in stages:
        moved = [(s ^ bit, b) if axis == "seq" else (s, b ^ bit) for s, b in ids]
        ids = ids + moved
    return ids


X_STAGE = ("batch", 2)
Y_STAGE = ("seq", 1)
CORE = ("batch", 1)


def gather_outer(state):
    for stage in outer_stages():
        state = jnp.concatenate([state, swap(state, *stage)], 0)
    return state


def gather_inner(state):
    half = state.shape[1] // 2
    outer = outer_stages()
    pieces = []
    for first, order in ((0, (X_STAGE, Y_STAGE)), (half, (Y_STAGE, X_STAGE))):
        part = state[:, first : first + half]
        part = jnp.concatenate([part, swap(part, *order[0])], 0)
        far = swap(part, *order[1])
        ids = relative_ids(outer + [order[0]])
        full = relative_ids(outer + list(order))
        far_ids = full[len(ids) :]
        for piece, names in ((part, ids), (far, far_ids)):
            pieces.append((piece, names, first))
            pieces.append((swap(piece, *CORE), [(s, b ^ 1) for s, b in names], first))
    return pieces


def place():
    return jnp.stack([lax.axis_index("seq"), lax.axis_index("batch")]).astype(jnp.int32)


def cuts(segments, first, half):
    found = []
    at = 0
    for name, rows in segments:
        low, high = max(at, first), min(at + rows, first + half)
        if low < high:
            found.append((name, low - at, low - first, high - low))
        at += rows
    return found


def assemble(spot, refs, pieces, segments, targets, outs, vec):
    for ref, (piece, names, first) in zip(refs, pieces):
        for p, (sr, br) in enumerate(names):
            s, b = spot[0] ^ sr, spot[1] ^ br
            for name, row, here, size in cuts(segments, first, piece.shape[1]):
                if name == "vec":
                    if br == 0:
                        vec(ref[p, here : here + size, :], s)
                else:
                    number, top, left = targets(name, row, s, b)
                    outs[number][
                        pl.ds(pl.multiple_of(top, 16), size), pl.ds(pl.multiple_of(left, 128), 128)
                    ] = ref[p, here : here + size, :]


def pack_order():
    outer = outer_stages()
    return [
        relative_ids(outer + [Y_STAGE, X_STAGE, CORE]),
        relative_ids(outer + [X_STAGE, Y_STAGE, CORE]),
    ]


def write_packed(spot, ins, vec_block, outs, segments, targets, orders):
    half = sum(size for _, size in segments) // 2
    for k, (names, first) in enumerate(zip(orders, (0, half))):
        for p, (sr, br) in enumerate(names):
            s, b = spot[0] ^ sr, spot[1] ^ br
            out = outs[2 * k + p // (len(names) // 2)]
            p = p % (len(names) // 2)
            for name, row, here, size in cuts(segments, first, half):
                if name == "vec":
                    out[p, here : here + size, :] = vec_block(s)
                else:
                    number, top, left = targets(name, row, s, b)
                    out[p, here : here + size, :] = ins[number][
                        pl.ds(pl.multiple_of(top, 16), size), pl.ds(pl.multiple_of(left, 128), 128)
                    ].astype(BF16)


def add_low(mine, theirs):
    return (mine.astype(F32) + theirs.astype(F32)).astype(BF16)


def join_pair(array):
    count = VEC_ROWS // 2
    return array[..., -VEC_ROWS:-count, :].astype(F32) + array[..., -count:, :].astype(F32)


def split_pair(total):
    high = lax.reduce_precision(total, 8, 7)
    return [high.astype(BF16), (total - high).astype(BF16)]


def add_pairs(mine, theirs):
    total = join_pair(mine) + join_pair(theirs)
    low = add_low(mine[..., :-VEC_ROWS, :], theirs[..., :-VEC_ROWS, :])
    return jnp.concatenate([low] + split_pair(total), -2)


ORDERS = ((CORE, X_STAGE, Y_STAGE), (CORE, Y_STAGE, X_STAGE))


def reduce_step(halves, step, last=False):
    done = []
    for k, (kept, sent) in enumerate(halves):
        theirs = swap(sent, *ORDERS[k][step])
        if last:
            done.append((kept, theirs))
            continue
        state = (add_pairs if k == 1 else add_low)(kept, theirs)
        count = state.shape[0] // 2
        done.append((state[:count], state[count:]))
    return done


def sum_rows(mine, theirs, spans):
    total = mine.astype(F32) + theirs.astype(F32)
    count = VEC_ROWS // 2
    return total, [total[at : at + count] + total[at + count : at + VEC_ROWS] for at in spans]


def joined_sum(couples):
    count = couples[0][0].shape[0]
    rows = sum(kept.shape[1] for kept, _, _ in couples)

    def kernel(*refs):
        ins, outs = refs[:-2], refs[-2:]
        for p in range(count):
            out = outs[p // (count // 2)]
            at = 0
            for k, (kept, _, vectors) in enumerate(couples):
                size = kept.shape[1]
                total, pairs = sum_rows(
                    ins[2 * k][p], ins[2 * k + 1][p], [size - VEC_ROWS] if vectors else []
                )
                out[p % (count // 2), at : at + size, :] = total.astype(BF16)
                for pair in pairs:
                    high = pair.astype(BF16)
                    low = (pair - high.astype(F32)).astype(BF16)
                    end = at + size
                    out[p % (count // 2), end - VEC_ROWS : end - VEC_ROWS // 2, :] = high
                    out[p % (count // 2), end - VEC_ROWS // 2 : end, :] = low
                at += size

    arrays = [array for kept, theirs, _ in couples for array in (kept, theirs)]
    return pl.pallas_call(
        kernel,
        out_shape=[jax.ShapeDtypeStruct((count // 2, rows, 128), BF16)] * 2,
        in_specs=[pl.BlockSpec(memory_space=pltpu.VMEM)] * len(arrays),
        out_specs=[pl.BlockSpec(memory_space=pltpu.VMEM)] * 2,
    )(*arrays)


def again(kept, theirs, spans):
    count, rows = kept.shape[:2]

    def kernel(mine_ref, theirs_ref, *outs):
        for p in range(count):
            out = outs[p // (count // 2)]
            q = p % (count // 2)
            total, pairs = sum_rows(mine_ref[p], theirs_ref[p], spans)
            out[q] = total.astype(BF16)
            for pair, at in zip(pairs, spans):
                high = pair.astype(BF16)
                out[q, at : at + VEC_ROWS // 2, :] = high
                low = (pair - high.astype(F32)).astype(BF16)
                out[q, at + VEC_ROWS // 2 : at + VEC_ROWS, :] = low

    return pl.pallas_call(
        kernel,
        out_shape=[jax.ShapeDtypeStruct((count // 2, rows, 128), BF16)] * 2,
        in_specs=[pl.BlockSpec(memory_space=pltpu.VMEM)] * 2,
        out_specs=[pl.BlockSpec(memory_space=pltpu.VMEM)] * 2,
    )(kept, theirs)


def finish(kept, theirs, parts, spans, shapes):
    def kernel(mine_ref, theirs_ref, *outs):
        total, pairs = sum_rows(mine_ref[0], theirs_ref[0], spans)
        for number, row, left, at, size in parts:
            outs[number][row : row + size, left : left + 128] = total[at : at + size]
        for k, pair in enumerate(pairs):
            outs[len(shapes) + k][...] = pair

    return pl.pallas_call(
        kernel,
        out_shape=[jax.ShapeDtypeStruct(shape, F32) for shape in shapes]
        + [jax.ShapeDtypeStruct((VEC_ROWS // 2, 128), F32)] * len(spans),
        in_specs=[pl.BlockSpec(memory_space=pltpu.VMEM)] * 2,
        out_specs=[pl.BlockSpec(memory_space=pltpu.VMEM)] * (len(shapes) + len(spans)),
    )(kept, theirs)


def reduce_end(groups, weights):
    couples = []
    parts = []
    spans = []
    at = 0
    for numbers, halves in groups:
        segments = columns([weights[n] for n in numbers]) + [("vec", VEC_ROWS)]
        for k, (kept, theirs) in enumerate(halves):
            couples.append((kept, theirs, k == 1))
            half = kept.shape[1]
            for name, row, here, size in cuts(segments, k * half, half):
                if name == "vec":
                    spans.append(at + here)
                else:
                    parts.append((numbers[name[0]], row, name[1] * 128, at + here, size))
            at += half
    kept, sent = joined_sum(couples)
    stages = outer_stages()[::-1]
    for k, stage in enumerate(stages):
        theirs = swap(sent, *stage)
        if k < len(stages) - 1:
            kept, sent = again(kept, theirs, spans)
    return finish(kept, theirs, parts, spans, [w.shape for w in weights])


def seq_stages():
    return [("seq", bit) for bit in bits_down(lax.axis_size("seq"))]


def gather_seq(array):
    state = array[None]
    for stage in seq_stages():
        state = jnp.concatenate([state, swap(state, *stage)], 0)
    return state


def reduce_seq(state):
    for stage in seq_stages()[::-1]:
        count = state.shape[0] // 2
        theirs = swap(state[count:], *stage)
        total = state[:count].astype(F32) + theirs.astype(F32)
        state = total if count == 1 else total.astype(BF16)
    return state[0]


def whole_tiles(weights, vectors):
    return (
        all(w.shape[0] % 16 == 0 and w.shape[1] % 128 == 0 for w in weights)
        and all(128 % v.shape[0] == 0 or v.shape[0] % 128 == 0 for v in vectors)
        and sum(v.shape[0] for v in vectors) % 128 == 0
    )


def columns(weights):
    return [
        ((i, c), weight.shape[0])
        for i, weight in enumerate(weights)
        for c in range(weight.shape[1] // 128)
    ]


def packed(weights):
    return [
        weight[:, c : c + 128] for weight in weights for c in range(0, weight.shape[1], 128)
    ]


def spots(weights):
    def targets(name, row, s, b):
        if name == "vec":
            return (len(weights), s * VEC_ROWS + row, 0)
        i, c = name
        rows, width = weights[i].shape
        return (i, s * rows + row, b * width + c * 128)

    return targets


def whole(weights):
    return [
        (w.shape[0] * lax.axis_size("seq"), w.shape[1] * lax.axis_size("batch")) for w in weights
    ]


def pack_shards(weights, vectors, after=None):
    segments = columns(weights) + ([("vec", VEC_ROWS)] if vectors else [])
    rows = sum(size for _, size in segments)
    extra = [] if after is None else [after]

    def kernel(spot, *refs):
        out = refs[-1]
        at = 0
        for ref, weight in zip(refs, weights):
            for left in range(0, weight.shape[1], 128):
                out[0, at : at + weight.shape[0], :] = ref[:, left : left + 128]
                at += weight.shape[0]
        if not vectors:
            return
        found = []
        for ref in refs[len(weights) : len(weights) + len(vectors)]:
            size = ref.shape[0]
            line = ref[...].astype(F32)
            if size < 128:
                line = jnp.concatenate([line[None]] * (128 // size), 1)
                lane = lax.broadcasted_iota(jnp.int32, line.shape, 1)
                found.append(jnp.where(lane // size == spot[0] % (128 // size), line, 0.0))
            else:
                found += [line[None, k : k + 128] for k in range(0, size, 128)]
        row = lax.broadcasted_iota(jnp.int32, (VEC_ROWS, 128), 0)
        block = jnp.zeros((VEC_ROWS, 128), F32)
        for k, line in enumerate(found):
            block = jnp.where(row == k, line, block)
        out[0, at:, :] = block.astype(BF16)

    return pl.pallas_call(
        kernel,
        out_shape=jax.ShapeDtypeStruct((1, rows, 128), BF16),
        in_specs=[pl.BlockSpec(memory_space=pltpu.SMEM)]
        + [pl.BlockSpec(memory_space=pltpu.VMEM)] * (len(weights) + len(vectors))
        + [pl.BlockSpec(memory_space=pl.ANY)] * len(extra),
        out_specs=pl.BlockSpec(memory_space=pltpu.VMEM),
    )(place(), *weights, *vectors, *extra)


def gather_plain(weights, vectors):
    wide = [lax.all_gather(w, "batch", axis=1, tiled=True) for w in weights]
    wide = [lax.all_gather(w, "seq", axis=0, tiled=True) for w in wide]
    return wide, [lax.all_gather(v, "seq", axis=0, tiled=True).astype(F32) for v in vectors]


def own_parts(lanes, sizes):
    outs = []
    row = 0
    for size in sizes:
        if size < 128:
            part = lax.axis_index("seq") % (128 // size)
            outs.append(lax.dynamic_slice(lanes[row], (part * size,), (size,)))
            row += 1
        else:
            outs.append(lanes[row : row + size // 128].reshape(-1))
            row += size // 128
    return outs


def reduce_plain(weights, grads, vectors):
    outs = [
        lax.psum_scatter(g.astype(BF16), "batch", scatter_dimension=1, tiled=True).astype(F32)
        for g in grads
    ]
    outs = outs + list(lax.psum(tuple(vectors), "batch"))
    return [lax.psum_scatter(o, "seq", scatter_dimension=0, tiled=True) for o in outs]


def dot(left, right, a=1, b=0):
    return lax.dot_general(left, right, (((a,), (b,)), ((), ())), preferred_element_type=F32)


def norm_parts(values):
    centred = values - jnp.mean(values, -1, keepdims=True)
    scale = lax.rsqrt(jnp.mean(centred * centred, -1, keepdims=True) + 1e-05)
    return centred * scale, scale


def norm_back(grad, unit, scale, gain):
    inner = grad * gain
    pull = jnp.mean(inner, -1, keepdims=True)
    twist = jnp.mean(inner * unit, -1, keepdims=True)
    return scale * (inner - pull - unit * twist)


def gelu_pair(values):
    bell = jnp.exp(-0.5 * values * values)
    t = 1.0 / (1.0 + (0.3275911 * 0.5**0.5) * jnp.abs(values))
    poly = 1.061405429 * 0.5
    for factor in (-1.453152027, 1.421413741, -0.284496736, 0.254829592):
        poly = poly * t + factor * 0.5
    below = poly * t * bell
    share = jnp.where(values < 0, below, 1.0 - below)
    return values * share, share + values * bell * 0.3989422804014327


def full(shape):
    return pl.BlockSpec(shape, lambda i: (0,) * len(shape))


def each(shape):
    return pl.BlockSpec((1,) + tuple(shape[1:]), lambda i: (i,) + (0,) * (len(shape) - 1))


NARROW = 8


def project(inputs, shards, slices, pieces, wide, lines, tiles):
    count, rows, width = inputs.shape
    half = rows // 2
    hidden = slices[5].shape[0] * lax.axis_size("seq")
    segments = columns(shards) + [("vec", VEC_ROWS)]
    targets = spots(shards)
    order = (0, 1, 2, 3, 4, 6)
    arrays = [piece for piece, _, _ in pieces] if tiles else list(wide) + list(lines)

    def kernel(spot, x_ref, *refs):
        ins = refs[: len(arrays)]
        out_ref, pooled_ref, q_ref, k_ref, v_ref, narrow_ref, wide_ref = refs[len(arrays) :]

        @pl.when(pl.program_id(0) == 0)
        def _():
            if tiles:
                narrow_ref[...] = jnp.zeros_like(narrow_ref)
                wide_ref[...] = jnp.zeros_like(wide_ref)

                def vec(block, s):
                    block = block.astype(F32)
                    row = 0
                    for k, member in enumerate(slices):
                        size = member.shape[0]
                        start = s * size
                        for at in range(0, size, 128):
                            left = pl.multiple_of((start + at) // 128 * 128, 128)
                            line = block[row : row + 1]
                            if k == 5:
                                wide_ref[0:1, pl.ds(left, 128)] += line
                            else:
                                to = order.index(k)
                                narrow_ref[to : to + 1, pl.ds(left, 128)] += line
                            row += 1

                assemble(spot, ins, pieces, segments, targets, (q_ref, k_ref, v_ref), vec)
            else:
                for ref, source in zip((q_ref, k_ref, v_ref, narrow_ref, wide_ref), ins):
                    ref[...] = source[...]

        unit, _ = norm_parts(x_ref[0].astype(F32))
        normed = (unit * narrow_ref[0:1, :] + narrow_ref[1:2, :]).astype(BF16)
        out_ref[0, :, :width] = dot(normed, q_ref[...]).astype(BF16)
        for k, ref in enumerate((k_ref, v_ref)):
            product = dot(normed, ref[...])
            out_ref[0, :, (k + 1) * width : (k + 2) * width] = product.astype(BF16)
            for j in range(2):
                mean = jnp.sum(product[j * half : (j + 1) * half], 0, keepdims=True) / half
                pooled_ref[0, j : j + 1, k * width : (k + 1) * width] = mean.astype(BF16)

    shapes = [(count, rows, 3 * width), (count, 2, 2 * width)]
    square = (width, width)
    return pl.pallas_call(
        kernel,
        grid=(count,),
        in_specs=[pl.BlockSpec(memory_space=pltpu.SMEM), each(inputs.shape)]
        + [pl.BlockSpec(memory_space=pltpu.VMEM)] * len(arrays),
        out_specs=[each(shape) for shape in shapes]
        + [full(square)] * 3
        + [full((NARROW, width)), full((1, hidden))],
        out_shape=[jax.ShapeDtypeStruct(shape, BF16) for shape in shapes + [square] * 3]
        + [jax.ShapeDtypeStruct((NARROW, width), F32), jax.ShapeDtypeStruct((1, hidden), F32)],
    )(place(), inputs, *arrays)


def head_mask(rows, lane_half):
    lane = lax.broadcasted_iota(jnp.int32, (rows, 2 * HEAD), 1)
    return (lane < HEAD) if lane_half == 0 else (lane >= HEAD)


def only(array, lane_half):
    return jnp.where(head_mask(array.shape[0], lane_half), array, jnp.zeros_like(array))


def scores_of(keys, query, visible, rows):
    scores = dot(keys, query, 1, 1) * HEAD ** (-0.5)
    far = jnp.where(visible > 0, scores[rows:], -1e30)
    return jnp.concatenate([scores[:rows], far], 0)


def attend(qkv, summaries, visible):
    count, rows, width = qkv.shape[0], qkv.shape[1], qkv.shape[2] // 3
    far = summaries.shape[1]

    def kernel(qkv_ref, sum_ref, vis_ref, mixed_ref, lse_ref):
        seen = vis_ref[...]
        for pair in range(HEADS // 2):
            at = pair * 2 * HEAD
            query = qkv_ref[0, :, at : at + 2 * HEAD]
            keys = jnp.concatenate(
                [
                    qkv_ref[0, :, width + at : width + at + 2 * HEAD],
                    sum_ref[0, :, at : at + 2 * HEAD],
                ],
                0,
            )
            values = jnp.concatenate(
                [
                    qkv_ref[0, :, 2 * width + at : 2 * width + at + 2 * HEAD],
                    sum_ref[0, :, width + at : width + at + 2 * HEAD],
                ],
                0,
            )
            total = None
            for side in range(2):
                scores = scores_of(keys, only(query, side), seen, rows)
                top = jnp.max(scores, 0, keepdims=True)
                powers = jnp.exp(scores - top)
                mass = jnp.sum(powers, 0, keepdims=True)
                head = 2 * pair + side
                lse_ref[0, head : head + 1, :] = top + jnp.log(mass)
                probs = (powers * (1.0 / mass)).astype(BF16)
                part = dot(only(values, side), probs, 0, 0)
                total = part if total is None else total + part
            mixed_ref[0, :, at : at + 2 * HEAD] = total.T.astype(BF16)

    block = (count, rows, width)
    return pl.pallas_call(
        kernel,
        grid=(count,),
        in_specs=[
            each(qkv.shape),
            each(summaries.shape),
            full((far, rows)),
        ],
        out_specs=[each(block), each((count, HEADS, rows))],
        out_shape=[
            jax.ShapeDtypeStruct(block, BF16),
            jax.ShapeDtypeStruct((count, HEADS, rows), F32),
        ],
    )(qkv, summaries, visible)


def split_rows(total):
    high = total.astype(BF16).astype(F32)
    return high, total - high


def vector_block(narrow, wide, per):
    def block(s):
        left = pl.multiple_of(s * per // 128 * 128, 128)
        found = narrow[:, pl.ds(left, 128)]
        if wide is not None:
            step = wide.shape[1] // narrow.shape[1] * per
            for k in range(step // 128):
                chunk = wide[:, pl.ds(pl.multiple_of(s * step + k * 128, 128), 128)]
                row = lax.broadcasted_iota(jnp.int32, chunk.shape, 0)
                keep = (row % (VEC_ROWS // 2)) == 4 + k
                found = found + jnp.where(keep, chunk, 0.0)
        return found.astype(BF16)

    return block


def feed(inputs, cotangent, mixed, narrow, long_bias, pieces, wide, shards, tiles):
    count, rows, width = inputs.shape
    hidden_width = long_bias.shape[1]
    arrays = [piece for piece, _, _ in pieces] if tiles else list(wide)
    step = 512
    grads = [(width, width), (width, hidden_width), (hidden_width, width)]
    segments = columns(shards) + [("vec", VEC_ROWS)]
    targets = spots(shards)
    orders = pack_order() if tiles else None
    half = sum(size for _, size in segments) // 2
    per = width // lax.axis_size("seq")

    def kernel(spot, x_ref, cot_ref, mixed_ref, lines_ref, bu_ref, *rest):
        ins, rest = rest[: len(arrays)], rest[len(arrays) :]
        out_ref, mgrad_ref, xgrad_ref, narrow_ref, wide_ref, *rest = rest
        if tiles:
            packs, rest = rest[:4], rest[4:]
            go_ref, gu_ref, gd_ref, high_ref, long_ref, wo_ref, wu_ref, wd_ref = rest
        else:
            go_ref, gu_ref, gd_ref = rest
            wo_ref, wu_ref, wd_ref = ins
        step_id = pl.program_id(0)
        bias, gain, shift, last = (lines_ref[k : k + 1, :] for k in (4, 2, 3, 5))

        @pl.when(step_id == 0)
        def _():
            for ref in (go_ref, gu_ref, gd_ref, narrow_ref, wide_ref):
                ref[...] = jnp.zeros_like(ref)
            if tiles:
                weights = (wo_ref, wu_ref, wd_ref)
                assemble(spot, ins, pieces, segments[:-1], targets, weights, None)

        middle = x_ref[0].astype(F32) + (dot(mixed_ref[0], wo_ref[...]) + bias)
        cot = cot_ref[0]
        tangent = cot.astype(BF16)
        unit, scale = norm_parts(middle)
        normed = (unit * gain + shift).astype(BF16)
        flipped = normed.T
        final = middle + last
        back = None
        for at in range(0, hidden_width, step):
            here = slice(at, at + step)
            hidden = dot(normed, wu_ref[:, here]) + bu_ref[:, here]
            active, slope = gelu_pair(hidden)
            active = active.astype(BF16)
            final = final + dot(active, wd_ref[here, :])
            gd_ref[here, :] += dot(active, tangent, 0, 0)
            grad = (dot(tangent, wd_ref[here, :], 1, 1) * slope).astype(BF16)
            gu_ref[:, here] += dot(flipped, grad)
            wide_ref[0:1, here] += jnp.sum(grad.astype(F32), 0, keepdims=True)
            part = dot(grad, wu_ref[:, here], 1, 1)
            back = part if back is None else back + part
        out_ref[0] = final.astype(BF16)
        narrow_ref[0:1, :] += jnp.sum(back * unit, 0, keepdims=True)
        narrow_ref[1:2, :] += jnp.sum(back, 0, keepdims=True)
        middle_grad = cot + norm_back(back, unit, scale, gain)
        mgrad_ref[0] = middle_grad
        branch = middle_grad.astype(BF16)
        narrow_ref[2:3, :] += jnp.sum(branch.astype(F32), 0, keepdims=True)
        narrow_ref[3:4, :] += jnp.sum(tangent.astype(F32), 0, keepdims=True)
        go_ref[...] += dot(mixed_ref[0], branch, 0, 0)
        xgrad_ref[0] = dot(branch, wo_ref[...], 1, 1).astype(BF16)

        if tiles:

            @pl.when(step_id == count - 1)
            def _():
                for ref, source, k in ((high_ref, narrow_ref, 8), (long_ref, wide_ref, 1)):
                    high, low = split_rows(source[...])
                    zero = jnp.zeros((8, source.shape[1]), F32)
                    if k == 1:
                        high = jnp.broadcast_to(high[0:1], zero.shape)
                        low = jnp.broadcast_to(low[0:1], zero.shape)
                    ref[...] = jnp.concatenate([high, zero, low, zero], 0)
                write_packed(
                    spot,
                    (go_ref, gu_ref, gd_ref),
                    vector_block(high_ref, long_ref, per),
                    packs,
                    segments,
                    targets,
                    orders,
                )

    block = inputs.shape
    out_shape = [
        jax.ShapeDtypeStruct(block, BF16),
        jax.ShapeDtypeStruct(block, F32),
        jax.ShapeDtypeStruct(block, BF16),
        jax.ShapeDtypeStruct((8, width), F32),
        jax.ShapeDtypeStruct((8, hidden_width), F32),
    ]
    out_specs = [each(block)] * 3 + [full((8, width)), full((8, hidden_width))]
    scratch = []
    if tiles:
        packed_shapes = [(len(names) // 2, half, 128) for names in orders for _ in range(2)]
        out_shape += [jax.ShapeDtypeStruct(shape, BF16) for shape in packed_shapes]
        out_specs += [pl.BlockSpec(memory_space=pltpu.VMEM)] * 4
        scratch = [pltpu.VMEM(shape, F32) for shape in grads]
        scratch += [pltpu.VMEM((VEC_ROWS, width), F32), pltpu.VMEM((VEC_ROWS, hidden_width), F32)]
        scratch += [pltpu.VMEM(shape, BF16) for shape in grads]
    else:
        out_shape += [jax.ShapeDtypeStruct(shape, F32) for shape in grads]
        out_specs += [full(shape) for shape in grads]
    return pl.pallas_call(
        kernel,
        grid=(count,),
        in_specs=[pl.BlockSpec(memory_space=pltpu.SMEM)]
        + [each(block)] * 3
        + [full(narrow.shape), full(long_bias.shape)]
        + [pl.BlockSpec(memory_space=pltpu.VMEM)] * len(arrays),
        out_specs=out_specs,
        out_shape=out_shape,
        scratch_shapes=scratch,
    )(place(), inputs, cotangent, mixed, narrow, long_bias, *arrays)


def attend_back(qkv, summaries, visible, lse, mixed_grad, first, number, before=(), after=()):
    count, rows, width = mixed_grad.shape
    far = summaries.shape[1]
    extra = list(before) + list(after)

    def each(shape):
        return pl.BlockSpec(
            (1,) + tuple(shape[1:]), lambda i: (i + first,) + (0,) * (len(shape) - 1)
        )

    def kernel(qkv_ref, sum_ref, vis_ref, lse_ref, grad_ref, *rest):
        dq_ref, dk_ref, dv_ref, far_ref = rest[len(extra) :]
        seen = vis_ref[...]
        for pair in range(HEADS // 2):
            at = pair * 2 * HEAD
            lanes = slice(at, at + 2 * HEAD)
            query = qkv_ref[0, :, lanes]
            pull = grad_ref[0, :, lanes]
            keys = jnp.concatenate(
                [qkv_ref[0, :, width + at : width + at + 2 * HEAD], sum_ref[0, :, lanes]], 0
            )
            values = jnp.concatenate(
                [
                    qkv_ref[0, :, 2 * width + at : 2 * width + at + 2 * HEAD],
                    sum_ref[0, :, width + at : width + at + 2 * HEAD],
                ],
                0,
            )
            d_query = d_keys = d_values = 0.0
            for side in range(2):
                head = 2 * pair + side
                own = only(query, side)
                own_pull = only(pull, side)
                scores = scores_of(keys, own, seen, rows)
                probs = jnp.exp(scores - lse_ref[0, head : head + 1, :])
                dots = dot(values, own_pull, 1, 1)
                centre = jnp.sum(probs * dots, 0, keepdims=True)
                slope = (probs * (dots - centre)).astype(BF16)
                d_values = d_values + dot(probs.astype(BF16), own_pull)
                d_keys = d_keys + dot(slope, own)
                d_query = d_query + dot(only(keys, side), slope, 0, 0)
            d_keys = d_keys * HEAD ** (-0.5)
            dq_ref[0, :, lanes] = (d_query * HEAD ** (-0.5)).T.astype(BF16)
            dk_ref[0, :, lanes] = d_keys[:rows]
            dv_ref[0, :, lanes] = d_values[:rows]
            far_ref[0, :, lanes] = d_keys[rows:].astype(BF16)
            far_ref[0, :, width + at : width + at + 2 * HEAD] = d_values[rows:].astype(BF16)

    block = mixed_grad.shape
    return pl.pallas_call(
        kernel,
        grid=(number,),
        in_specs=[
            each(qkv.shape),
            each(summaries.shape),
            full((far, rows)),
            each(lse.shape),
            each(block),
        ]
        + [pl.BlockSpec(memory_space=pl.ANY)] * len(extra),
        out_specs=[each(block)] * 3 + [each(summaries.shape)],
        out_shape=[
            jax.ShapeDtypeStruct(block, BF16),
            jax.ShapeDtypeStruct(block, F32),
            jax.ShapeDtypeStruct(block, F32),
            jax.ShapeDtypeStruct(summaries.shape, BF16),
        ],
        input_output_aliases={5 + k: k for k in range(len(before))},
    )(qkv, summaries, visible, lse, mixed_grad, *extra)


def project_back(
    inputs, d_query, d_keys, d_values, owned, weights, narrow, middle_grad, shards, tiles, after
):
    count, rows, width = inputs.shape
    half_span = rows // 2
    segments = columns(shards) + [("vec", VEC_ROWS)]
    targets = spots(shards)
    orders = pack_order() if tiles else None
    half = sum(size for _, size in segments) // 2
    per = width // lax.axis_size("seq")

    def kernel(spot, x_ref, dq_ref, dk_ref, dv_ref, own_ref, wq_ref, wk_ref, wv_ref,
               lines_ref, mgrad_ref, *rest):
        igrad_ref, narrow_ref, *rest = rest[len(after) :]
        gain, shift = lines_ref[0:1, :], lines_ref[1:2, :]
        if tiles:
            packs, (gq_ref, gk_ref, gv_ref, high_ref) = rest[:4], rest[4:]
        else:
            gq_ref, gk_ref, gv_ref = rest
        step_id = pl.program_id(0)

        @pl.when(step_id == 0)
        def _():
            for ref in (gq_ref, gk_ref, gv_ref, narrow_ref):
                ref[...] = jnp.zeros_like(ref)

        unit, scale = norm_parts(x_ref[0].astype(F32))
        flipped = (unit * gain + shift).astype(BF16).T
        back = dot(dq_ref[0], wq_ref[...], 1, 1)
        gq_ref[...] += dot(flipped, dq_ref[0])
        for k, (direct, w_ref, g_ref) in enumerate(
            ((dk_ref, wk_ref, gk_ref), (dv_ref, wv_ref, gv_ref))
        ):
            act = jnp.concatenate(
                [
                    direct[0, j * half_span : (j + 1) * half_span, :]
                    + own_ref[0, j : j + 1, k * width : (k + 1) * width] / half_span
                    for j in range(2)
                ],
                0,
            ).astype(BF16)
            g_ref[...] += dot(flipped, act)
            back = back + dot(act, w_ref[...], 1, 1)
        narrow_ref[0:1, :] += jnp.sum(back * unit, 0, keepdims=True)
        narrow_ref[1:2, :] += jnp.sum(back, 0, keepdims=True)
        igrad_ref[0] = mgrad_ref[0] + norm_back(back, unit, scale, gain)

        if tiles:

            @pl.when(step_id == count - 1)
            def _():
                high, low = split_rows(narrow_ref[...])
                zero = jnp.zeros_like(high)
                high_ref[...] = jnp.concatenate([high, zero, low, zero], 0)
                write_packed(
                    spot,
                    (gq_ref, gk_ref, gv_ref),
                    vector_block(high_ref, None, per),
                    packs,
                    segments,
                    targets,
                    orders,
                )

    block = inputs.shape
    square = (width, width)
    out_shape = [jax.ShapeDtypeStruct(block, F32), jax.ShapeDtypeStruct((8, width), F32)]
    out_specs = [each(block), full((8, width))]
    scratch = []
    if tiles:
        packed_shapes = [(len(names) // 2, half, 128) for names in orders for _ in range(2)]
        out_shape += [jax.ShapeDtypeStruct(shape, BF16) for shape in packed_shapes]
        out_specs += [pl.BlockSpec(memory_space=pltpu.VMEM)] * 4
        scratch = [pltpu.VMEM(square, F32)] * 3 + [pltpu.VMEM((VEC_ROWS, width), F32)]
    else:
        out_shape += [jax.ShapeDtypeStruct(square, F32)] * 3
        out_specs += [full(square)] * 3
    return pl.pallas_call(
        kernel,
        grid=(count,),
        in_specs=[pl.BlockSpec(memory_space=pltpu.SMEM)]
        + [each(block)] * 4
        + [each(owned.shape)]
        + [full(square)] * 3
        + [full(narrow.shape), each(block)]
        + [pl.BlockSpec(memory_space=pl.ANY)] * len(after),
        out_specs=out_specs,
        out_shape=out_shape,
        scratch_shapes=scratch,
    )(place(), inputs, d_query, d_keys, d_values, owned, *weights, narrow, middle_grad, *after)


def local(
    inputs,
    cotangent,
    query_weight,
    key_weight,
    value_weight,
    out_weight,
    up_weight,
    down_weight,
    norm1_gain,
    norm1_bias,
    norm2_gain,
    norm2_bias,
    out_bias,
    up_bias,
    down_bias,
):
    shards = [query_weight, key_weight, value_weight, out_weight, up_weight, down_weight]
    slices = [norm1_gain, norm1_bias, norm2_gain, norm2_bias, out_bias, up_bias, down_bias]
    tiles = whole_tiles(shards, slices)
    count, rows, width = inputs.shape
    wide, lines, early, late = [None] * 6, (), (), ()
    if tiles:
        state = gather_outer(pack_shards(shards[:3], slices))
        other = gather_outer(pack_shards(shards[3:], [], state))
        early = gather_inner(state)
        late = gather_inner(other)
    else:
        wide, members = gather_plain(shards, slices)
        blank = jnp.zeros((NARROW - 6, width), F32)
        lines = (
            jnp.concatenate([jnp.stack([members[k] for k in (0, 1, 2, 3, 4, 6)]), blank]),
            members[5][None],
        )
    qkv, pooled, w_query, w_key, w_value, narrow, long_bias = project(
        inputs, shards[:3], slices, early, wide[:3], lines, tiles
    )
    summaries = jnp.transpose(gather_seq(pooled), (1, 0, 2, 3)).reshape(count, -1, 2 * width)
    here = lax.axis_index("seq")
    marks = jnp.array([s for s, _ in relative_ids(seq_stages())], jnp.int32)
    visible = jnp.repeat((marks ^ here) < here, 2).astype(F32)
    visible = jnp.broadcast_to(visible[:, None], (visible.shape[0], rows))
    mixed, lse = attend(qkv, summaries, visible)
    outputs, middle_grad, mixed_grad, narrow_two, wide_two, *second = feed(
        inputs, cotangent, mixed, narrow, long_bias, late, wide[3:], shards[3:], tiles
    )
    ties = []
    if tiles:
        second = reduce_step([tuple(second[:2]), tuple(second[2:])], 0)
        ties = [member for couple in second for member in couple]
    begun = attend_back(qkv, summaries, visible, lse, mixed_grad, 0, count // 2)
    d_query, d_keys, d_values, terms = attend_back(
        qkv, summaries, visible, lse, mixed_grad, count // 2, count - count // 2, begun, ties
    )
    if tiles:
        second = reduce_step(second, 1)
        ties = [member for couple in second for member in couple]
    terms = jnp.transpose(terms.reshape(count, -1, 2, 2 * width), (1, 0, 2, 3))
    owned = reduce_seq(terms)
    input_grad, narrow_one, *first = project_back(
        inputs,
        d_query,
        d_keys,
        d_values,
        owned,
        (w_query, w_key, w_value),
        narrow,
        middle_grad,
        shards[:3],
        tiles,
        ties,
    )
    if tiles:
        second = reduce_step(second, 2, True)
        first = reduce_step([tuple(first[:2]), tuple(first[2:])], 0)
        first = reduce_step(reduce_step(first, 1), 2, True)
        *matrices, lines_two, lines_one = reduce_end([((3, 4, 5), second), ((0, 1, 2), first)], shards)
        size = norm1_gain.shape[0]
        tail = own_parts(lines_two, [size] * 4 + [up_bias.shape[0]])
        front = own_parts(lines_one, [size] * 2)
        vectors = front + tail[:3] + [tail[4], tail[3]]
    else:
        vectors = [
            narrow_one[0],
            narrow_one[1],
            narrow_two[0],
            narrow_two[1],
            narrow_two[2],
            wide_two[0],
            narrow_two[3],
        ]
        reduced = reduce_plain(shards, list(first) + list(second), vectors)
        matrices, vectors = reduced[:6], reduced[6:]
    return (outputs, input_grad, *matrices, *vectors)


def solution(mesh):
    placed = (
        P("batch", "seq", None),
        P("batch", "seq", None),
        P("seq", "batch"),
        P("seq", "batch"),
        P("seq", "batch"),
        P("seq", "batch"),
        P("seq", "batch"),
        P("seq", "batch"),
        P("seq"),
        P("seq"),
        P("seq"),
        P("seq"),
        P("seq"),
        P("seq"),
        P("seq"),
    )
    return jax.shard_map(
        local,
        mesh=mesh,
        in_specs=placed,
        out_specs=(
            P("batch", "seq", None),
            P("batch", "seq", None),
            P("seq", "batch"),
            P("seq", "batch"),
            P("seq", "batch"),
            P("seq", "batch"),
            P("seq", "batch"),
            P("seq", "batch"),
            P("seq"),
            P("seq"),
            P("seq"),
            P("seq"),
            P("seq"),
            P("seq"),
            P("seq"),
        ),
        check_vma=False,
    )
```

```python
import jax
import jax.numpy as jnp
from jax import lax
from jax.experimental import pallas as pl
from jax.experimental.pallas import tpu as pltpu
from jax.sharding import PartitionSpec as P


HEADS = 8
HEAD = 64
VEC_ROWS = 32
F32 = jnp.float32
BF16 = jnp.bfloat16


def swap(array, axis, bit):
    count = lax.axis_size(axis)
    return lax.ppermute(array, axis, [(i, i ^ bit) for i in range(count)])


def bits_down(count):
    return [1 << k for k in range(count.bit_length() - 2, -1, -1)]


def outer_stages():
    seq = [("seq", bit) for bit in bits_down(lax.axis_size("seq")) if bit > 1]
    batch = [("batch", bit) for bit in bits_down(lax.axis_size("batch")) if bit > 2]
    return batch + seq


def relative_ids(stages):
    ids = [(0, 0)]
    for axis, bit in stages:
        moved = [(s ^ bit, b) if axis == "seq" else (s, b ^ bit) for s, b in ids]
        ids = ids + moved
    return ids


X_STAGE = ("batch", 2)
Y_STAGE = ("seq", 1)
CORE = ("batch", 1)


def gather_outer(state):
    for stage in outer_stages():
        state = jnp.concatenate([state, swap(state, *stage)], 0)
    return state


def gather_inner(state):
    half = state.shape[1] // 2
    outer = outer_stages()
    pieces = []
    for first, order in ((0, (X_STAGE, Y_STAGE)), (half, (Y_STAGE, X_STAGE))):
        part = state[:, first : first + half]
        part = jnp.concatenate([part, swap(part, *order[0])], 0)
        far = swap(part, *order[1])
        ids = relative_ids(outer + [order[0]])
        full = relative_ids(outer + list(order))
        far_ids = full[len(ids) :]
        for piece, names in ((part, ids), (far, far_ids)):
            pieces.append((piece, names, first))
            pieces.append((swap(piece, *CORE), [(s, b ^ 1) for s, b in names], first))
    return pieces


def place():
    return jnp.stack([lax.axis_index("seq"), lax.axis_index("batch")]).astype(jnp.int32)


def cuts(segments, first, half):
    found = []
    at = 0
    for name, rows in segments:
        low, high = max(at, first), min(at + rows, first + half)
        if low < high:
            found.append((name, low - at, low - first, high - low))
        at += rows
    return found


def assemble(spot, refs, pieces, segments, targets, outs, vec):
    for ref, (piece, names, first) in zip(refs, pieces):
        for p, (sr, br) in enumerate(names):
            s, b = spot[0] ^ sr, spot[1] ^ br
            for name, row, here, size in cuts(segments, first, piece.shape[1]):
                if name == "vec":
                    if br == 0:
                        vec(ref[p, here : here + size, :], s)
                else:
                    number, top, left = targets(name, row, s, b)
                    outs[number][
                        pl.ds(pl.multiple_of(top, 16), size), pl.ds(pl.multiple_of(left, 128), 128)
                    ] = ref[p, here : here + size, :]


def pack_order():
    outer = outer_stages()
    return [
        relative_ids(outer + [Y_STAGE, X_STAGE, CORE]),
        relative_ids(outer + [X_STAGE, Y_STAGE, CORE]),
    ]


def write_packed(spot, ins, vec_block, outs, segments, targets, orders):
    half = sum(size for _, size in segments) // 2
    for k, (names, first) in enumerate(zip(orders, (0, half))):
        for p, (sr, br) in enumerate(names):
            s, b = spot[0] ^ sr, spot[1] ^ br
            out = outs[2 * k + p // (len(names) // 2)]
            p = p % (len(names) // 2)
            for name, row, here, size in cuts(segments, first, half):
                if name == "vec":
                    out[p, here : here + size, :] = vec_block(s)
                else:
                    number, top, left = targets(name, row, s, b)
                    out[p, here : here + size, :] = ins[number][
                        pl.ds(pl.multiple_of(top, 16), size), pl.ds(pl.multiple_of(left, 128), 128)
                    ].astype(BF16)


def add_low(mine, theirs):
    return (mine.astype(F32) + theirs.astype(F32)).astype(BF16)


def join_pair(array):
    count = VEC_ROWS // 2
    return array[..., -VEC_ROWS:-count, :].astype(F32) + array[..., -count:, :].astype(F32)


def split_pair(total):
    high = lax.reduce_precision(total, 8, 7)
    return [high.astype(BF16), (total - high).astype(BF16)]


def add_pairs(mine, theirs):
    total = join_pair(mine) + join_pair(theirs)
    low = add_low(mine[..., :-VEC_ROWS, :], theirs[..., :-VEC_ROWS, :])
    return jnp.concatenate([low] + split_pair(total), -2)


ORDERS = ((CORE, X_STAGE, Y_STAGE), (CORE, Y_STAGE, X_STAGE))


def reduce_step(halves, step, last=False):
    done = []
    for k, (kept, sent) in enumerate(halves):
        theirs = swap(sent, *ORDERS[k][step])
        if last:
            done.append((kept, theirs))
            continue
        state = (add_pairs if k == 1 else add_low)(kept, theirs)
        count = state.shape[0] // 2
        done.append((state[:count], state[count:]))
    return done


def sum_rows(mine, theirs, spans):
    total = mine.astype(F32) + theirs.astype(F32)
    count = VEC_ROWS // 2
    return total, [total[at : at + count] + total[at + count : at + VEC_ROWS] for at in spans]


def joined_sum(couples):
    count = couples[0][0].shape[0]
    rows = sum(kept.shape[1] for kept, _, _ in couples)

    def kernel(*refs):
        ins, outs = refs[:-2], refs[-2:]
        for p in range(count):
            out = outs[p // (count // 2)]
            at = 0
            for k, (kept, _, vectors) in enumerate(couples):
                size = kept.shape[1]
                total, pairs = sum_rows(
                    ins[2 * k][p], ins[2 * k + 1][p], [size - VEC_ROWS] if vectors else []
                )
                out[p % (count // 2), at : at + size, :] = total.astype(BF16)
                for pair in pairs:
                    high = pair.astype(BF16)
                    low = (pair - high.astype(F32)).astype(BF16)
                    end = at + size
                    out[p % (count // 2), end - VEC_ROWS : end - VEC_ROWS // 2, :] = high
                    out[p % (count // 2), end - VEC_ROWS // 2 : end, :] = low
                at += size

    arrays = [array for kept, theirs, _ in couples for array in (kept, theirs)]
    return pl.pallas_call(
        kernel,
        cost_estimate=cost(2),
        out_shape=[jax.ShapeDtypeStruct((count // 2, rows, 128), BF16)] * 2,
        in_specs=[pl.BlockSpec(memory_space=pltpu.VMEM)] * len(arrays),
        out_specs=[pl.BlockSpec(memory_space=pltpu.VMEM)] * 2,
    )(*arrays)


def again(kept, theirs, spans):
    count, rows = kept.shape[:2]

    def kernel(mine_ref, theirs_ref, *outs):
        for p in range(count):
            out = outs[p // (count // 2)]
            q = p % (count // 2)
            total, pairs = sum_rows(mine_ref[p], theirs_ref[p], spans)
            out[q] = total.astype(BF16)
            for pair, at in zip(pairs, spans):
                high = pair.astype(BF16)
                out[q, at : at + VEC_ROWS // 2, :] = high
                low = (pair - high.astype(F32)).astype(BF16)
                out[q, at + VEC_ROWS // 2 : at + VEC_ROWS, :] = low

    return pl.pallas_call(
        kernel,
        cost_estimate=cost(2),
        out_shape=[jax.ShapeDtypeStruct((count // 2, rows, 128), BF16)] * 2,
        in_specs=[pl.BlockSpec(memory_space=pltpu.VMEM)] * 2,
        out_specs=[pl.BlockSpec(memory_space=pltpu.VMEM)] * 2,
    )(kept, theirs)


def finish(kept, theirs, parts, spans, shapes, sizes):
    def kernel(spot, mine_ref, theirs_ref, *outs):
        total, pairs = sum_rows(mine_ref[0], theirs_ref[0], spans)
        for number, row, left, at, size in parts:
            outs[number][row : row + size, left : left + 128] = total[at : at + size]
        (pair,) = pairs
        row = 0
        for out, size in zip(outs[len(shapes) :], sizes):
            if size < 128:
                line = pair[row : row + 1]
                found = line[:, :size]
                for k in range(1, 128 // size):
                    part = line[:, k * size : (k + 1) * size]
                    found = jnp.where(spot[0] % (128 // size) == k, part, found)
                out[...] = found.reshape(size)
                row += 1
            else:
                for at in range(0, size, 128):
                    out[at : at + 128] = pair[row : row + 1].reshape(128)
                    row += 1

    return pl.pallas_call(
        kernel,
        cost_estimate=cost(2),
        out_shape=[jax.ShapeDtypeStruct(shape, F32) for shape in shapes]
        + [jax.ShapeDtypeStruct((size,), F32) for size in sizes],
        in_specs=[pl.BlockSpec(memory_space=pltpu.SMEM)]
        + [pl.BlockSpec(memory_space=pltpu.VMEM)] * 2,
        out_specs=[pl.BlockSpec(memory_space=pltpu.VMEM)] * (len(shapes) + len(sizes)),
    )(place(), kept, theirs)


def reduce_end(halves, weights, sizes):
    segments = columns(weights) + [("vec", VEC_ROWS)]
    parts = []
    spans = []
    at = 0
    for k, (kept, _) in enumerate(halves):
        half = kept.shape[1]
        for name, row, here, size in cuts(segments, k * half, half):
            if name == "vec":
                spans.append(at + here)
            else:
                parts.append((name[0], row, name[1] * 128, at + here, size))
        at += half
    kept, sent = joined_sum([(kept, theirs, k == 1) for k, (kept, theirs) in enumerate(halves)])
    stages = outer_stages()[::-1]
    for k, stage in enumerate(stages):
        theirs = swap(sent, *stage)
        if k < len(stages) - 1:
            kept, sent = again(kept, theirs, spans)
    return list(finish(kept, theirs, parts, spans, [w.shape for w in weights], sizes))


def seq_stages():
    return [("seq", bit) for bit in bits_down(lax.axis_size("seq"))]


def gather_seq(array):
    state = array[None]
    for stage in seq_stages():
        state = jnp.concatenate([state, swap(state, *stage)], 0)
    return state


def reduce_seq(state):
    for stage in seq_stages()[::-1]:
        count = state.shape[0] // 2
        theirs = swap(state[count:], *stage)
        total = state[:count].astype(F32) + theirs.astype(F32)
        state = total if count == 1 else total.astype(BF16)
    return state[0]


def whole_tiles(weights, vectors):
    return (
        all(w.shape[0] % 16 == 0 and w.shape[1] % 128 == 0 for w in weights)
        and all(128 % v.shape[0] == 0 or v.shape[0] % 128 == 0 for v in vectors)
        and sum(v.shape[0] for v in vectors) % 128 == 0
    )


def columns(weights):
    return [
        ((i, c), weight.shape[0])
        for i, weight in enumerate(weights)
        for c in range(weight.shape[1] // 128)
    ]


def spots(weights):
    def targets(name, row, s, b):
        if name == "vec":
            return (len(weights), s * VEC_ROWS + row, 0)
        i, c = name
        rows, width = weights[i].shape
        return (i, s * rows + row, b * width + c * 128)

    return targets


def pack_shards(weights, vectors, after=None):
    segments = columns(weights) + ([("vec", VEC_ROWS)] if vectors else [])
    rows = sum(size for _, size in segments)
    extra = [] if after is None else [after]

    def kernel(spot, *refs):
        out = refs[-1]
        at = 0
        for ref, weight in zip(refs, weights):
            for left in range(0, weight.shape[1], 128):
                out[0, at : at + weight.shape[0], :] = ref[:, left : left + 128]
                at += weight.shape[0]
        if not vectors:
            return
        found = []
        for ref in refs[len(weights) : len(weights) + len(vectors)]:
            size = ref.shape[0]
            line = ref[...].astype(F32)
            if size < 128:
                line = jnp.concatenate([line[None]] * (128 // size), 1)
                lane = lax.broadcasted_iota(jnp.int32, line.shape, 1)
                found.append(jnp.where(lane // size == spot[0] % (128 // size), line, 0.0))
            else:
                found += [line[None, k : k + 128] for k in range(0, size, 128)]
        row = lax.broadcasted_iota(jnp.int32, (VEC_ROWS, 128), 0)
        block = jnp.zeros((VEC_ROWS, 128), F32)
        for k, line in enumerate(found):
            block = jnp.where(row == k, line, block)
        out[0, at:, :] = block.astype(BF16)

    return pl.pallas_call(
        kernel,
        out_shape=jax.ShapeDtypeStruct((1, rows, 128), BF16),
        in_specs=[pl.BlockSpec(memory_space=pltpu.SMEM)]
        + [pl.BlockSpec(memory_space=pltpu.VMEM)] * (len(weights) + len(vectors))
        + [pl.BlockSpec(memory_space=pl.ANY)] * len(extra),
        out_specs=pl.BlockSpec(memory_space=pltpu.VMEM),
    )(place(), *weights, *vectors, *extra)


def gather_plain(weights, vectors):
    wide = [lax.all_gather(w, "batch", axis=1, tiled=True) for w in weights]
    wide = [lax.all_gather(w, "seq", axis=0, tiled=True) for w in wide]
    return wide, [lax.all_gather(v, "seq", axis=0, tiled=True).astype(F32) for v in vectors]


def reduce_plain(grads, vectors):
    outs = [
        lax.psum_scatter(g.astype(BF16), "batch", scatter_dimension=1, tiled=True).astype(F32)
        for g in grads
    ]
    outs = outs + list(lax.psum(tuple(vectors), "batch"))
    return [lax.psum_scatter(o, "seq", scatter_dimension=0, tiled=True) for o in outs]


def dot(left, right, a=1, b=0):
    return lax.dot_general(left, right, (((a,), (b,)), ((), ())), preferred_element_type=F32)


def norm_parts(values):
    centred = values - jnp.mean(values, -1, keepdims=True)
    scale = lax.rsqrt(jnp.mean(centred * centred, -1, keepdims=True) + 1e-05)
    return centred * scale, scale


def norm_back(grad, unit, scale, gain):
    inner = grad * gain
    pull = jnp.mean(inner, -1, keepdims=True)
    twist = jnp.mean(inner * unit, -1, keepdims=True)
    return scale * (inner - pull - unit * twist)


def gelu_pair(values):
    bell = jnp.exp(-0.5 * values * values)
    t = 1.0 / (1.0 + (0.3275911 * 0.5**0.5) * jnp.abs(values))
    poly = 1.061405429 * 0.5
    for factor in (-1.453152027, 1.421413741, -0.284496736, 0.254829592):
        poly = poly * t + factor * 0.5
    below = poly * t * bell
    share = jnp.where(values < 0, below, 1.0 - below)
    return values * share, share + values * bell * 0.3989422804014327


def full(shape):
    return pl.BlockSpec(shape, lambda i: (0,) * len(shape))


def each(shape):
    return pl.BlockSpec((1,) + tuple(shape[1:]), lambda i: (i,) + (0,) * (len(shape) - 1))


NARROW = 8


def cost(micros):
    return pl.CostEstimate(flops=int(micros * 1e9), transcendentals=0, bytes_accessed=1 << 20)


def spread(shape, first=0):
    return pl.BlockSpec((shape[0], 1) + tuple(shape[2:]), lambda i: (0, i + first, 0, 0))


def project(inputs, shards, slices, pieces, wide, lines, tiles):
    count, rows, width = inputs.shape
    half = rows // 2
    hidden = slices[5].shape[0] * lax.axis_size("seq")
    segments = columns(shards) + [("vec", VEC_ROWS)]
    targets = spots(shards)
    order = (0, 1, 2, 3, 4, 6)
    arrays = [piece for piece, _, _ in pieces] if tiles else list(wide) + list(lines)

    def kernel(spot, x_ref, *refs):
        ins = refs[: len(arrays)]
        out_ref, pooled_ref, q_ref, k_ref, v_ref, narrow_ref, wide_ref = refs[len(arrays) :]

        @pl.when(pl.program_id(0) == 0)
        def _():
            if tiles:
                narrow_ref[...] = jnp.zeros_like(narrow_ref)
                wide_ref[...] = jnp.zeros_like(wide_ref)

                def vec(block, s):
                    block = block.astype(F32)
                    row = 0
                    for k, member in enumerate(slices):
                        size = member.shape[0]
                        start = s * size
                        for at in range(0, size, 128):
                            left = pl.multiple_of((start + at) // 128 * 128, 128)
                            line = block[row : row + 1]
                            if k == 5:
                                wide_ref[0:1, pl.ds(left, 128)] += line
                            else:
                                to = order.index(k)
                                narrow_ref[to : to + 1, pl.ds(left, 128)] += line
                            row += 1

                assemble(spot, ins, pieces, segments, targets, (q_ref, k_ref, v_ref), vec)
            else:
                for ref, source in zip((q_ref, k_ref, v_ref, narrow_ref, wide_ref), ins):
                    ref[...] = source[...]

        unit, _ = norm_parts(x_ref[0].astype(F32))
        normed = (unit * narrow_ref[0:1, :] + narrow_ref[1:2, :]).astype(BF16)
        out_ref[0, :, :width] = dot(normed, q_ref[...]).astype(BF16)
        for k, ref in enumerate((k_ref, v_ref)):
            product = dot(normed, ref[...])
            out_ref[0, :, (k + 1) * width : (k + 2) * width] = product.astype(BF16)
            for j in range(2):
                mean = jnp.sum(product[j * half : (j + 1) * half], 0, keepdims=True) / half
                pooled_ref[0, j : j + 1, k * width : (k + 1) * width] = mean.astype(BF16)

    shapes = [(count, rows, 3 * width), (count, 2, 2 * width)]
    square = (width, width)
    return pl.pallas_call(
        kernel,
        cost_estimate=cost(6),
        grid=(count,),
        in_specs=[pl.BlockSpec(memory_space=pltpu.SMEM), each(inputs.shape)]
        + [pl.BlockSpec(memory_space=pltpu.VMEM)] * len(arrays),
        out_specs=[each(shape) for shape in shapes]
        + [full(square)] * 3
        + [full((NARROW, width)), full((1, hidden))],
        out_shape=[jax.ShapeDtypeStruct(shape, BF16) for shape in shapes + [square] * 3]
        + [jax.ShapeDtypeStruct((NARROW, width), F32), jax.ShapeDtypeStruct((1, hidden), F32)],
    )(place(), inputs, *arrays)


def head_mask(rows, lane_half):
    lane = lax.broadcasted_iota(jnp.int32, (rows, 2 * HEAD), 1)
    return (lane < HEAD) if lane_half == 0 else (lane >= HEAD)


def only(array, lane_half):
    return jnp.where(head_mask(array.shape[0], lane_half), array, jnp.zeros_like(array))


def seen_rows(seq, far, rows):
    row = lax.broadcasted_iota(jnp.int32, (far, rows), 0) // 2
    seen = jnp.zeros((far, rows), F32)
    for p, (rel, _) in enumerate(relative_ids(seq_stages())):
        seen = jnp.where(row == p, jnp.where((seq ^ rel) < seq, 1.0, 0.0), seen)
    return seen


def scores_of(keys, query, visible, rows):
    scores = dot(keys, query, 1, 1) * HEAD ** (-0.5)
    far = jnp.where(visible > 0, scores[rows:], -1e30)
    return jnp.concatenate([scores[:rows], far], 0)


def attend(qkv, summaries):
    count, rows, width = qkv.shape[0], qkv.shape[1], qkv.shape[2] // 3
    far = 2 * summaries.shape[0]

    def kernel(spot, qkv_ref, sum_ref, mixed_ref, lse_ref):
        seen = seen_rows(spot[0], far, rows)
        spans = jnp.concatenate([sum_ref[p, 0] for p in range(far // 2)], 0)
        for pair in range(HEADS // 2):
            at = pair * 2 * HEAD
            query = qkv_ref[0, :, at : at + 2 * HEAD]
            keys = jnp.concatenate(
                [
                    qkv_ref[0, :, width + at : width + at + 2 * HEAD],
                    spans[:, at : at + 2 * HEAD],
                ],
                0,
            )
            values = jnp.concatenate(
                [
                    qkv_ref[0, :, 2 * width + at : 2 * width + at + 2 * HEAD],
                    spans[:, width + at : width + at + 2 * HEAD],
                ],
                0,
            )
            total = None
            for side in range(2):
                scores = scores_of(keys, only(query, side), seen, rows)
                top = jnp.max(scores, 0, keepdims=True)
                powers = jnp.exp(scores - top)
                mass = jnp.sum(powers, 0, keepdims=True)
                head = 2 * pair + side
                lse_ref[0, head : head + 1, :] = top + jnp.log(mass)
                probs = (powers * (1.0 / mass)).astype(BF16)
                part = dot(only(values, side), probs, 0, 0)
                total = part if total is None else total + part
            mixed_ref[0, :, at : at + 2 * HEAD] = total.T.astype(BF16)

    block = (count, rows, width)
    return pl.pallas_call(
        kernel,
        cost_estimate=cost(8),
        grid=(count,),
        in_specs=[
            pl.BlockSpec(memory_space=pltpu.SMEM),
            each(qkv.shape),
            spread(summaries.shape),
        ],
        out_specs=[each(block), each((count, HEADS, rows))],
        out_shape=[
            jax.ShapeDtypeStruct(block, BF16),
            jax.ShapeDtypeStruct((count, HEADS, rows), F32),
        ],
    )(place(), qkv, summaries)


def split_rows(total):
    high = total.astype(BF16).astype(F32)
    return high, total - high


def vector_block(narrow, wide, per):
    def block(s):
        left = pl.multiple_of(s * per // 128 * 128, 128)
        found = narrow[:, pl.ds(left, 128)]
        if wide is not None:
            step = wide.shape[1] // narrow.shape[1] * per
            for k in range(step // 128):
                chunk = wide[:, pl.ds(pl.multiple_of(s * step + k * 128, 128), 128)]
                row = lax.broadcasted_iota(jnp.int32, chunk.shape, 0)
                keep = (row % (VEC_ROWS // 2)) == 4 + k
                found = found + jnp.where(keep, chunk, 0.0)
        return found.astype(BF16)

    return block


def feed(inputs, cotangent, mixed, narrow, long_bias, pieces, wide, shards, tiles):
    count, _, width = inputs.shape
    hidden_width = long_bias.shape[1]
    arrays = [piece for piece, _, _ in pieces] if tiles else list(wide)
    step = 512
    grads = [(width, width), (width, hidden_width), (hidden_width, width)]
    segments = columns(shards) + [("vec", VEC_ROWS)]
    targets = spots(shards)
    orders = pack_order() if tiles else None
    half = sum(size for _, size in segments) // 2
    per = width // lax.axis_size("seq")

    def kernel(spot, x_ref, cot_ref, mixed_ref, lines_ref, bu_ref, *rest):
        ins, rest = rest[: len(arrays)], rest[len(arrays) :]
        out_ref, mgrad_ref, xgrad_ref, narrow_ref, wide_ref, *rest = rest
        if tiles:
            packs, rest = rest[:4], rest[4:]
            go_ref, gu_ref, gd_ref, high_ref, long_ref, wo_ref, wu_ref, wd_ref = rest
        else:
            go_ref, gu_ref, gd_ref = rest
            wo_ref, wu_ref, wd_ref = ins
        step_id = pl.program_id(0)
        bias, gain, shift, last = (lines_ref[k : k + 1, :] for k in (4, 2, 3, 5))

        @pl.when(step_id == 0)
        def _():
            for ref in (go_ref, gu_ref, gd_ref, narrow_ref, wide_ref):
                ref[...] = jnp.zeros_like(ref)
            if tiles:
                weights = (wo_ref, wu_ref, wd_ref)
                assemble(spot, ins, pieces, segments[:-1], targets, weights, None)

        middle = x_ref[0].astype(F32) + (dot(mixed_ref[0], wo_ref[...]) + bias)
        cot = cot_ref[0]
        tangent = cot.astype(BF16)
        unit, scale = norm_parts(middle)
        normed = (unit * gain + shift).astype(BF16)
        flipped = normed.T
        final = middle + last
        back = None
        for at in range(0, hidden_width, step):
            here = slice(at, at + step)
            hidden = dot(normed, wu_ref[:, here]) + bu_ref[:, here]
            active, slope = gelu_pair(hidden)
            active = active.astype(BF16)
            final = final + dot(active, wd_ref[here, :])
            gd_ref[here, :] += dot(active, tangent, 0, 0)
            grad = (dot(tangent, wd_ref[here, :], 1, 1) * slope).astype(BF16)
            gu_ref[:, here] += dot(flipped, grad)
            wide_ref[0:1, here] += jnp.sum(grad.astype(F32), 0, keepdims=True)
            part = dot(grad, wu_ref[:, here], 1, 1)
            back = part if back is None else back + part
        out_ref[0] = final.astype(BF16)
        narrow_ref[0:1, :] += jnp.sum(back * unit, 0, keepdims=True)
        narrow_ref[1:2, :] += jnp.sum(back, 0, keepdims=True)
        middle_grad = cot + norm_back(back, unit, scale, gain)
        mgrad_ref[0] = middle_grad
        branch = middle_grad.astype(BF16)
        narrow_ref[2:3, :] += jnp.sum(branch.astype(F32), 0, keepdims=True)
        narrow_ref[3:4, :] += jnp.sum(tangent.astype(F32), 0, keepdims=True)
        go_ref[...] += dot(mixed_ref[0], branch, 0, 0)
        xgrad_ref[0] = dot(branch, wo_ref[...], 1, 1).astype(BF16)

        if tiles:

            @pl.when(step_id == count - 1)
            def _():
                for ref, source, k in ((high_ref, narrow_ref, 8), (long_ref, wide_ref, 1)):
                    high, low = split_rows(source[...])
                    zero = jnp.zeros((8, source.shape[1]), F32)
                    if k == 1:
                        high = jnp.broadcast_to(high[0:1], zero.shape)
                        low = jnp.broadcast_to(low[0:1], zero.shape)
                    ref[...] = jnp.concatenate([high, zero, low, zero], 0)
                write_packed(
                    spot,
                    (go_ref, gu_ref, gd_ref),
                    vector_block(high_ref, long_ref, per),
                    packs,
                    segments,
                    targets,
                    orders,
                )

    block = inputs.shape
    out_shape = [
        jax.ShapeDtypeStruct(block, BF16),
        jax.ShapeDtypeStruct(block, F32),
        jax.ShapeDtypeStruct(block, BF16),
        jax.ShapeDtypeStruct((8, width), F32),
        jax.ShapeDtypeStruct((8, hidden_width), F32),
    ]
    out_specs = [each(block)] * 3 + [full((8, width)), full((8, hidden_width))]
    scratch = []
    if tiles:
        packed_shapes = [(len(names) // 2, half, 128) for names in orders for _ in range(2)]
        out_shape += [jax.ShapeDtypeStruct(shape, BF16) for shape in packed_shapes]
        out_specs += [pl.BlockSpec(memory_space=pltpu.VMEM)] * 4
        scratch = [pltpu.VMEM(shape, F32) for shape in grads]
        scratch += [pltpu.VMEM((VEC_ROWS, width), F32), pltpu.VMEM((VEC_ROWS, hidden_width), F32)]
        scratch += [pltpu.VMEM(shape, BF16) for shape in grads]
    else:
        out_shape += [jax.ShapeDtypeStruct(shape, F32) for shape in grads]
        out_specs += [full(shape) for shape in grads]
    return pl.pallas_call(
        kernel,
        cost_estimate=cost(35),
        grid=(count,),
        in_specs=[pl.BlockSpec(memory_space=pltpu.SMEM)]
        + [each(block)] * 3
        + [full(narrow.shape), full(long_bias.shape)]
        + [pl.BlockSpec(memory_space=pltpu.VMEM)] * len(arrays),
        out_specs=out_specs,
        out_shape=out_shape,
        scratch_shapes=scratch,
    )(place(), inputs, cotangent, mixed, narrow, long_bias, *arrays)


def attend_back(qkv, summaries, lse, mixed_grad, first, number, before=(), after=()):
    _, rows, width = mixed_grad.shape
    far = 2 * summaries.shape[0]
    extra = list(before) + list(after)

    def each(shape):
        return pl.BlockSpec(
            (1,) + tuple(shape[1:]), lambda i: (i + first,) + (0,) * (len(shape) - 1)
        )

    def kernel(spot, qkv_ref, sum_ref, lse_ref, grad_ref, *rest):
        dq_ref, dk_ref, dv_ref, far_ref = rest[len(extra) :]
        seen = seen_rows(spot[0], far, rows)
        spans = jnp.concatenate([sum_ref[p, 0] for p in range(far // 2)], 0)
        for pair in range(HEADS // 2):
            at = pair * 2 * HEAD
            lanes = slice(at, at + 2 * HEAD)
            query = qkv_ref[0, :, lanes]
            pull = grad_ref[0, :, lanes]
            keys = jnp.concatenate(
                [qkv_ref[0, :, width + at : width + at + 2 * HEAD], spans[:, lanes]], 0
            )
            values = jnp.concatenate(
                [
                    qkv_ref[0, :, 2 * width + at : 2 * width + at + 2 * HEAD],
                    spans[:, width + at : width + at + 2 * HEAD],
                ],
                0,
            )
            d_query = d_keys = d_values = 0.0
            for side in range(2):
                head = 2 * pair + side
                own = only(query, side)
                own_pull = only(pull, side)
                scores = scores_of(keys, own, seen, rows)
                probs = jnp.exp(scores - lse_ref[0, head : head + 1, :])
                dots = dot(values, own_pull, 1, 1)
                centre = jnp.sum(probs * dots, 0, keepdims=True)
                slope = (probs * (dots - centre)).astype(BF16)
                d_values = d_values + dot(probs.astype(BF16), own_pull)
                d_keys = d_keys + dot(slope, own)
                d_query = d_query + dot(only(keys, side), slope, 0, 0)
            d_keys = d_keys * HEAD ** (-0.5)
            dq_ref[0, :, lanes] = (d_query * HEAD ** (-0.5)).T.astype(BF16)
            dk_ref[0, :, lanes] = d_keys[:rows]
            dv_ref[0, :, lanes] = d_values[:rows]
            for k, terms in enumerate((d_keys, d_values)):
                left = k * width + at
                for p in range(far // 2):
                    part = terms[rows + 2 * p : rows + 2 * p + 2].astype(BF16)
                    far_ref[p, 0, :, left : left + 2 * HEAD] = part

    block = mixed_grad.shape
    return pl.pallas_call(
        kernel,
        cost_estimate=cost(7),
        grid=(number,),
        in_specs=[
            pl.BlockSpec(memory_space=pltpu.SMEM),
            each(qkv.shape),
            spread(summaries.shape, first),
            each(lse.shape),
            each(block),
        ]
        + [pl.BlockSpec(memory_space=pl.ANY)] * len(extra),
        out_specs=[each(block)] * 3 + [spread(summaries.shape, first)],
        out_shape=[
            jax.ShapeDtypeStruct(block, BF16),
            jax.ShapeDtypeStruct(block, F32),
            jax.ShapeDtypeStruct(block, F32),
            jax.ShapeDtypeStruct(summaries.shape, BF16),
        ],
        input_output_aliases={5 + k: k for k in range(len(before))},
    )(place(), qkv, summaries, lse, mixed_grad, *extra)


def project_back(
    inputs, d_query, d_keys, d_values, owned, weights, narrow, middle_grad, shards, tiles, after
):
    count, rows, width = inputs.shape
    half_span = rows // 2
    segments = columns(shards) + [("vec", VEC_ROWS)]
    targets = spots(shards)
    orders = pack_order() if tiles else None
    half = sum(size for _, size in segments) // 2
    per = width // lax.axis_size("seq")

    def kernel(spot, x_ref, dq_ref, dk_ref, dv_ref, own_ref, wq_ref, wk_ref, wv_ref,
               lines_ref, mgrad_ref, *rest):
        igrad_ref, narrow_ref, *rest = rest[len(after) :]
        gain, shift = lines_ref[0:1, :], lines_ref[1:2, :]
        if tiles:
            packs, (gq_ref, gk_ref, gv_ref, high_ref) = rest[:4], rest[4:]
        else:
            gq_ref, gk_ref, gv_ref = rest
        step_id = pl.program_id(0)

        @pl.when(step_id == 0)
        def _():
            for ref in (gq_ref, gk_ref, gv_ref, narrow_ref):
                ref[...] = jnp.zeros_like(ref)

        unit, scale = norm_parts(x_ref[0].astype(F32))
        flipped = (unit * gain + shift).astype(BF16).T
        back = dot(dq_ref[0], wq_ref[...], 1, 1)
        gq_ref[...] += dot(flipped, dq_ref[0])
        for k, (direct, w_ref, g_ref) in enumerate(
            ((dk_ref, wk_ref, gk_ref), (dv_ref, wv_ref, gv_ref))
        ):
            act = jnp.concatenate(
                [
                    direct[0, j * half_span : (j + 1) * half_span, :]
                    + own_ref[0, j : j + 1, k * width : (k + 1) * width] / half_span
                    for j in range(2)
                ],
                0,
            ).astype(BF16)
            g_ref[...] += dot(flipped, act)
            back = back + dot(act, w_ref[...], 1, 1)
        narrow_ref[0:1, :] += jnp.sum(back * unit, 0, keepdims=True)
        narrow_ref[1:2, :] += jnp.sum(back, 0, keepdims=True)
        igrad_ref[0] = mgrad_ref[0] + norm_back(back, unit, scale, gain)

        if tiles:

            @pl.when(step_id == count - 1)
            def _():
                high, low = split_rows(narrow_ref[...])
                zero = jnp.zeros_like(high)
                high_ref[...] = jnp.concatenate([high, zero, low, zero], 0)
                write_packed(
                    spot,
                    (gq_ref, gk_ref, gv_ref),
                    vector_block(high_ref, None, per),
                    packs,
                    segments,
                    targets,
                    orders,
                )

    block = inputs.shape
    square = (width, width)
    out_shape = [jax.ShapeDtypeStruct(block, F32), jax.ShapeDtypeStruct((8, width), F32)]
    out_specs = [each(block), full((8, width))]
    scratch = []
    if tiles:
        packed_shapes = [(len(names) // 2, half, 128) for names in orders for _ in range(2)]
        out_shape += [jax.ShapeDtypeStruct(shape, BF16) for shape in packed_shapes]
        out_specs += [pl.BlockSpec(memory_space=pltpu.VMEM)] * 4
        scratch = [pltpu.VMEM(square, F32)] * 3 + [pltpu.VMEM((VEC_ROWS, width), F32)]
    else:
        out_shape += [jax.ShapeDtypeStruct(square, F32)] * 3
        out_specs += [full(square)] * 3
    return pl.pallas_call(
        kernel,
        cost_estimate=cost(10),
        grid=(count,),
        in_specs=[pl.BlockSpec(memory_space=pltpu.SMEM)]
        + [each(block)] * 4
        + [each(owned.shape)]
        + [full(square)] * 3
        + [full(narrow.shape), each(block)]
        + [pl.BlockSpec(memory_space=pl.ANY)] * len(after),
        out_specs=out_specs,
        out_shape=out_shape,
        scratch_shapes=scratch,
    )(place(), inputs, d_query, d_keys, d_values, owned, *weights, narrow, middle_grad, *after)


def layer(
    inputs,
    cotangent,
    query_weight,
    key_weight,
    value_weight,
    out_weight,
    up_weight,
    down_weight,
    norm1_gain,
    norm1_bias,
    norm2_gain,
    norm2_bias,
    out_bias,
    up_bias,
    down_bias,
):
    shards = [query_weight, key_weight, value_weight, out_weight, up_weight, down_weight]
    slices = [norm1_gain, norm1_bias, norm2_gain, norm2_bias, out_bias, up_bias, down_bias]
    tiles = whole_tiles(shards, slices)
    count, _, width = inputs.shape
    wide, lines, early, late = [None] * 6, (), (), ()
    if tiles:
        state = gather_outer(pack_shards(shards[:3], slices))
        other = gather_outer(pack_shards(shards[3:], [], state))
        early = gather_inner(state)
        late = gather_inner(other)
    else:
        wide, members = gather_plain(shards, slices)
        blank = jnp.zeros((NARROW - 6, width), F32)
        lines = (
            jnp.concatenate([jnp.stack([members[k] for k in (0, 1, 2, 3, 4, 6)]), blank]),
            members[5][None],
        )
    qkv, pooled, w_query, w_key, w_value, narrow, long_bias = project(
        inputs, shards[:3], slices, early, wide[:3], lines, tiles
    )
    summaries = gather_seq(pooled)
    mixed, lse = attend(qkv, summaries)
    outputs, middle_grad, mixed_grad, narrow_two, wide_two, *second = feed(
        inputs, cotangent, mixed, narrow, long_bias, late, wide[3:], shards[3:], tiles
    )
    ties = []
    if tiles:
        second = reduce_step([tuple(second[:2]), tuple(second[2:])], 0)
        ties = [member for couple in second for member in couple]
    begun = attend_back(qkv, summaries, lse, mixed_grad, 0, count // 2)
    d_query, d_keys, d_values, terms = attend_back(
        qkv, summaries, lse, mixed_grad, count // 2, count - count // 2, begun, ties
    )
    if tiles:
        second = reduce_step(second, 1)
        ties = [member for couple in second for member in couple]
    owned = reduce_seq(terms)
    input_grad, narrow_one, *first = project_back(
        inputs,
        d_query,
        d_keys,
        d_values,
        owned,
        (w_query, w_key, w_value),
        narrow,
        middle_grad,
        shards[:3],
        tiles,
        ties,
    )
    if tiles:
        size = norm1_gain.shape[0]
        second = reduce_step(second, 2, True)
        first = reduce_step([tuple(first[:2]), tuple(first[2:])], 0)
        first = reduce_step(reduce_step(first, 1), 2, True)
        tail = reduce_end(second, shards[3:], [size] * 4 + [up_bias.shape[0]])
        front = reduce_end(first, shards[:3], [size] * 2)
        matrices = front[:3] + tail[:3]
        vectors = front[3:] + tail[3:6] + [tail[7], tail[6]]
    else:
        vectors = [
            narrow_one[0],
            narrow_one[1],
            narrow_two[0],
            narrow_two[1],
            narrow_two[2],
            wide_two[0],
            narrow_two[3],
        ]
        reduced = reduce_plain(list(first) + list(second), vectors)
        matrices, vectors = reduced[:6], reduced[6:]
    return (outputs, input_grad, *matrices, *vectors)


def solution(mesh):
    placed = (
        P("batch", "seq", None),
        P("batch", "seq", None),
        P("seq", "batch"),
        P("seq", "batch"),
        P("seq", "batch"),
        P("seq", "batch"),
        P("seq", "batch"),
        P("seq", "batch"),
        P("seq"),
        P("seq"),
        P("seq"),
        P("seq"),
        P("seq"),
        P("seq"),
        P("seq"),
    )
    return jax.shard_map(
        layer,
        mesh=mesh,
        in_specs=placed,
        out_specs=(
            P("batch", "seq", None),
            P("batch", "seq", None),
            P("seq", "batch"),
            P("seq", "batch"),
            P("seq", "batch"),
            P("seq", "batch"),
            P("seq", "batch"),
            P("seq", "batch"),
            P("seq"),
            P("seq"),
            P("seq"),
            P("seq"),
            P("seq"),
            P("seq"),
            P("seq"),
        ),
        check_vma=False,
    )
```

```python
import jax
import jax.numpy as jnp
from jax import lax
from jax.experimental import pallas as pl
from jax.experimental.pallas import tpu as pltpu
from jax.sharding import PartitionSpec as P


HEADS = 8
HEAD = 64
VEC_ROWS = 32
F32 = jnp.float32
BF16 = jnp.bfloat16


def swap(array, axis, bit):
    count = lax.axis_size(axis)
    return lax.ppermute(array, axis, [(i, i ^ bit) for i in range(count)])


def bits_down(count):
    return [1 << k for k in range(count.bit_length() - 2, -1, -1)]


def outer_stages():
    seq = [("seq", bit) for bit in bits_down(lax.axis_size("seq")) if bit > 1]
    batch = [("batch", bit) for bit in bits_down(lax.axis_size("batch")) if bit > 2]
    return batch + seq


def relative_ids(stages):
    ids = [(0, 0)]
    for axis, bit in stages:
        moved = [(s ^ bit, b) if axis == "seq" else (s, b ^ bit) for s, b in ids]
        ids = ids + moved
    return ids


X_STAGE = ("batch", 2)
Y_STAGE = ("seq", 1)
CORE = ("batch", 1)


def gather_outer(state):
    for stage in outer_stages():
        theirs = swap(state, *stage)
        state = jnp.concatenate([state, theirs], 0)
    return state


def gather_inner(state):
    half = state.shape[1] // 2
    outer = outer_stages()
    pieces = []
    for k, order in enumerate(((X_STAGE, Y_STAGE), (Y_STAGE, X_STAGE))):
        first = k * half
        part = state[:, first : first + half]
        theirs = swap(part, *order[0])
        part = jnp.concatenate([part, theirs], 0)
        far = swap(part, *order[1])
        ids = relative_ids(outer + [order[0]])
        full = relative_ids(outer + list(order))
        far_ids = full[len(ids) :]
        for piece, names in ((part, ids), (far, far_ids)):
            pieces.append((piece, names, first))
            pieces.append((swap(piece, *CORE), [(s, b ^ 1) for s, b in names], first))
    return pieces


def place():
    return jnp.stack([lax.axis_index("seq"), lax.axis_index("batch")]).astype(jnp.int32)


def cuts(segments, first, half):
    found = []
    at = 0
    for name, rows in segments:
        low, high = max(at, first), min(at + rows, first + half)
        if low < high:
            found.append((name, low - at, low - first, high - low))
        at += rows
    return found


def assemble(spot, refs, pieces, segments, targets, outs, vec):
    for ref, (piece, names, first) in zip(refs, pieces):
        for p, (sr, br) in enumerate(names):
            s, b = spot[0] ^ sr, spot[1] ^ br
            for name, row, here, size in cuts(segments, first, piece.shape[1]):
                if name == "vec":
                    if br == 0:
                        vec(ref[p, here : here + size, :], s)
                else:
                    number, top, left = targets(name, row, s, b)
                    outs[number][
                        pl.ds(pl.multiple_of(top, 16), size), pl.ds(pl.multiple_of(left, 128), 128)
                    ] = ref[p, here : here + size, :]


def pack_order():
    outer = outer_stages()
    return [
        relative_ids(outer + [Y_STAGE, X_STAGE, CORE]),
        relative_ids(outer + [X_STAGE, Y_STAGE, CORE]),
    ]


def write_packed(spot, ins, vec_block, outs, segments, targets, orders):
    half = sum(size for _, size in segments) // 2
    for k, (names, first) in enumerate(zip(orders, (0, half))):
        for p, (sr, br) in enumerate(names):
            s, b = spot[0] ^ sr, spot[1] ^ br
            out = outs[2 * k + p // (len(names) // 2)]
            p = p % (len(names) // 2)
            for name, row, here, size in cuts(segments, first, half):
                if name == "vec":
                    out[p, here : here + size, :] = vec_block(s)
                else:
                    number, top, left = targets(name, row, s, b)
                    out[p, here : here + size, :] = ins[number][
                        pl.ds(pl.multiple_of(top, 16), size), pl.ds(pl.multiple_of(left, 128), 128)
                    ].astype(BF16)


def add_low(mine, theirs):
    return (mine.astype(F32) + theirs.astype(F32)).astype(BF16)


def join_pair(array):
    count = VEC_ROWS // 2
    return array[..., -VEC_ROWS:-count, :].astype(F32) + array[..., -count:, :].astype(F32)


def split_pair(total):
    high = lax.reduce_precision(total, 8, 7)
    return [high.astype(BF16), (total - high).astype(BF16)]


def add_pairs(mine, theirs):
    total = join_pair(mine) + join_pair(theirs)
    low = add_low(mine[..., :-VEC_ROWS, :], theirs[..., :-VEC_ROWS, :])
    return jnp.concatenate([low] + split_pair(total), -2)


ORDERS = ((CORE, X_STAGE, Y_STAGE), (CORE, Y_STAGE, X_STAGE))


def reduce_step(halves, step, last=False):
    done = []
    for k, (kept, sent) in enumerate(halves):
        theirs = swap(sent, *ORDERS[k][step])
        if last:
            done.append((kept, theirs))
            continue
        state = (add_pairs if k == 1 else add_low)(kept, theirs)
        count = state.shape[0] // 2
        done.append((state[:count], state[count:]))
    return done


def sum_rows(mine, theirs, spans):
    total = mine.astype(F32) + theirs.astype(F32)
    count = VEC_ROWS // 2
    return total, [total[at : at + count] + total[at + count : at + VEC_ROWS] for at in spans]


def joined_sum(couples):
    count = couples[0][0].shape[0]
    rows = sum(kept.shape[1] for kept, _, _ in couples)

    def kernel(*refs):
        ins, outs = refs[:-2], refs[-2:]
        for p in range(count):
            out = outs[p // (count // 2)]
            at = 0
            for k, (kept, _, vectors) in enumerate(couples):
                size = kept.shape[1]
                total, pairs = sum_rows(
                    ins[2 * k][p], ins[2 * k + 1][p], [size - VEC_ROWS] if vectors else []
                )
                out[p % (count // 2), at : at + size, :] = total.astype(BF16)
                for pair in pairs:
                    high = pair.astype(BF16)
                    low = (pair - high.astype(F32)).astype(BF16)
                    end = at + size
                    out[p % (count // 2), end - VEC_ROWS : end - VEC_ROWS // 2, :] = high
                    out[p % (count // 2), end - VEC_ROWS // 2 : end, :] = low
                at += size

    arrays = [array for kept, theirs, _ in couples for array in (kept, theirs)]
    return pl.pallas_call(
        kernel,
        cost_estimate=cost(2),
        out_shape=[jax.ShapeDtypeStruct((count // 2, rows, 128), BF16)] * 2,
        in_specs=[pl.BlockSpec(memory_space=pltpu.VMEM)] * len(arrays),
        out_specs=[pl.BlockSpec(memory_space=pltpu.VMEM)] * 2,
    )(*arrays)


def again(kept, theirs, spans):
    count, rows = kept.shape[:2]

    def kernel(mine_ref, theirs_ref, *outs):
        for p in range(count):
            out = outs[p // (count // 2)]
            q = p % (count // 2)
            total, pairs = sum_rows(mine_ref[p], theirs_ref[p], spans)
            out[q] = total.astype(BF16)
            for pair, at in zip(pairs, spans):
                high = pair.astype(BF16)
                out[q, at : at + VEC_ROWS // 2, :] = high
                low = (pair - high.astype(F32)).astype(BF16)
                out[q, at + VEC_ROWS // 2 : at + VEC_ROWS, :] = low

    return pl.pallas_call(
        kernel,
        cost_estimate=cost(2),
        out_shape=[jax.ShapeDtypeStruct((count // 2, rows, 128), BF16)] * 2,
        in_specs=[pl.BlockSpec(memory_space=pltpu.VMEM)] * 2,
        out_specs=[pl.BlockSpec(memory_space=pltpu.VMEM)] * 2,
    )(kept, theirs)


def finish(kept, theirs, parts, spans, shapes, sizes):
    def kernel(spot, mine_ref, theirs_ref, *outs):
        total, pairs = sum_rows(mine_ref[0], theirs_ref[0], spans)
        for number, row, left, at, size in parts:
            outs[number][row : row + size, left : left + 128] = total[at : at + size]
        (pair,) = pairs
        row = 0
        for out, size in zip(outs[len(shapes) :], sizes):
            if size < 128:
                line = pair[row : row + 1]
                found = line[:, :size]
                for k in range(1, 128 // size):
                    part = line[:, k * size : (k + 1) * size]
                    found = jnp.where(spot[0] % (128 // size) == k, part, found)
                out[...] = found.reshape(size)
                row += 1
            else:
                for at in range(0, size, 128):
                    out[at : at + 128] = pair[row : row + 1].reshape(128)
                    row += 1

    return pl.pallas_call(
        kernel,
        cost_estimate=cost(2),
        out_shape=[jax.ShapeDtypeStruct(shape, F32) for shape in shapes]
        + [jax.ShapeDtypeStruct((size,), F32) for size in sizes],
        in_specs=[pl.BlockSpec(memory_space=pltpu.SMEM)]
        + [pl.BlockSpec(memory_space=pltpu.VMEM)] * 2,
        out_specs=[pl.BlockSpec(memory_space=pltpu.VMEM)] * (len(shapes) + len(sizes)),
    )(place(), kept, theirs)


def reduce_end(halves, weights, sizes):
    segments = columns(weights) + [("vec", VEC_ROWS)]
    parts = []
    spans = []
    at = 0
    for k, (kept, _) in enumerate(halves):
        half = kept.shape[1]
        for name, row, here, size in cuts(segments, k * half, half):
            if name == "vec":
                spans.append(at + here)
            else:
                parts.append((name[0], row, name[1] * 128, at + here, size))
        at += half
    kept, sent = joined_sum([(kept, theirs, k == 1) for k, (kept, theirs) in enumerate(halves)])
    stages = outer_stages()[::-1]
    for k, stage in enumerate(stages):
        theirs = swap(sent, *stage)
        if k < len(stages) - 1:
            kept, sent = again(kept, theirs, spans)
    return list(finish(kept, theirs, parts, spans, [w.shape for w in weights], sizes))


def seq_stages():
    return [("seq", bit) for bit in bits_down(lax.axis_size("seq"))]


def gather_seq(array):
    state = array[None]
    for stage in seq_stages():
        state = jnp.concatenate([state, swap(state, *stage)], 0)
    return state


def reduce_seq(state):
    for stage in seq_stages()[::-1]:
        count = state.shape[0] // 2
        theirs = swap(state[count:], *stage)
        total = state[:count].astype(F32) + theirs.astype(F32)
        state = total if count == 1 else total.astype(BF16)
    return state[0]


def whole_tiles(weights, vectors):
    return (
        all(w.shape[0] % 16 == 0 and w.shape[1] % 128 == 0 for w in weights)
        and all(128 % v.shape[0] == 0 or v.shape[0] % 128 == 0 for v in vectors)
        and sum(v.shape[0] for v in vectors) % 128 == 0
    )


def columns(weights):
    return [
        ((i, c), weight.shape[0])
        for i, weight in enumerate(weights)
        for c in range(weight.shape[1] // 128)
    ]


def spots(weights):
    def targets(name, row, s, b):
        if name == "vec":
            return (len(weights), s * VEC_ROWS + row, 0)
        i, c = name
        rows, width = weights[i].shape
        return (i, s * rows + row, b * width + c * 128)

    return targets


def pack_shards(weights, vectors, after=None):
    segments = columns(weights) + ([("vec", VEC_ROWS)] if vectors else [])
    rows = sum(size for _, size in segments)
    extra = [] if after is None else [after]

    def kernel(spot, *refs):
        out = refs[-1]
        at = 0
        for ref, weight in zip(refs, weights):
            for left in range(0, weight.shape[1], 128):
                out[0, at : at + weight.shape[0], :] = ref[:, left : left + 128]
                at += weight.shape[0]
        if not vectors:
            return
        found = []
        for ref in refs[len(weights) : len(weights) + len(vectors)]:
            size = ref.shape[0]
            line = ref[...].astype(F32)
            if size < 128:
                line = jnp.concatenate([line[None]] * (128 // size), 1)
                lane = lax.broadcasted_iota(jnp.int32, line.shape, 1)
                found.append(jnp.where(lane // size == spot[0] % (128 // size), line, 0.0))
            else:
                found += [line[None, k : k + 128] for k in range(0, size, 128)]
        row = lax.broadcasted_iota(jnp.int32, (VEC_ROWS, 128), 0)
        block = jnp.zeros((VEC_ROWS, 128), F32)
        for k, line in enumerate(found):
            block = jnp.where(row == k, line, block)
        out[0, at:, :] = block.astype(BF16)

    return pl.pallas_call(
        kernel,
        out_shape=jax.ShapeDtypeStruct((1, rows, 128), BF16),
        in_specs=[pl.BlockSpec(memory_space=pltpu.SMEM)]
        + [pl.BlockSpec(memory_space=pltpu.VMEM)] * (len(weights) + len(vectors))
        + [pl.BlockSpec(memory_space=pl.ANY)] * len(extra),
        out_specs=pl.BlockSpec(memory_space=pltpu.VMEM),
    )(place(), *weights, *vectors, *extra)


def gather_plain(weights, vectors):
    wide = [lax.all_gather(w, "batch", axis=1, tiled=True) for w in weights]
    wide = [lax.all_gather(w, "seq", axis=0, tiled=True) for w in wide]
    return wide, [lax.all_gather(v, "seq", axis=0, tiled=True).astype(F32) for v in vectors]


def reduce_plain(grads, vectors):
    outs = [
        lax.psum_scatter(g.astype(BF16), "batch", scatter_dimension=1, tiled=True).astype(F32)
        for g in grads
    ]
    outs = outs + list(lax.psum(tuple(vectors), "batch"))
    return [lax.psum_scatter(o, "seq", scatter_dimension=0, tiled=True) for o in outs]


def dot(left, right, a=1, b=0):
    return lax.dot_general(left, right, (((a,), (b,)), ((), ())), preferred_element_type=F32)


def norm_parts(values):
    centred = values - jnp.mean(values, -1, keepdims=True)
    scale = lax.rsqrt(jnp.mean(centred * centred, -1, keepdims=True) + 1e-05)
    return centred * scale, scale


def norm_back(grad, unit, scale, gain):
    inner = grad * gain
    pull = jnp.mean(inner, -1, keepdims=True)
    twist = jnp.mean(inner * unit, -1, keepdims=True)
    return scale * (inner - pull - unit * twist)


def gelu_pair(values):
    bell = jnp.exp(-0.5 * values * values)
    t = 1.0 / (1.0 + (0.3275911 * 0.5**0.5) * jnp.abs(values))
    poly = 1.061405429 * 0.5
    for factor in (-1.453152027, 1.421413741, -0.284496736, 0.254829592):
        poly = poly * t + factor * 0.5
    below = poly * t * bell
    share = jnp.where(values < 0, below, 1.0 - below)
    return values * share, share + values * bell * 0.3989422804014327


def full(shape):
    return pl.BlockSpec(shape, lambda i: (0,) * len(shape))


def each(shape):
    return pl.BlockSpec((1,) + tuple(shape[1:]), lambda i: (i,) + (0,) * (len(shape) - 1))


NARROW = 8


def cost(micros):
    return pl.CostEstimate(flops=int(micros * 1e9), transcendentals=0, bytes_accessed=1 << 20)


def spread(shape, first=0):
    return pl.BlockSpec((shape[0], 1) + tuple(shape[2:]), lambda i: (0, i + first, 0, 0))


def span_means(inputs):
    count, rows, width = inputs.shape
    half = rows // 2

    def kernel(x_ref, out_ref):
        unit, _ = norm_parts(x_ref[0].astype(F32))
        for j in range(2):
            mean = jnp.sum(unit[j * half : (j + 1) * half], 0, keepdims=True) / half
            high = mean.astype(BF16)
            out_ref[0, j : j + 1, :width] = high
            out_ref[0, j : j + 1, width:] = (mean - high.astype(F32)).astype(BF16)

    shape = (count, 2, 2 * width)
    return pl.pallas_call(
        kernel,
        cost_estimate=cost(3),
        grid=(count,),
        in_specs=[each(inputs.shape)],
        out_specs=each(shape),
        out_shape=jax.ShapeDtypeStruct(shape, BF16),
    )(inputs)


def far_means(ref):
    rows = jnp.concatenate([ref[p, 0].astype(F32) for p in range(ref.shape[0])], 0)
    width = rows.shape[1] // 2
    return rows[:, :width] + rows[:, width:]


def project(inputs, means, shards, slices, pieces, wide, lines, tiles):
    count, rows, width = inputs.shape
    far = 2 * means.shape[0]
    hidden = slices[5].shape[0] * lax.axis_size("seq")
    segments = columns(shards) + [("vec", VEC_ROWS)]
    targets = spots(shards)
    order = (0, 1, 2, 3, 4, 6)
    arrays = [piece for piece, _, _ in pieces] if tiles else list(wide) + list(lines)

    def kernel(spot, x_ref, means_ref, *refs):
        ins = refs[: len(arrays)]
        out_ref, sums_ref, q_ref, k_ref, v_ref, narrow_ref, wide_ref = refs[len(arrays) :]

        @pl.when(pl.program_id(0) == 0)
        def _():
            if tiles:
                narrow_ref[...] = jnp.zeros_like(narrow_ref)
                wide_ref[...] = jnp.zeros_like(wide_ref)

                def vec(block, s):
                    block = block.astype(F32)
                    row = 0
                    for k, member in enumerate(slices):
                        size = member.shape[0]
                        start = s * size
                        for at in range(0, size, 128):
                            left = pl.multiple_of((start + at) // 128 * 128, 128)
                            line = block[row : row + 1]
                            if k == 5:
                                wide_ref[0:1, pl.ds(left, 128)] += line
                            else:
                                to = order.index(k)
                                narrow_ref[to : to + 1, pl.ds(left, 128)] += line
                            row += 1

                assemble(spot, ins, pieces, segments, targets, (q_ref, k_ref, v_ref), vec)
            else:
                for ref, source in zip((q_ref, k_ref, v_ref, narrow_ref, wide_ref), ins):
                    ref[...] = source[...]

        unit, _ = norm_parts(x_ref[0].astype(F32))
        normed = (unit * narrow_ref[0:1, :] + narrow_ref[1:2, :]).astype(BF16)
        out_ref[0, :, :width] = dot(normed, q_ref[...]).astype(BF16)
        mean = far_means(means_ref) * narrow_ref[0:1, :] + narrow_ref[1:2, :]
        high = mean.astype(BF16)
        low = (mean - high.astype(F32)).astype(BF16)
        joined = jnp.concatenate([normed, high, low], 0)
        for k, ref in enumerate((k_ref, v_ref)):
            product = dot(joined, ref[...])
            out_ref[0, :, (k + 1) * width : (k + 2) * width] = product[:rows].astype(BF16)
            total = product[rows : rows + far] + product[rows + far :]
            sums_ref[0, :, k * width : (k + 1) * width] = total.astype(BF16)

    shapes = [(count, rows, 3 * width), (count, far, 2 * width)]
    square = (width, width)
    return pl.pallas_call(
        kernel,
        cost_estimate=cost(6),
        grid=(count,),
        in_specs=[
            pl.BlockSpec(memory_space=pltpu.SMEM),
            each(inputs.shape),
            spread(means.shape),
        ]
        + [pl.BlockSpec(memory_space=pltpu.VMEM)] * len(arrays),
        out_specs=[each(shape) for shape in shapes]
        + [full(square)] * 3
        + [full((NARROW, width)), full((1, hidden))],
        out_shape=[jax.ShapeDtypeStruct(shape, BF16) for shape in shapes + [square] * 3]
        + [jax.ShapeDtypeStruct((NARROW, width), F32), jax.ShapeDtypeStruct((1, hidden), F32)],
    )(place(), inputs, means, *arrays)


def head_mask(rows, lane_half):
    lane = lax.broadcasted_iota(jnp.int32, (rows, 2 * HEAD), 1)
    return (lane < HEAD) if lane_half == 0 else (lane >= HEAD)


def only(array, lane_half):
    return jnp.where(head_mask(array.shape[0], lane_half), array, jnp.zeros_like(array))


def seen_rows(seq, far, rows):
    row = lax.broadcasted_iota(jnp.int32, (far, rows), 0) // 2
    seen = jnp.zeros((far, rows), F32)
    for p, (rel, _) in enumerate(relative_ids(seq_stages())):
        seen = jnp.where(row == p, jnp.where((seq ^ rel) < seq, 1.0, 0.0), seen)
    return seen


def scores_of(keys, query, visible, rows):
    scores = dot(keys, query, 1, 1) * HEAD ** (-0.5)
    far = jnp.where(visible > 0, scores[rows:], -1e30)
    return jnp.concatenate([scores[:rows], far], 0)


def attend(qkv, summaries):
    count, rows, width = qkv.shape[0], qkv.shape[1], qkv.shape[2] // 3
    far = summaries.shape[1]

    def kernel(spot, qkv_ref, sum_ref, mixed_ref, lse_ref):
        seen = seen_rows(spot[0], far, rows)
        spans = sum_ref[0]
        for pair in range(HEADS // 2):
            at = pair * 2 * HEAD
            query = qkv_ref[0, :, at : at + 2 * HEAD]
            keys = jnp.concatenate(
                [
                    qkv_ref[0, :, width + at : width + at + 2 * HEAD],
                    spans[:, at : at + 2 * HEAD],
                ],
                0,
            )
            values = jnp.concatenate(
                [
                    qkv_ref[0, :, 2 * width + at : 2 * width + at + 2 * HEAD],
                    spans[:, width + at : width + at + 2 * HEAD],
                ],
                0,
            )
            total = None
            for side in range(2):
                scores = scores_of(keys, only(query, side), seen, rows)
                top = jnp.max(scores, 0, keepdims=True)
                powers = jnp.exp(scores - top)
                mass = jnp.sum(powers, 0, keepdims=True)
                head = 2 * pair + side
                lse_ref[0, head : head + 1, :] = top + jnp.log(mass)
                probs = (powers * (1.0 / mass)).astype(BF16)
                part = dot(only(values, side), probs, 0, 0)
                total = part if total is None else total + part
            mixed_ref[0, :, at : at + 2 * HEAD] = total.T.astype(BF16)

    block = (count, rows, width)
    return pl.pallas_call(
        kernel,
        cost_estimate=cost(8),
        grid=(count,),
        in_specs=[
            pl.BlockSpec(memory_space=pltpu.SMEM),
            each(qkv.shape),
            each(summaries.shape),
        ],
        out_specs=[each(block), each((count, HEADS, rows))],
        out_shape=[
            jax.ShapeDtypeStruct(block, BF16),
            jax.ShapeDtypeStruct((count, HEADS, rows), F32),
        ],
    )(place(), qkv, summaries)


def split_rows(total):
    high = total.astype(BF16).astype(F32)
    return high, total - high


def vector_block(narrow, wide, per):
    def block(s):
        left = pl.multiple_of(s * per // 128 * 128, 128)
        found = narrow[:, pl.ds(left, 128)]
        if wide is not None:
            step = wide.shape[1] // narrow.shape[1] * per
            for k in range(step // 128):
                chunk = wide[:, pl.ds(pl.multiple_of(s * step + k * 128, 128), 128)]
                row = lax.broadcasted_iota(jnp.int32, chunk.shape, 0)
                keep = (row % (VEC_ROWS // 2)) == 4 + k
                found = found + jnp.where(keep, chunk, 0.0)
        return found.astype(BF16)

    return block


def feed(inputs, cotangent, mixed, narrow, long_bias, pieces, wide, shards, tiles):
    count, _, width = inputs.shape
    hidden_width = long_bias.shape[1]
    arrays = [piece for piece, _, _ in pieces] if tiles else list(wide)
    step = 512
    grads = [(width, width), (width, hidden_width), (hidden_width, width)]
    segments = columns(shards) + [("vec", VEC_ROWS)]
    targets = spots(shards)
    orders = pack_order() if tiles else None
    half = sum(size for _, size in segments) // 2
    per = width // lax.axis_size("seq")

    def kernel(spot, x_ref, cot_ref, mixed_ref, lines_ref, bu_ref, *rest):
        ins, rest = rest[: len(arrays)], rest[len(arrays) :]
        out_ref, mgrad_ref, xgrad_ref, narrow_ref, wide_ref, *rest = rest
        if tiles:
            packs, rest = rest[:4], rest[4:]
            go_ref, gu_ref, gd_ref, high_ref, long_ref, wo_ref, wu_ref, wd_ref = rest
        else:
            go_ref, gu_ref, gd_ref = rest
            wo_ref, wu_ref, wd_ref = ins
        step_id = pl.program_id(0)
        bias, gain, shift, last = (lines_ref[k : k + 1, :] for k in (4, 2, 3, 5))

        @pl.when(step_id == 0)
        def _():
            for ref in (go_ref, gu_ref, gd_ref, narrow_ref, wide_ref):
                ref[...] = jnp.zeros_like(ref)
            if tiles:
                weights = (wo_ref, wu_ref, wd_ref)
                assemble(spot, ins, pieces, segments[:-1], targets, weights, None)

        middle = x_ref[0].astype(F32) + (dot(mixed_ref[0], wo_ref[...]) + bias)
        cot = cot_ref[0]
        tangent = cot.astype(BF16)
        unit, scale = norm_parts(middle)
        normed = (unit * gain + shift).astype(BF16)
        flipped = normed.T
        final = middle + last
        back = None
        for at in range(0, hidden_width, step):
            here = slice(at, at + step)
            hidden = dot(normed, wu_ref[:, here]) + bu_ref[:, here]
            active, slope = gelu_pair(hidden)
            active = active.astype(BF16)
            final = final + dot(active, wd_ref[here, :])
            gd_ref[here, :] += dot(active, tangent, 0, 0)
            grad = (dot(tangent, wd_ref[here, :], 1, 1) * slope).astype(BF16)
            gu_ref[:, here] += dot(flipped, grad)
            wide_ref[0:1, here] += jnp.sum(grad.astype(F32), 0, keepdims=True)
            part = dot(grad, wu_ref[:, here], 1, 1)
            back = part if back is None else back + part
        out_ref[0] = final.astype(BF16)
        narrow_ref[0:1, :] += jnp.sum(back * unit, 0, keepdims=True)
        narrow_ref[1:2, :] += jnp.sum(back, 0, keepdims=True)
        middle_grad = cot + norm_back(back, unit, scale, gain)
        mgrad_ref[0] = middle_grad
        branch = middle_grad.astype(BF16)
        narrow_ref[2:3, :] += jnp.sum(branch.astype(F32), 0, keepdims=True)
        narrow_ref[3:4, :] += jnp.sum(tangent.astype(F32), 0, keepdims=True)
        go_ref[...] += dot(mixed_ref[0], branch, 0, 0)
        xgrad_ref[0] = dot(branch, wo_ref[...], 1, 1).astype(BF16)

        if tiles:

            @pl.when(step_id == count - 1)
            def _():
                for ref, source, k in ((high_ref, narrow_ref, 8), (long_ref, wide_ref, 1)):
                    high, low = split_rows(source[...])
                    zero = jnp.zeros((8, source.shape[1]), F32)
                    if k == 1:
                        high = jnp.broadcast_to(high[0:1], zero.shape)
                        low = jnp.broadcast_to(low[0:1], zero.shape)
                    ref[...] = jnp.concatenate([high, zero, low, zero], 0)
                write_packed(
                    spot,
                    (go_ref, gu_ref, gd_ref),
                    vector_block(high_ref, long_ref, per),
                    packs,
                    segments,
                    targets,
                    orders,
                )

    block = inputs.shape
    out_shape = [
        jax.ShapeDtypeStruct(block, BF16),
        jax.ShapeDtypeStruct(block, F32),
        jax.ShapeDtypeStruct(block, BF16),
        jax.ShapeDtypeStruct((8, width), F32),
        jax.ShapeDtypeStruct((8, hidden_width), F32),
    ]
    out_specs = [each(block)] * 3 + [full((8, width)), full((8, hidden_width))]
    scratch = []
    if tiles:
        packed_shapes = [(len(names) // 2, half, 128) for names in orders for _ in range(2)]
        out_shape += [jax.ShapeDtypeStruct(shape, BF16) for shape in packed_shapes]
        out_specs += [pl.BlockSpec(memory_space=pltpu.VMEM)] * 4
        scratch = [pltpu.VMEM(shape, F32) for shape in grads]
        scratch += [pltpu.VMEM((VEC_ROWS, width), F32), pltpu.VMEM((VEC_ROWS, hidden_width), F32)]
        scratch += [pltpu.VMEM(shape, BF16) for shape in grads]
    else:
        out_shape += [jax.ShapeDtypeStruct(shape, F32) for shape in grads]
        out_specs += [full(shape) for shape in grads]
    return pl.pallas_call(
        kernel,
        cost_estimate=cost(35),
        grid=(count,),
        in_specs=[pl.BlockSpec(memory_space=pltpu.SMEM)]
        + [each(block)] * 3
        + [full(narrow.shape), full(long_bias.shape)]
        + [pl.BlockSpec(memory_space=pltpu.VMEM)] * len(arrays),
        out_specs=out_specs,
        out_shape=out_shape,
        scratch_shapes=scratch,
    )(place(), inputs, cotangent, mixed, narrow, long_bias, *arrays)


def attend_back(qkv, summaries, lse, mixed_grad, first, number, before=(), after=()):
    _, rows, width = mixed_grad.shape
    far = summaries.shape[1]
    extra = list(before) + list(after)

    def each(shape):
        return pl.BlockSpec(
            (1,) + tuple(shape[1:]), lambda i: (i + first,) + (0,) * (len(shape) - 1)
        )

    def kernel(spot, qkv_ref, sum_ref, lse_ref, grad_ref, *rest):
        dq_ref, dk_ref, dv_ref, far_ref = rest[len(extra) :]
        seen = seen_rows(spot[0], far, rows)
        spans = sum_ref[0]
        for pair in range(HEADS // 2):
            at = pair * 2 * HEAD
            lanes = slice(at, at + 2 * HEAD)
            query = qkv_ref[0, :, lanes]
            pull = grad_ref[0, :, lanes]
            keys = jnp.concatenate(
                [qkv_ref[0, :, width + at : width + at + 2 * HEAD], spans[:, lanes]], 0
            )
            values = jnp.concatenate(
                [
                    qkv_ref[0, :, 2 * width + at : 2 * width + at + 2 * HEAD],
                    spans[:, width + at : width + at + 2 * HEAD],
                ],
                0,
            )
            d_query = d_keys = d_values = 0.0
            for side in range(2):
                head = 2 * pair + side
                own = only(query, side)
                own_pull = only(pull, side)
                scores = scores_of(keys, own, seen, rows)
                probs = jnp.exp(scores - lse_ref[0, head : head + 1, :])
                dots = dot(values, own_pull, 1, 1)
                centre = jnp.sum(probs * dots, 0, keepdims=True)
                slope = (probs * (dots - centre)).astype(BF16)
                d_values = d_values + dot(probs.astype(BF16), own_pull)
                d_keys = d_keys + dot(slope, own)
                d_query = d_query + dot(only(keys, side), slope, 0, 0)
            d_keys = d_keys * HEAD ** (-0.5)
            dq_ref[0, :, lanes] = (d_query * HEAD ** (-0.5)).T.astype(BF16)
            dk_ref[0, :, lanes] = d_keys[:rows].astype(BF16)
            dv_ref[0, :, lanes] = d_values[:rows].astype(BF16)
            for k, terms in enumerate((d_keys, d_values)):
                left = k * width + at
                far_ref[0, :, left : left + 2 * HEAD] = terms[rows:].astype(BF16)

    block = mixed_grad.shape
    return pl.pallas_call(
        kernel,
        cost_estimate=cost(7),
        grid=(number,),
        in_specs=[
            pl.BlockSpec(memory_space=pltpu.SMEM),
            each(qkv.shape),
            each(summaries.shape),
            each(lse.shape),
            each(block),
        ]
        + [pl.BlockSpec(memory_space=pl.ANY)] * len(extra),
        out_specs=[each(block)] * 3 + [each(summaries.shape)],
        out_shape=[
            jax.ShapeDtypeStruct(block, BF16),
            jax.ShapeDtypeStruct(block, BF16),
            jax.ShapeDtypeStruct(block, BF16),
            jax.ShapeDtypeStruct(summaries.shape, BF16),
        ],
        input_output_aliases={5 + k: k for k in range(len(before))},
    )(place(), qkv, summaries, lse, mixed_grad, *extra)


def project_back(
    inputs, d_query, d_keys, d_values, terms, means, weights, narrow, shards, tiles
):
    count, rows, width = inputs.shape
    segments = columns(shards) + [("vec", VEC_ROWS)]
    targets = spots(shards)
    orders = pack_order() if tiles else None
    half = sum(size for _, size in segments) // 2
    per = width // lax.axis_size("seq")

    def kernel(spot, x_ref, dq_ref, dk_ref, dv_ref, terms_ref, means_ref, wq_ref, wk_ref, wv_ref,
               lines_ref, back_ref, far_ref, narrow_ref, *rest):
        gain, shift = lines_ref[0:1, :], lines_ref[1:2, :]
        if tiles:
            packs, (gq_ref, gk_ref, gv_ref, high_ref) = rest[:4], rest[4:]
        else:
            gq_ref, gk_ref, gv_ref = rest
        step_id = pl.program_id(0)

        @pl.when(step_id == 0)
        def _():
            for ref in (gq_ref, gk_ref, gv_ref, narrow_ref):
                ref[...] = jnp.zeros_like(ref)

        unit, _ = norm_parts(x_ref[0].astype(F32))
        unit_far = far_means(means_ref)
        joined = jnp.concatenate([unit, unit_far], 0)
        flipped = (joined * gain + shift).astype(BF16).T
        gq_ref[...] += dot(flipped[:, :rows], dq_ref[0])
        both = None
        for k, (direct, w_ref, g_ref) in enumerate(
            ((dk_ref, wk_ref, gk_ref), (dv_ref, wv_ref, gv_ref))
        ):
            act = jnp.concatenate([direct[0], terms_ref[0, :, k * width : (k + 1) * width]], 0)
            g_ref[...] += dot(flipped, act)
            part = dot(act, w_ref[...], 1, 1)
            both = part if both is None else both + part
        back = both[:rows] + dot(dq_ref[0], wq_ref[...], 1, 1)
        far = both[rows:]
        back_ref[0] = back
        for p in range(far.shape[0] // 2):
            far_ref[p, 0] = far[2 * p : 2 * p + 2].astype(BF16)
        narrow_ref[0:1, :] += jnp.sum(back * unit, 0, keepdims=True) + jnp.sum(
            far * unit_far, 0, keepdims=True
        )
        narrow_ref[1:2, :] += jnp.sum(both, 0, keepdims=True) + jnp.sum(
            back - both[:rows], 0, keepdims=True
        )

        if tiles:

            @pl.when(step_id == count - 1)
            def _():
                high, low = split_rows(narrow_ref[...])
                zero = jnp.zeros_like(high)
                high_ref[...] = jnp.concatenate([high, zero, low, zero], 0)
                write_packed(
                    spot,
                    (gq_ref, gk_ref, gv_ref),
                    vector_block(high_ref, None, per),
                    packs,
                    segments,
                    targets,
                    orders,
                )

    block = inputs.shape
    square = (width, width)
    sent = means.shape[:3] + (width,)
    out_shape = [
        jax.ShapeDtypeStruct(block, F32),
        jax.ShapeDtypeStruct(sent, BF16),
        jax.ShapeDtypeStruct((8, width), F32),
    ]
    out_specs = [each(block), spread(sent), full((8, width))]
    scratch = []
    if tiles:
        packed_shapes = [(len(names) // 2, half, 128) for names in orders for _ in range(2)]
        out_shape += [jax.ShapeDtypeStruct(shape, BF16) for shape in packed_shapes]
        out_specs += [pl.BlockSpec(memory_space=pltpu.VMEM)] * 4
        scratch = [pltpu.VMEM(square, F32)] * 3 + [pltpu.VMEM((VEC_ROWS, width), F32)]
    else:
        out_shape += [jax.ShapeDtypeStruct(square, F32)] * 3
        out_specs += [full(square)] * 3
    return pl.pallas_call(
        kernel,
        cost_estimate=cost(10),
        grid=(count,),
        in_specs=[pl.BlockSpec(memory_space=pltpu.SMEM)]
        + [each(block)] * 4
        + [each(terms.shape), spread(means.shape)]
        + [full(square)] * 3
        + [full(narrow.shape)],
        out_specs=out_specs,
        out_shape=out_shape,
        scratch_shapes=scratch,
    )(place(), inputs, d_query, d_keys, d_values, terms, means, *weights, narrow)


def input_back(inputs, back, owned, narrow, middle_grad):
    count, rows, _ = inputs.shape
    half = rows // 2

    def kernel(x_ref, back_ref, own_ref, lines_ref, mgrad_ref, out_ref):
        unit, scale = norm_parts(x_ref[0].astype(F32))
        back = jnp.concatenate(
            [
                back_ref[0, j * half : (j + 1) * half, :] + own_ref[0, j : j + 1, :] / half
                for j in range(2)
            ],
            0,
        )
        out_ref[0] = mgrad_ref[0] + norm_back(back, unit, scale, lines_ref[0:1, :])

    return pl.pallas_call(
        kernel,
        cost_estimate=cost(4),
        grid=(count,),
        in_specs=[each(inputs.shape)] * 2
        + [each(owned.shape), full(narrow.shape), each(inputs.shape)],
        out_specs=each(inputs.shape),
        out_shape=jax.ShapeDtypeStruct(inputs.shape, F32),
    )(inputs, back, owned, narrow, middle_grad)


def layer(
    inputs,
    cotangent,
    query_weight,
    key_weight,
    value_weight,
    out_weight,
    up_weight,
    down_weight,
    norm1_gain,
    norm1_bias,
    norm2_gain,
    norm2_bias,
    out_bias,
    up_bias,
    down_bias,
):
    shards = [query_weight, key_weight, value_weight, out_weight, up_weight, down_weight]
    slices = [norm1_gain, norm1_bias, norm2_gain, norm2_bias, out_bias, up_bias, down_bias]
    tiles = whole_tiles(shards, slices)
    count, _, width = inputs.shape
    wide, lines, early, late = [None] * 6, (), (), ()
    if tiles:
        state = gather_outer(pack_shards(shards[:3], slices))
        other = gather_outer(pack_shards(shards[3:], [], state))
        early = gather_inner(state)
        late = gather_inner(other)
    else:
        wide, members = gather_plain(shards, slices)
        blank = jnp.zeros((NARROW - 6, width), F32)
        lines = (
            jnp.concatenate([jnp.stack([members[k] for k in (0, 1, 2, 3, 4, 6)]), blank]),
            members[5][None],
        )
    means = gather_seq(span_means(inputs))
    qkv, summaries, w_query, w_key, w_value, narrow, long_bias = project(
        inputs, means, shards[:3], slices, early, wide[:3], lines, tiles
    )
    mixed, lse = attend(qkv, summaries)
    outputs, middle_grad, mixed_grad, narrow_two, wide_two, *second = feed(
        inputs, cotangent, mixed, narrow, long_bias, late, wide[3:], shards[3:], tiles
    )
    ties = []
    if tiles:
        second = reduce_step([tuple(second[:2]), tuple(second[2:])], 0)
        ties = [member for couple in second for member in couple]
    begun = attend_back(qkv, summaries, lse, mixed_grad, 0, count // 2)
    d_query, d_keys, d_values, terms = attend_back(
        qkv, summaries, lse, mixed_grad, count // 2, count - count // 2, begun, ties
    )
    back, far_back, narrow_one, *first = project_back(
        inputs,
        d_query,
        d_keys,
        d_values,
        terms,
        means,
        (w_query, w_key, w_value),
        narrow,
        shards[:3],
        tiles,
    )
    owned = reduce_seq(far_back)
    input_grad = input_back(inputs, back, owned, narrow, middle_grad)
    if tiles:
        size = norm1_gain.shape[0]
        second = reduce_step(reduce_step(second, 1), 2, True)
        first = reduce_step([tuple(first[:2]), tuple(first[2:])], 0)
        first = reduce_step(reduce_step(first, 1), 2, True)
        tail = reduce_end(second, shards[3:], [size] * 4 + [up_bias.shape[0]])
        front = reduce_end(first, shards[:3], [size] * 2)
        matrices = front[:3] + tail[:3]
        vectors = front[3:] + tail[3:6] + [tail[7], tail[6]]
    else:
        vectors = [
            narrow_one[0],
            narrow_one[1],
            narrow_two[0],
            narrow_two[1],
            narrow_two[2],
            wide_two[0],
            narrow_two[3],
        ]
        reduced = reduce_plain(list(first) + list(second), vectors)
        matrices, vectors = reduced[:6], reduced[6:]
    return (outputs, input_grad, *matrices, *vectors)


def solution(mesh):
    placed = (
        P("batch", "seq", None),
        P("batch", "seq", None),
        P("seq", "batch"),
        P("seq", "batch"),
        P("seq", "batch"),
        P("seq", "batch"),
        P("seq", "batch"),
        P("seq", "batch"),
        P("seq"),
        P("seq"),
        P("seq"),
        P("seq"),
        P("seq"),
        P("seq"),
        P("seq"),
    )
    return jax.shard_map(
        layer,
        mesh=mesh,
        in_specs=placed,
        out_specs=(
            P("batch", "seq", None),
            P("batch", "seq", None),
            P("seq", "batch"),
            P("seq", "batch"),
            P("seq", "batch"),
            P("seq", "batch"),
            P("seq", "batch"),
            P("seq", "batch"),
            P("seq"),
            P("seq"),
            P("seq"),
            P("seq"),
            P("seq"),
            P("seq"),
            P("seq"),
        ),
        check_vma=False,
    )
```

```python
import jax
import jax.numpy as jnp
from jax import lax
from jax.experimental import pallas as pl
from jax.experimental.pallas import tpu as pltpu
from jax.sharding import PartitionSpec as P


HEADS = 8
HEAD = 64
VEC_ROWS = 32
F32 = jnp.float32
BF16 = jnp.bfloat16


def swap(array, axis, bit):
    count = lax.axis_size(axis)
    return lax.ppermute(array, axis, [(i, i ^ bit) for i in range(count)])


def bits_down(count):
    return [1 << k for k in range(count.bit_length() - 2, -1, -1)]


def outer_stages():
    seq = [("seq", bit) for bit in bits_down(lax.axis_size("seq")) if bit > 1]
    batch = [("batch", bit) for bit in bits_down(lax.axis_size("batch")) if bit > 2]
    return batch + seq


def relative_ids(stages):
    ids = [(0, 0)]
    for axis, bit in stages:
        moved = [(s ^ bit, b) if axis == "seq" else (s, b ^ bit) for s, b in ids]
        ids = ids + moved
    return ids


X_STAGE = ("batch", 2)
Y_STAGE = ("seq", 1)
CORE = ("batch", 1)


def gather_outer(state):
    for stage in outer_stages():
        theirs = swap(state, *stage)
        state = jnp.concatenate([state, theirs], 0)
    return state


def gather_inner(state):
    half = state.shape[1] // 2
    outer = outer_stages()
    pieces = []
    for k, order in enumerate(((X_STAGE, Y_STAGE), (Y_STAGE, X_STAGE))):
        first = k * half
        part = state[:, first : first + half]
        theirs = swap(part, *order[0])
        part = jnp.concatenate([part, theirs], 0)
        far = swap(part, *order[1])
        ids = relative_ids(outer + [order[0]])
        full = relative_ids(outer + list(order))
        far_ids = full[len(ids) :]
        for piece, names in ((part, ids), (far, far_ids)):
            pieces.append((piece, names, first))
            theirs = swap(piece, *CORE)
            pieces.append((theirs, [(s, b ^ 1) for s, b in names], first))
    return pieces


def place():
    return jnp.stack([lax.axis_index("seq"), lax.axis_index("batch")]).astype(jnp.int32)


def cuts(segments, first, half):
    found = []
    at = 0
    for name, rows in segments:
        low, high = max(at, first), min(at + rows, first + half)
        if low < high:
            found.append((name, low - at, low - first, high - low))
        at += rows
    return found


def assemble(spot, refs, pieces, segments, targets, outs, vec):
    for ref, (piece, names, first) in zip(refs, pieces):
        for p, (sr, br) in enumerate(names):
            s, b = spot[0] ^ sr, spot[1] ^ br
            for name, row, here, size in cuts(segments, first, piece.shape[1]):
                if name == "vec":
                    if br == 0:
                        vec(ref[p, here : here + size, :], s)
                else:
                    number, top, left = targets(name, row, s, b)
                    outs[number][
                        pl.ds(pl.multiple_of(top, 16), size), pl.ds(pl.multiple_of(left, 128), 128)
                    ] = ref[p, here : here + size, :]


def pack_order():
    outer = outer_stages()
    return [
        relative_ids(outer + [Y_STAGE, X_STAGE, CORE]),
        relative_ids(outer + [X_STAGE, Y_STAGE, CORE]),
    ]


def write_packed(spot, ins, vec_block, outs, segments, targets, orders):
    half = sum(size for _, size in segments) // 2
    for k, (names, first) in enumerate(zip(orders, (0, half))):
        for p, (sr, br) in enumerate(names):
            s, b = spot[0] ^ sr, spot[1] ^ br
            out = outs[2 * k + p // (len(names) // 2)]
            p = p % (len(names) // 2)
            for name, row, here, size in cuts(segments, first, half):
                if name == "vec":
                    out[p, here : here + size, :] = vec_block(s)
                else:
                    number, top, left = targets(name, row, s, b)
                    out[p, here : here + size, :] = ins[number][
                        pl.ds(pl.multiple_of(top, 16), size), pl.ds(pl.multiple_of(left, 128), 128)
                    ].astype(BF16)


ORDERS = ((CORE, X_STAGE, Y_STAGE), (CORE, Y_STAGE, X_STAGE))


def reduce_step(halves, step, last=False):
    done = []
    for k, (kept, sent) in enumerate(halves):
        theirs = swap(sent, *ORDERS[k][step])
        if last:
            done.append((kept, theirs))
            continue
        done.append(tuple(joined_sum([(kept, theirs, k == 1)])))
    return done


def sum_rows(mine, theirs, spans):
    total = mine.astype(F32) + theirs.astype(F32)
    count = VEC_ROWS // 2
    return total, [total[at : at + count] + total[at + count : at + VEC_ROWS] for at in spans]


def joined_sum(couples):
    count = couples[0][0].shape[0]
    rows = sum(kept.shape[1] for kept, _, _ in couples)

    def kernel(*refs):
        ins, outs = refs[:-2], refs[-2:]
        for p in range(count):
            out = outs[p // (count // 2)]
            at = 0
            for k, (kept, _, vectors) in enumerate(couples):
                size = kept.shape[1]
                total, pairs = sum_rows(
                    ins[2 * k][p], ins[2 * k + 1][p], [size - VEC_ROWS] if vectors else []
                )
                out[p % (count // 2), at : at + size, :] = total.astype(BF16)
                for pair in pairs:
                    high = pair.astype(BF16)
                    low = (pair - high.astype(F32)).astype(BF16)
                    end = at + size
                    out[p % (count // 2), end - VEC_ROWS : end - VEC_ROWS // 2, :] = high
                    out[p % (count // 2), end - VEC_ROWS // 2 : end, :] = low
                at += size

    arrays = [array for kept, theirs, _ in couples for array in (kept, theirs)]
    return pl.pallas_call(
        kernel,
        cost_estimate=cost(2),
        out_shape=[jax.ShapeDtypeStruct((count // 2, rows, 128), BF16)] * 2,
        in_specs=[pl.BlockSpec(memory_space=pltpu.VMEM)] * len(arrays),
        out_specs=[pl.BlockSpec(memory_space=pltpu.VMEM)] * 2,
    )(*arrays)


def again(kept, theirs, spans):
    count, rows = kept.shape[:2]

    def kernel(mine_ref, theirs_ref, *outs):
        for p in range(count):
            out = outs[p // (count // 2)]
            q = p % (count // 2)
            total, pairs = sum_rows(mine_ref[p], theirs_ref[p], spans)
            out[q] = total.astype(BF16)
            for pair, at in zip(pairs, spans):
                high = pair.astype(BF16)
                out[q, at : at + VEC_ROWS // 2, :] = high
                low = (pair - high.astype(F32)).astype(BF16)
                out[q, at + VEC_ROWS // 2 : at + VEC_ROWS, :] = low

    return pl.pallas_call(
        kernel,
        cost_estimate=cost(2),
        out_shape=[jax.ShapeDtypeStruct((count // 2, rows, 128), BF16)] * 2,
        in_specs=[pl.BlockSpec(memory_space=pltpu.VMEM)] * 2,
        out_specs=[pl.BlockSpec(memory_space=pltpu.VMEM)] * 2,
    )(kept, theirs)


def finish(kept, theirs, parts, spans, shapes, sizes):
    def kernel(spot, mine_ref, theirs_ref, *outs):
        total, pairs = sum_rows(mine_ref[0], theirs_ref[0], spans)
        for number, row, left, at, size in parts:
            outs[number][row : row + size, left : left + 128] = total[at : at + size]
        (pair,) = pairs
        row = 0
        for out, size in zip(outs[len(shapes) :], sizes):
            if size < 128:
                line = pair[row : row + 1]
                found = line[:, :size]
                for k in range(1, 128 // size):
                    part = line[:, k * size : (k + 1) * size]
                    found = jnp.where(spot[0] % (128 // size) == k, part, found)
                out[...] = found.reshape(size)
                row += 1
            else:
                for at in range(0, size, 128):
                    out[at : at + 128] = pair[row : row + 1].reshape(128)
                    row += 1

    return pl.pallas_call(
        kernel,
        cost_estimate=cost(2),
        out_shape=[jax.ShapeDtypeStruct(shape, F32) for shape in shapes]
        + [jax.ShapeDtypeStruct((size,), F32) for size in sizes],
        in_specs=[pl.BlockSpec(memory_space=pltpu.SMEM)]
        + [pl.BlockSpec(memory_space=pltpu.VMEM)] * 2,
        out_specs=[pl.BlockSpec(memory_space=pltpu.VMEM)] * (len(shapes) + len(sizes)),
    )(place(), kept, theirs)


def reduce_end(halves, weights, sizes):
    segments = columns(weights) + [("vec", VEC_ROWS)]
    parts = []
    spans = []
    at = 0
    for k, (kept, _) in enumerate(halves):
        half = kept.shape[1]
        for name, row, here, size in cuts(segments, k * half, half):
            if name == "vec":
                spans.append(at + here)
            else:
                parts.append((name[0], row, name[1] * 128, at + here, size))
        at += half
    kept, sent = joined_sum([(kept, theirs, k == 1) for k, (kept, theirs) in enumerate(halves)])
    stages = outer_stages()[::-1]
    for k, stage in enumerate(stages):
        theirs = swap(sent, *stage)
        if k < len(stages) - 1:
            kept, sent = again(kept, theirs, spans)
    return list(finish(kept, theirs, parts, spans, [w.shape for w in weights], sizes))


def seq_stages():
    return [("seq", bit) for bit in bits_down(lax.axis_size("seq"))]


def gather_seq(array):
    state = array[None]
    for stage in seq_stages():
        theirs = swap(state, *stage)
        state = jnp.concatenate([state, theirs], 0)
    return state


def reduce_seq(state):
    for stage in seq_stages()[::-1]:
        count = state.shape[0] // 2
        theirs = swap(state[count:], *stage)
        total = state[:count].astype(F32) + theirs.astype(F32)
        state = total if count == 1 else total.astype(BF16)
    return state[0]


def whole_tiles(weights, vectors):
    return (
        all(w.shape[0] % 16 == 0 and w.shape[1] % 128 == 0 for w in weights)
        and all(128 % v.shape[0] == 0 or v.shape[0] % 128 == 0 for v in vectors)
        and sum(v.shape[0] for v in vectors) % 128 == 0
    )


def columns(weights):
    return [
        ((i, c), weight.shape[0])
        for i, weight in enumerate(weights)
        for c in range(weight.shape[1] // 128)
    ]


def spots(weights):
    def targets(name, row, s, b):
        if name == "vec":
            return (len(weights), s * VEC_ROWS + row, 0)
        i, c = name
        rows, width = weights[i].shape
        return (i, s * rows + row, b * width + c * 128)

    return targets


def pack_shards(weights, vectors, after=None):
    segments = columns(weights) + ([("vec", VEC_ROWS)] if vectors else [])
    rows = sum(size for _, size in segments)
    extra = [] if after is None else [after]

    def kernel(spot, *refs):
        out = refs[-1]
        at = 0
        for ref, weight in zip(refs, weights):
            for left in range(0, weight.shape[1], 128):
                out[0, at : at + weight.shape[0], :] = ref[:, left : left + 128]
                at += weight.shape[0]
        if not vectors:
            return
        found = []
        for ref in refs[len(weights) : len(weights) + len(vectors)]:
            size = ref.shape[0]
            line = ref[...].astype(F32)
            if size < 128:
                line = jnp.concatenate([line[None]] * (128 // size), 1)
                lane = lax.broadcasted_iota(jnp.int32, line.shape, 1)
                found.append(jnp.where(lane // size == spot[0] % (128 // size), line, 0.0))
            else:
                found += [line[None, k : k + 128] for k in range(0, size, 128)]
        row = lax.broadcasted_iota(jnp.int32, (VEC_ROWS, 128), 0)
        block = jnp.zeros((VEC_ROWS, 128), F32)
        for k, line in enumerate(found):
            block = jnp.where(row == k, line, block)
        out[0, at:, :] = block.astype(BF16)

    return pl.pallas_call(
        kernel,
        out_shape=jax.ShapeDtypeStruct((1, rows, 128), BF16),
        in_specs=[pl.BlockSpec(memory_space=pltpu.SMEM)]
        + [pl.BlockSpec(memory_space=pltpu.VMEM)] * (len(weights) + len(vectors))
        + [pl.BlockSpec(memory_space=pl.ANY)] * len(extra),
        out_specs=pl.BlockSpec(memory_space=pltpu.VMEM),
    )(place(), *weights, *vectors, *extra)


def gather_plain(weights, vectors):
    wide = [lax.all_gather(w, "batch", axis=1, tiled=True) for w in weights]
    wide = [lax.all_gather(w, "seq", axis=0, tiled=True) for w in wide]
    return wide, [lax.all_gather(v, "seq", axis=0, tiled=True).astype(F32) for v in vectors]


def reduce_plain(grads, vectors):
    outs = [
        lax.psum_scatter(g.astype(BF16), "batch", scatter_dimension=1, tiled=True).astype(F32)
        for g in grads
    ]
    outs = outs + list(lax.psum(tuple(vectors), "batch"))
    return [lax.psum_scatter(o, "seq", scatter_dimension=0, tiled=True) for o in outs]


def dot(left, right, a=1, b=0):
    return lax.dot_general(left, right, (((a,), (b,)), ((), ())), preferred_element_type=F32)


def norm_parts(values):
    centred = values - jnp.mean(values, -1, keepdims=True)
    scale = lax.rsqrt(jnp.mean(centred * centred, -1, keepdims=True) + 1e-05)
    return centred * scale, scale


def norm_back(grad, unit, scale, gain):
    inner = grad * gain
    pull = jnp.mean(inner, -1, keepdims=True)
    twist = jnp.mean(inner * unit, -1, keepdims=True)
    return scale * (inner - pull - unit * twist)


def gelu_pair(values):
    bell = jnp.exp(-0.5 * values * values)
    t = 1.0 / (1.0 + (0.3275911 * 0.5**0.5) * jnp.abs(values))
    poly = 1.061405429 * 0.5
    for factor in (-1.453152027, 1.421413741, -0.284496736, 0.254829592):
        poly = poly * t + factor * 0.5
    below = poly * t * bell
    share = jnp.where(values < 0, below, 1.0 - below)
    return values * share, share + values * bell * 0.3989422804014327


def full(shape):
    return pl.BlockSpec(shape, lambda i: (0,) * len(shape))


def each(shape):
    return pl.BlockSpec((1,) + tuple(shape[1:]), lambda i: (i,) + (0,) * (len(shape) - 1))


NARROW = 8


def cost(micros):
    return pl.CostEstimate(flops=int(micros * 1e9), transcendentals=0, bytes_accessed=1 << 20)


def spread(shape, first=0):
    return pl.BlockSpec((shape[0], 1) + tuple(shape[2:]), lambda i: (0, i + first, 0, 0))


def span_means(inputs):
    count, rows, width = inputs.shape
    half = rows // 2

    def kernel(x_ref, out_ref):
        unit, _ = norm_parts(x_ref[0].astype(F32))
        for j in range(2):
            mean = jnp.sum(unit[j * half : (j + 1) * half], 0, keepdims=True) / half
            high = mean.astype(BF16)
            out_ref[0, j : j + 1, :width] = high
            out_ref[0, j : j + 1, width:] = (mean - high.astype(F32)).astype(BF16)

    shape = (count, 2, 2 * width)
    return pl.pallas_call(
        kernel,
        cost_estimate=cost(3),
        grid=(count,),
        in_specs=[each(inputs.shape)],
        out_specs=each(shape),
        out_shape=jax.ShapeDtypeStruct(shape, BF16),
    )(inputs)


def far_means(ref):
    rows = jnp.concatenate([ref[p, 0].astype(F32) for p in range(ref.shape[0])], 0)
    width = rows.shape[1] // 2
    return rows[:, :width] + rows[:, width:]


def project(inputs, means, shards, slices, pieces, wide, lines, tiles):
    count, rows, width = inputs.shape
    far = 2 * means.shape[0]
    hidden = slices[5].shape[0] * lax.axis_size("seq")
    segments = columns(shards) + [("vec", VEC_ROWS)]
    targets = spots(shards)
    order = (0, 1, 2, 3, 4, 6)
    arrays = [piece for piece, _, _ in pieces] if tiles else list(wide) + list(lines)

    def kernel(spot, x_ref, means_ref, *refs):
        ins = refs[: len(arrays)]
        out_ref, sums_ref, q_ref, k_ref, v_ref, narrow_ref, wide_ref = refs[len(arrays) :]

        @pl.when(pl.program_id(0) == 0)
        def _():
            if tiles:
                narrow_ref[...] = jnp.zeros_like(narrow_ref)
                wide_ref[...] = jnp.zeros_like(wide_ref)

                def vec(block, s):
                    block = block.astype(F32)
                    row = 0
                    for k, member in enumerate(slices):
                        size = member.shape[0]
                        start = s * size
                        for at in range(0, size, 128):
                            left = pl.multiple_of((start + at) // 128 * 128, 128)
                            line = block[row : row + 1]
                            if k == 5:
                                wide_ref[0:1, pl.ds(left, 128)] += line
                            else:
                                to = order.index(k)
                                narrow_ref[to : to + 1, pl.ds(left, 128)] += line
                            row += 1

                assemble(spot, ins, pieces, segments, targets, (q_ref, k_ref, v_ref), vec)
            else:
                for ref, source in zip((q_ref, k_ref, v_ref, narrow_ref, wide_ref), ins):
                    ref[...] = source[...]

        unit, _ = norm_parts(x_ref[0].astype(F32))
        normed = (unit * narrow_ref[0:1, :] + narrow_ref[1:2, :]).astype(BF16)
        out_ref[0, :, :width] = dot(normed, q_ref[...]).astype(BF16)
        mean = far_means(means_ref) * narrow_ref[0:1, :] + narrow_ref[1:2, :]
        high = mean.astype(BF16)
        low = (mean - high.astype(F32)).astype(BF16)
        joined = jnp.concatenate([normed, high, low], 0)
        for k, ref in enumerate((k_ref, v_ref)):
            product = dot(joined, ref[...])
            out_ref[0, :, (k + 1) * width : (k + 2) * width] = product[:rows].astype(BF16)
            total = product[rows : rows + far] + product[rows + far :]
            sums_ref[0, :, k * width : (k + 1) * width] = total.astype(BF16)

    shapes = [(count, rows, 3 * width), (count, far, 2 * width)]
    square = (width, width)
    return pl.pallas_call(
        kernel,
        cost_estimate=cost(6),
        grid=(count,),
        in_specs=[
            pl.BlockSpec(memory_space=pltpu.SMEM),
            each(inputs.shape),
            spread(means.shape),
        ]
        + [pl.BlockSpec(memory_space=pltpu.VMEM)] * len(arrays),
        out_specs=[each(shape) for shape in shapes]
        + [full(square)] * 3
        + [full((NARROW, width)), full((1, hidden))],
        out_shape=[jax.ShapeDtypeStruct(shape, BF16) for shape in shapes + [square] * 3]
        + [jax.ShapeDtypeStruct((NARROW, width), F32), jax.ShapeDtypeStruct((1, hidden), F32)],
    )(place(), inputs, means, *arrays)


def head_mask(rows, lane_half):
    lane = lax.broadcasted_iota(jnp.int32, (rows, 2 * HEAD), 1)
    return (lane < HEAD) if lane_half == 0 else (lane >= HEAD)


def only(array, lane_half):
    return jnp.where(head_mask(array.shape[0], lane_half), array, jnp.zeros_like(array))


def seen_rows(seq, far, rows):
    row = lax.broadcasted_iota(jnp.int32, (far, rows), 0) // 2
    seen = jnp.zeros((far, rows), F32)
    for p, (rel, _) in enumerate(relative_ids(seq_stages())):
        seen = jnp.where(row == p, jnp.where((seq ^ rel) < seq, 1.0, 0.0), seen)
    return seen


def scores_of(keys, query, visible, rows):
    scores = dot(keys, query, 1, 1) * HEAD ** (-0.5)
    far = jnp.where(visible > 0, scores[rows:], -1e30)
    return jnp.concatenate([scores[:rows], far], 0)


def attend(qkv, summaries):
    count, rows, width = qkv.shape[0], qkv.shape[1], qkv.shape[2] // 3
    far = summaries.shape[1]

    def kernel(spot, qkv_ref, sum_ref, mixed_ref, lse_ref):
        seen = seen_rows(spot[0], far, rows)
        spans = sum_ref[0]
        for pair in range(HEADS // 2):
            at = pair * 2 * HEAD
            query = qkv_ref[0, :, at : at + 2 * HEAD]
            keys = jnp.concatenate(
                [
                    qkv_ref[0, :, width + at : width + at + 2 * HEAD],
                    spans[:, at : at + 2 * HEAD],
                ],
                0,
            )
            values = jnp.concatenate(
                [
                    qkv_ref[0, :, 2 * width + at : 2 * width + at + 2 * HEAD],
                    spans[:, width + at : width + at + 2 * HEAD],
                ],
                0,
            )
            total = None
            for side in range(2):
                scores = scores_of(keys, only(query, side), seen, rows)
                top = jnp.max(scores, 0, keepdims=True)
                powers = jnp.exp(scores - top)
                mass = jnp.sum(powers, 0, keepdims=True)
                head = 2 * pair + side
                lse_ref[0, head : head + 1, :] = top + jnp.log(mass)
                probs = (powers * (1.0 / mass)).astype(BF16)
                part = dot(only(values, side), probs, 0, 0)
                total = part if total is None else total + part
            mixed_ref[0, :, at : at + 2 * HEAD] = total.T.astype(BF16)

    block = (count, rows, width)
    return pl.pallas_call(
        kernel,
        cost_estimate=cost(8),
        grid=(count,),
        in_specs=[
            pl.BlockSpec(memory_space=pltpu.SMEM),
            each(qkv.shape),
            each(summaries.shape),
        ],
        out_specs=[each(block), each((count, HEADS, rows))],
        out_shape=[
            jax.ShapeDtypeStruct(block, BF16),
            jax.ShapeDtypeStruct((count, HEADS, rows), F32),
        ],
    )(place(), qkv, summaries)


def split_rows(total):
    high = total.astype(BF16).astype(F32)
    return high, total - high


def vector_block(narrow, wide, per):
    def block(s):
        left = pl.multiple_of(s * per // 128 * 128, 128)
        found = narrow[:, pl.ds(left, 128)]
        if wide is not None:
            step = wide.shape[1] // narrow.shape[1] * per
            for k in range(step // 128):
                chunk = wide[:, pl.ds(pl.multiple_of(s * step + k * 128, 128), 128)]
                row = lax.broadcasted_iota(jnp.int32, chunk.shape, 0)
                keep = (row % (VEC_ROWS // 2)) == 4 + k
                found = found + jnp.where(keep, chunk, 0.0)
        return found.astype(BF16)

    return block


def feed(inputs, cotangent, mixed, narrow, long_bias, pieces, wide, shards, tiles):
    count, _, width = inputs.shape
    hidden_width = long_bias.shape[1]
    arrays = [piece for piece, _, _ in pieces] if tiles else list(wide)
    step = 512
    grads = [(width, width), (width, hidden_width), (hidden_width, width)]
    segments = columns(shards) + [("vec", VEC_ROWS)]
    targets = spots(shards)
    orders = pack_order() if tiles else None
    half = sum(size for _, size in segments) // 2
    per = width // lax.axis_size("seq")

    def kernel(spot, x_ref, cot_ref, mixed_ref, lines_ref, bu_ref, *rest):
        ins, rest = rest[: len(arrays)], rest[len(arrays) :]
        out_ref, mgrad_ref, xgrad_ref, narrow_ref, wide_ref, *rest = rest
        if tiles:
            packs, rest = rest[:4], rest[4:]
            go_ref, gu_ref, gd_ref, high_ref, long_ref, wo_ref, wu_ref, wd_ref = rest
        else:
            go_ref, gu_ref, gd_ref = rest
            wo_ref, wu_ref, wd_ref = ins
        step_id = pl.program_id(0)
        bias, gain, shift, last = (lines_ref[k : k + 1, :] for k in (4, 2, 3, 5))

        @pl.when(step_id == 0)
        def _():
            for ref in (go_ref, gu_ref, gd_ref, narrow_ref, wide_ref):
                ref[...] = jnp.zeros_like(ref)
            if tiles:
                weights = (wo_ref, wu_ref, wd_ref)
                assemble(spot, ins, pieces, segments[:-1], targets, weights, None)

        middle = x_ref[0].astype(F32) + (dot(mixed_ref[0], wo_ref[...]) + bias)
        cot = cot_ref[0]
        tangent = cot.astype(BF16)
        unit, scale = norm_parts(middle)
        normed = (unit * gain + shift).astype(BF16)
        flipped = normed.T
        final = middle + last
        back = None
        for at in range(0, hidden_width, step):
            here = slice(at, at + step)
            hidden = dot(normed, wu_ref[:, here]) + bu_ref[:, here]
            active, slope = gelu_pair(hidden)
            active = active.astype(BF16)
            final = final + dot(active, wd_ref[here, :])
            gd_ref[here, :] += dot(active, tangent, 0, 0)
            grad = (dot(tangent, wd_ref[here, :], 1, 1) * slope).astype(BF16)
            gu_ref[:, here] += dot(flipped, grad)
            wide_ref[0:1, here] += jnp.sum(grad.astype(F32), 0, keepdims=True)
            part = dot(grad, wu_ref[:, here], 1, 1)
            back = part if back is None else back + part
        out_ref[0] = final.astype(BF16)
        narrow_ref[0:1, :] += jnp.sum(back * unit, 0, keepdims=True)
        narrow_ref[1:2, :] += jnp.sum(back, 0, keepdims=True)
        middle_grad = cot + norm_back(back, unit, scale, gain)
        mgrad_ref[0] = middle_grad
        branch = middle_grad.astype(BF16)
        narrow_ref[2:3, :] += jnp.sum(branch.astype(F32), 0, keepdims=True)
        narrow_ref[3:4, :] += jnp.sum(tangent.astype(F32), 0, keepdims=True)
        go_ref[...] += dot(mixed_ref[0], branch, 0, 0)
        xgrad_ref[0] = dot(branch, wo_ref[...], 1, 1).astype(BF16)

        if tiles:

            @pl.when(step_id == count - 1)
            def _():
                for ref, source, k in ((high_ref, narrow_ref, 8), (long_ref, wide_ref, 1)):
                    high, low = split_rows(source[...])
                    zero = jnp.zeros((8, source.shape[1]), F32)
                    if k == 1:
                        high = jnp.broadcast_to(high[0:1], zero.shape)
                        low = jnp.broadcast_to(low[0:1], zero.shape)
                    ref[...] = jnp.concatenate([high, zero, low, zero], 0)
                write_packed(
                    spot,
                    (go_ref, gu_ref, gd_ref),
                    vector_block(high_ref, long_ref, per),
                    packs,
                    segments,
                    targets,
                    orders,
                )

    block = inputs.shape
    out_shape = [
        jax.ShapeDtypeStruct(block, BF16),
        jax.ShapeDtypeStruct(block, F32),
        jax.ShapeDtypeStruct(block, BF16),
        jax.ShapeDtypeStruct((8, width), F32),
        jax.ShapeDtypeStruct((8, hidden_width), F32),
    ]
    out_specs = [each(block)] * 3 + [full((8, width)), full((8, hidden_width))]
    scratch = []
    if tiles:
        packed_shapes = [(len(names) // 2, half, 128) for names in orders for _ in range(2)]
        out_shape += [jax.ShapeDtypeStruct(shape, BF16) for shape in packed_shapes]
        out_specs += [pl.BlockSpec(memory_space=pltpu.VMEM)] * 4
        scratch = [pltpu.VMEM(shape, F32) for shape in grads]
        scratch += [pltpu.VMEM((VEC_ROWS, width), F32), pltpu.VMEM((VEC_ROWS, hidden_width), F32)]
        scratch += [pltpu.VMEM(shape, BF16) for shape in grads]
    else:
        out_shape += [jax.ShapeDtypeStruct(shape, F32) for shape in grads]
        out_specs += [full(shape) for shape in grads]
    return pl.pallas_call(
        kernel,
        cost_estimate=cost(35),
        grid=(count,),
        in_specs=[pl.BlockSpec(memory_space=pltpu.SMEM)]
        + [each(block)] * 3
        + [full(narrow.shape), full(long_bias.shape)]
        + [pl.BlockSpec(memory_space=pltpu.VMEM)] * len(arrays),
        out_specs=out_specs,
        out_shape=out_shape,
        scratch_shapes=scratch,
    )(place(), inputs, cotangent, mixed, narrow, long_bias, *arrays)


def attend_back(qkv, summaries, lse, mixed_grad, first, number, before=(), after=()):
    _, rows, width = mixed_grad.shape
    far = summaries.shape[1]
    extra = list(before) + list(after)

    def each(shape):
        return pl.BlockSpec(
            (1,) + tuple(shape[1:]), lambda i: (i + first,) + (0,) * (len(shape) - 1)
        )

    def kernel(spot, qkv_ref, sum_ref, lse_ref, grad_ref, *rest):
        dq_ref, dk_ref, dv_ref, far_ref = rest[len(extra) :]
        seen = seen_rows(spot[0], far, rows)
        spans = sum_ref[0]
        for pair in range(HEADS // 2):
            at = pair * 2 * HEAD
            lanes = slice(at, at + 2 * HEAD)
            query = qkv_ref[0, :, lanes]
            pull = grad_ref[0, :, lanes]
            keys = jnp.concatenate(
                [qkv_ref[0, :, width + at : width + at + 2 * HEAD], spans[:, lanes]], 0
            )
            values = jnp.concatenate(
                [
                    qkv_ref[0, :, 2 * width + at : 2 * width + at + 2 * HEAD],
                    spans[:, width + at : width + at + 2 * HEAD],
                ],
                0,
            )
            d_query = d_keys = d_values = 0.0
            for side in range(2):
                head = 2 * pair + side
                own = only(query, side)
                own_pull = only(pull, side)
                scores = scores_of(keys, own, seen, rows)
                probs = jnp.exp(scores - lse_ref[0, head : head + 1, :])
                dots = dot(values, own_pull, 1, 1)
                centre = jnp.sum(probs * dots, 0, keepdims=True)
                slope = (probs * (dots - centre)).astype(BF16)
                d_values = d_values + dot(probs.astype(BF16), own_pull)
                d_keys = d_keys + dot(slope, own)
                d_query = d_query + dot(only(keys, side), slope, 0, 0)
            d_keys = d_keys * HEAD ** (-0.5)
            dq_ref[0, :, lanes] = (d_query * HEAD ** (-0.5)).T.astype(BF16)
            dk_ref[0, :, lanes] = d_keys[:rows].astype(BF16)
            dv_ref[0, :, lanes] = d_values[:rows].astype(BF16)
            for k, terms in enumerate((d_keys, d_values)):
                left = k * width + at
                far_ref[0, :, left : left + 2 * HEAD] = terms[rows:].astype(BF16)

    block = mixed_grad.shape
    return pl.pallas_call(
        kernel,
        cost_estimate=cost(7),
        grid=(number,),
        in_specs=[
            pl.BlockSpec(memory_space=pltpu.SMEM),
            each(qkv.shape),
            each(summaries.shape),
            each(lse.shape),
            each(block),
        ]
        + [pl.BlockSpec(memory_space=pl.ANY)] * len(extra),
        out_specs=[each(block)] * 3 + [each(summaries.shape)],
        out_shape=[
            jax.ShapeDtypeStruct(block, BF16),
            jax.ShapeDtypeStruct(block, BF16),
            jax.ShapeDtypeStruct(block, BF16),
            jax.ShapeDtypeStruct(summaries.shape, BF16),
        ],
        input_output_aliases={5 + k: k for k in range(len(before))},
    )(place(), qkv, summaries, lse, mixed_grad, *extra)


def project_back(
    inputs, d_query, d_keys, d_values, terms, means, weights, narrow, shards, tiles
):
    count, rows, width = inputs.shape
    segments = columns(shards) + [("vec", VEC_ROWS)]
    targets = spots(shards)
    orders = pack_order() if tiles else None
    half = sum(size for _, size in segments) // 2
    per = width // lax.axis_size("seq")

    def kernel(spot, x_ref, dq_ref, dk_ref, dv_ref, terms_ref, means_ref, wq_ref, wk_ref, wv_ref,
               lines_ref, back_ref, far_ref, narrow_ref, *rest):
        gain, shift = lines_ref[0:1, :], lines_ref[1:2, :]
        if tiles:
            packs, (gq_ref, gk_ref, gv_ref, high_ref) = rest[:4], rest[4:]
        else:
            gq_ref, gk_ref, gv_ref = rest
        step_id = pl.program_id(0)

        @pl.when(step_id == 0)
        def _():
            for ref in (gq_ref, gk_ref, gv_ref, narrow_ref):
                ref[...] = jnp.zeros_like(ref)

        unit, _ = norm_parts(x_ref[0].astype(F32))
        unit_far = far_means(means_ref)
        joined = jnp.concatenate([unit, unit_far], 0)
        flipped = (joined * gain + shift).astype(BF16).T
        gq_ref[...] += dot(flipped[:, :rows], dq_ref[0])
        both = None
        for k, (direct, w_ref, g_ref) in enumerate(
            ((dk_ref, wk_ref, gk_ref), (dv_ref, wv_ref, gv_ref))
        ):
            act = jnp.concatenate([direct[0], terms_ref[0, :, k * width : (k + 1) * width]], 0)
            g_ref[...] += dot(flipped, act)
            part = dot(act, w_ref[...], 1, 1)
            both = part if both is None else both + part
        back = both[:rows] + dot(dq_ref[0], wq_ref[...], 1, 1)
        far = both[rows:]
        back_ref[0] = back
        for p in range(far.shape[0] // 2):
            far_ref[p, 0] = far[2 * p : 2 * p + 2].astype(BF16)
        narrow_ref[0:1, :] += jnp.sum(back * unit, 0, keepdims=True) + jnp.sum(
            far * unit_far, 0, keepdims=True
        )
        narrow_ref[1:2, :] += jnp.sum(both, 0, keepdims=True) + jnp.sum(
            back - both[:rows], 0, keepdims=True
        )

        if tiles:

            @pl.when(step_id == count - 1)
            def _():
                high, low = split_rows(narrow_ref[...])
                zero = jnp.zeros_like(high)
                high_ref[...] = jnp.concatenate([high, zero, low, zero], 0)
                write_packed(
                    spot,
                    (gq_ref, gk_ref, gv_ref),
                    vector_block(high_ref, None, per),
                    packs,
                    segments,
                    targets,
                    orders,
                )

    block = inputs.shape
    square = (width, width)
    sent = means.shape[:3] + (width,)
    out_shape = [
        jax.ShapeDtypeStruct(block, F32),
        jax.ShapeDtypeStruct(sent, BF16),
        jax.ShapeDtypeStruct((8, width), F32),
    ]
    out_specs = [each(block), spread(sent), full((8, width))]
    scratch = []
    if tiles:
        packed_shapes = [(len(names) // 2, half, 128) for names in orders for _ in range(2)]
        out_shape += [jax.ShapeDtypeStruct(shape, BF16) for shape in packed_shapes]
        out_specs += [pl.BlockSpec(memory_space=pltpu.VMEM)] * 4
        scratch = [pltpu.VMEM(square, F32)] * 3 + [pltpu.VMEM((VEC_ROWS, width), F32)]
    else:
        out_shape += [jax.ShapeDtypeStruct(square, F32)] * 3
        out_specs += [full(square)] * 3
    return pl.pallas_call(
        kernel,
        cost_estimate=cost(10),
        grid=(count,),
        in_specs=[pl.BlockSpec(memory_space=pltpu.SMEM)]
        + [each(block)] * 4
        + [each(terms.shape), spread(means.shape)]
        + [full(square)] * 3
        + [full(narrow.shape)],
        out_specs=out_specs,
        out_shape=out_shape,
        scratch_shapes=scratch,
    )(place(), inputs, d_query, d_keys, d_values, terms, means, *weights, narrow)


def input_back(inputs, back, owned, narrow, middle_grad):
    count, rows, _ = inputs.shape
    half = rows // 2

    def kernel(x_ref, back_ref, own_ref, lines_ref, mgrad_ref, out_ref):
        unit, scale = norm_parts(x_ref[0].astype(F32))
        back = jnp.concatenate(
            [
                back_ref[0, j * half : (j + 1) * half, :] + own_ref[0, j : j + 1, :] / half
                for j in range(2)
            ],
            0,
        )
        out_ref[0] = mgrad_ref[0] + norm_back(back, unit, scale, lines_ref[0:1, :])

    return pl.pallas_call(
        kernel,
        cost_estimate=cost(4),
        grid=(count,),
        in_specs=[each(inputs.shape)] * 2
        + [each(owned.shape), full(narrow.shape), each(inputs.shape)],
        out_specs=each(inputs.shape),
        out_shape=jax.ShapeDtypeStruct(inputs.shape, F32),
    )(inputs, back, owned, narrow, middle_grad)


def layer(
    inputs,
    cotangent,
    query_weight,
    key_weight,
    value_weight,
    out_weight,
    up_weight,
    down_weight,
    norm1_gain,
    norm1_bias,
    norm2_gain,
    norm2_bias,
    out_bias,
    up_bias,
    down_bias,
):
    shards = [query_weight, key_weight, value_weight, out_weight, up_weight, down_weight]
    slices = [norm1_gain, norm1_bias, norm2_gain, norm2_bias, out_bias, up_bias, down_bias]
    tiles = whole_tiles(shards, slices)
    count, _, width = inputs.shape
    wide, lines, early, late = [None] * 6, (), (), ()
    if tiles:
        state = gather_outer(pack_shards(shards[:3], slices))
        other = gather_outer(pack_shards(shards[3:], [], state))
        early = gather_inner(state)
        late = gather_inner(other)
    else:
        wide, members = gather_plain(shards, slices)
        blank = jnp.zeros((NARROW - 6, width), F32)
        lines = (
            jnp.concatenate([jnp.stack([members[k] for k in (0, 1, 2, 3, 4, 6)]), blank]),
            members[5][None],
        )
    means = gather_seq(span_means(inputs))
    qkv, summaries, w_query, w_key, w_value, narrow, long_bias = project(
        inputs, means, shards[:3], slices, early, wide[:3], lines, tiles
    )
    mixed, lse = attend(qkv, summaries)
    outputs, middle_grad, mixed_grad, narrow_two, wide_two, *second = feed(
        inputs, cotangent, mixed, narrow, long_bias, late, wide[3:], shards[3:], tiles
    )
    ties = []
    if tiles:
        second = reduce_step([tuple(second[:2]), tuple(second[2:])], 0)
        ties = [member for couple in second for member in couple]
    begun = attend_back(qkv, summaries, lse, mixed_grad, 0, count // 2)
    d_query, d_keys, d_values, terms = attend_back(
        qkv, summaries, lse, mixed_grad, count // 2, count - count // 2, begun, ties
    )
    back, far_back, narrow_one, *first = project_back(
        inputs,
        d_query,
        d_keys,
        d_values,
        terms,
        means,
        (w_query, w_key, w_value),
        narrow,
        shards[:3],
        tiles,
    )
    owned = reduce_seq(far_back)
    input_grad = input_back(inputs, back, owned, narrow, middle_grad)
    if tiles:
        size = norm1_gain.shape[0]
        second = reduce_step(reduce_step(second, 1), 2, True)
        first = reduce_step([tuple(first[:2]), tuple(first[2:])], 0)
        first = reduce_step(reduce_step(first, 1), 2, True)
        tail = reduce_end(second, shards[3:], [size] * 4 + [up_bias.shape[0]])
        front = reduce_end(first, shards[:3], [size] * 2)
        matrices = front[:3] + tail[:3]
        vectors = front[3:] + tail[3:6] + [tail[7], tail[6]]
    else:
        vectors = [
            narrow_one[0],
            narrow_one[1],
            narrow_two[0],
            narrow_two[1],
            narrow_two[2],
            wide_two[0],
            narrow_two[3],
        ]
        reduced = reduce_plain(list(first) + list(second), vectors)
        matrices, vectors = reduced[:6], reduced[6:]
    return (outputs, input_grad, *matrices, *vectors)


def solution(mesh):
    placed = (
        P("batch", "seq", None),
        P("batch", "seq", None),
        P("seq", "batch"),
        P("seq", "batch"),
        P("seq", "batch"),
        P("seq", "batch"),
        P("seq", "batch"),
        P("seq", "batch"),
        P("seq"),
        P("seq"),
        P("seq"),
        P("seq"),
        P("seq"),
        P("seq"),
        P("seq"),
    )
    return jax.shard_map(
        layer,
        mesh=mesh,
        in_specs=placed,
        out_specs=(
            P("batch", "seq", None),
            P("batch", "seq", None),
            P("seq", "batch"),
            P("seq", "batch"),
            P("seq", "batch"),
            P("seq", "batch"),
            P("seq", "batch"),
            P("seq", "batch"),
            P("seq"),
            P("seq"),
            P("seq"),
            P("seq"),
            P("seq"),
            P("seq"),
            P("seq"),
        ),
        check_vma=False,
    )
```
